256 devices in a mesh: row: 128 (over y, z, x), head: 2 (over core).
Axes of the slice: x: 4, y: 4, z: 8, core: 2. Of those that a mesh axis runs over, the one named last changes fastest.
Arguments:
- query_single: bfloat16 [128, 384], P('row'), may hold values from -6 to 6
- key_single: bfloat16 [8192, 384], P('row'), may hold values from -6 to 6
- pair: bfloat16 [128, 8192, 128], P('row'), may hold values from -6 to 32
- query_frames: float32 [12, 128], P(None, 'row'), may hold values from -2.5 to 2.5, as said below
- key_frames: float32 [12, 8192], P(None, 'row'), may hold values from -2.5 to 2.5, as said below
- w_query: bfloat16 [384, 96], P(None, 'head'), may hold values from -0.3125 to 0.3125
- w_key: bfloat16 [384, 96], P(None, 'head'), may hold values from -0.3125 to 0.3125
- w_value: bfloat16 [384, 96], P(None, 'head'), may hold values from -0.3125 to 0.3125
- w_query_points: bfloat16 [384, 72], P(None, 'head'), may hold values from -0.3125 to 0.3125
- w_key_points: bfloat16 [384, 72], P(None, 'head'), may hold values from -0.3125 to 0.3125
- w_value_points: bfloat16 [384, 144], P(None, 'head'), may hold values from -0.3125 to 0.3125
- head_weight: float32 [6], P('head'), may hold values from -2.5 to 0.5
- bias_weight: bfloat16 [6, 128], P('head'), as said below
- w_out: bfloat16 [1056, 384], P('head'), may hold values from -0.1875 to 0.1875
- d_out: bfloat16 [128, 384], P('row'), may hold values from -24 to 24
Outputs:
- output: bfloat16 [128, 384], P('row')
- grad_query: float32 [128, 384], P('row')
- grad_keys: float32 [8192, 384], P('row')
The draws below stay inside these ranges and needn't reach their ends.
Inputs may be any that keep to these rules, and one draw needn't show every extreme that they name: `bias_weight`: entries within -2.5 and 2.5 over the square root of 128. `query_frames`: rows 0 to 8 of each column form a rotation matrix. `key_frames`: rows 0 to 8 of each column form a rotation matrix.
All inputs are finite; a program needn't handle non-finite values.
Results may differ from the reference program's by a relative error of at most 0.012.
The reference program's roundings to bfloat16 on the way count: a program that leaves them out, or rounds other values in their place, can miss the bound.
Values may be sent and summed in bfloat16 or wider, within the bound.
A program may use at most 64 MiB of HBM per device.

```python
import math
import jax
import jax.numpy as jnp
from jax import lax

CS = 384
H = 6
C = 16
PQ = 4
PV = 8
CZ = 128
Q = 128
K = 8192


def frame_table(key, count):
    key_rot, key_move = jax.random.split(key)
    along = jax.random.normal(key_rot, (3, count), jnp.float32)
    scale_inv = 1.0 / jnp.sqrt(1.0 + jnp.sum(along * along, axis=0))
    scalar_part = scale_inv
    vector_one = along[0] * scale_inv
    vector_two = along[1] * scale_inv
    vector_three = along[2] * scale_inv
    entries = [scalar_part * scalar_part + vector_one * vector_one - vector_two * vector_two - vector_three * vector_three, 2.0 * (vector_one * vector_two - scalar_part * vector_three), 2.0 * (vector_one * vector_three + scalar_part * vector_two), 2.0 * (vector_one * vector_two + scalar_part * vector_three), scalar_part * scalar_part - vector_one * vector_one + vector_two * vector_two - vector_three * vector_three, 2.0 * (vector_two * vector_three - scalar_part * vector_one), 2.0 * (vector_one * vector_three - scalar_part * vector_two), 2.0 * (vector_two * vector_three + scalar_part * vector_one), scalar_part * scalar_part - vector_one * vector_one - vector_two * vector_two + vector_three * vector_three]
    moves = jnp.clip(0.5 * jax.random.normal(key_move, (3, count), jnp.float32), -2.5, 2.5)
    return jnp.concatenate([jnp.stack(entries, axis=0), moves], axis=0)


def draw_query_frames(key, part):
    return frame_table(jax.random.fold_in(key, 17), Q)


def draw_key_frames(key, part):
    return frame_table(jax.random.fold_in(key, 29), K)


def draw_pair(key, part):
    return jnp.clip(jax.random.normal(key, (Q, K, CZ), jnp.float32), -6.0, 6.0).astype(jnp.bfloat16)


def draw_bias_weight(key, part):
    return (jnp.clip(jax.random.normal(key, (H, CZ), jnp.float32), -2.5, 2.5) / math.sqrt(CZ)).astype(jnp.bfloat16)


def shard_levels(stream_key, shape, shards, least, largest):
    def one(axis_at, parts):
        draws = jax.random.uniform(jax.random.fold_in(jax.random.fold_in(stream_key, 6), axis_at), (parts,), jnp.float32, least / len(shards), largest / len(shards))
        return jnp.repeat(jnp.exp(draws), shape[axis_at] // parts).reshape((-1,) + (1,) * (len(shape) - axis_at - 1))

    loudness = one(*shards[0])
    for cut in shards[1:]:
        loudness = loudness * one(*cut)
    return loudness


def noise(key, dims, deviation, reach, shards=(), kind=jnp.bfloat16):
    array = deviation * jax.random.normal(key, dims, jnp.float32)
    if shards:
        array = array * shard_levels(key, dims, shards, -0.22, 0.18)
    return jnp.clip(array, -reach, reach).astype(kind)


def setup_inputs(seed: int = 0) -> dict:
    seeds = jax.random.split(jax.random.key(seed), 16)
    return {
        "query_single": noise(seeds[0], (Q, CS), 1.0, 6.0, ((0, 128),)),
        "key_single": noise(seeds[1], (K, CS), 1.0, 6.0, ((0, 128),)),
        "pair": draw_pair(jax.random.fold_in(seeds[15], 71), 0),
        "query_frames": draw_query_frames(jax.random.fold_in(seeds[15], 71), 0),
        "key_frames": draw_key_frames(jax.random.fold_in(seeds[15], 71), 0),
        "w_query": noise(seeds[5], (CS, H * C), CS ** -0.5, 0.3125, ((1, 2),)),
        "w_key": noise(seeds[6], (CS, H * C), CS ** -0.5, 0.3125, ((1, 2),)),
        "w_value": noise(seeds[7], (CS, H * C), CS ** -0.5, 0.3125, ((1, 2),)),
        "w_query_points": noise(seeds[8], (CS, H * PQ * 3), CS ** -0.5, 0.3125, ((1, 2),)),
        "w_key_points": noise(seeds[9], (CS, H * PQ * 3), CS ** -0.5, 0.3125, ((1, 2),)),
        "w_value_points": noise(seeds[10], (CS, H * PV * 3), CS ** -0.5, 0.3125, ((1, 2),)),
        "head_weight": jnp.clip(-2.5 + 3.0 * jax.random.uniform(seeds[11], (H,), jnp.float32) ** shard_levels(seeds[11], (H,), ((0, 2),), -0.2, 0.2), -2.5, 0.5),
        "bias_weight": draw_bias_weight(jax.random.fold_in(seeds[15], 71), 0),
        "w_out": noise(seeds[13], (H * (C + 4 * PV + CZ), CS), (H * (C + 4 * PV + CZ)) ** -0.5, 0.1875, ((0, 2),)),
        "d_out": jnp.clip(jax.random.uniform(seeds[14], (Q, CS), jnp.float32, -24.0, 24.0) * shard_levels(seeds[14], (Q, CS), ((0, 128),), -0.4, 0.0), -24.0, 24.0).astype(jnp.bfloat16),
    }


LOGIT_SCALE = math.sqrt(1.0 / 3.0)

def point_scale(points):
    return math.sqrt(2.0 / (9.0 * points))

def product(form, former, latter):
    return jnp.einsum(form, former.astype(jnp.float32), latter.astype(jnp.float32))

def frame_parts(frames):
    columns = frames.shape[1]
    return (frames[:9].reshape(3, 3, columns), frames[9:12])

def rotate(vectors, rotation):
    return jnp.einsum('xyn,nhpy->nhpx', rotation, vectors, precision=lax.Precision.HIGHEST)

def unrotate(vectors, rotation):
    return jnp.einsum('xyn,nhpx->nhpy', rotation, vectors, precision=lax.Precision.HIGHEST)

def split_columns(packed, extents, axis_index):
    pieces = []
    cursor = 0
    for extent in extents:
        pieces.append(lax.slice_in_dim(packed, cursor, cursor + extent, axis=axis_index))
        cursor = cursor + extent
    return pieces

def key_side(key_single, key_frames, w_key, w_value, w_key_points, w_value_points, head_count):
    rows_k = key_single.shape[0]
    rotation, offset = frame_parts(key_frames)
    offset_rows = jnp.transpose(offset)[:, None, None, :]
    keys_b = jnp.dot(key_single, w_key, preferred_element_type=jnp.float32).astype(jnp.bfloat16)
    values_b = jnp.dot(key_single, w_value, preferred_element_type=jnp.float32).astype(jnp.bfloat16)
    local_k = jnp.dot(key_single, w_key_points, preferred_element_type=jnp.float32).reshape(rows_k, head_count, PQ, 3)
    key_pts = (rotate(local_k, rotation) + offset_rows).astype(jnp.bfloat16).reshape(rows_k, -1)
    local_v = jnp.dot(key_single, w_value_points, preferred_element_type=jnp.float32).reshape(rows_k, head_count, PV, 3)
    value_pts = (rotate(local_v, rotation) + offset_rows).astype(jnp.bfloat16).reshape(rows_k, -1)
    return (keys_b, values_b, key_pts, value_pts)

def query_pass(query_single, pair, query_frames, w_query, w_query_points, head_weight, bias_weight, w_out, d_out, keys_all, values_all, kp_all, vp_all):
    rows_q = query_single.shape[0]
    head_count = head_weight.shape[0]
    rotation, offset = frame_parts(query_frames)
    offset_rows = jnp.transpose(offset)[:, None, None, :]
    point_gain = (jax.nn.softplus(head_weight) * point_scale(PQ))[None, :, None]
    query_b = jnp.dot(query_single, w_query, preferred_element_type=jnp.float32).astype(jnp.bfloat16).reshape(rows_q, head_count, C)
    local_q = jnp.dot(query_single, w_query_points, preferred_element_type=jnp.float32).reshape(rows_q, head_count, PQ, 3)
    query_pts = (rotate(local_q, rotation) + offset_rows).astype(jnp.bfloat16).reshape(rows_q, head_count, 3 * PQ)
    query_sq = lax.optimization_barrier(jnp.sum(jnp.square(query_pts.astype(jnp.float32)), axis=-1))
    key_sq = lax.optimization_barrier(jnp.sum(jnp.square(kp_all.astype(jnp.float32)), axis=-1))
    pair_bias = product('hc,qkc->qhk', bias_weight, pair)
    distance = query_sq[:, :, None] + jnp.transpose(key_sq)[None, :, :] - 2.0 * product('qhe,khe->qhk', query_pts, kp_all)
    logits = LOGIT_SCALE * (product('qhc,khc->qhk', query_b, keys_all) / math.sqrt(C) + pair_bias - 0.5 * point_gain * distance)
    attention = jax.nn.softmax(logits, axis=-1)
    attention_b = attention.astype(jnp.bfloat16)
    attended = product('qhk,khc->qhc', attention_b, values_all)
    point_sum = product('qhk,khe->qhe', attention_b, vp_all).reshape(rows_q, head_count, PV, 3)
    pair_out = product('qhk,qkc->qhc', attention_b, pair)
    local_pts = unrotate(point_sum - offset_rows, rotation)
    lengths = jnp.sqrt(1.0 + lax.optimization_barrier(jnp.sum(jnp.square(local_pts), axis=-1)))
    features = jnp.concatenate([attended, local_pts.reshape(rows_q, head_count, 3 * PV), lengths, pair_out], axis=-1)
    features = features.astype(jnp.bfloat16).reshape(rows_q, -1)
    output_part = jnp.dot(features, w_out, preferred_element_type=jnp.float32)
    d_features = jnp.dot(d_out, jnp.transpose(w_out), preferred_element_type=jnp.float32).reshape(rows_q, head_count, -1)
    d_attended = d_features[:, :, :C].astype(jnp.bfloat16)
    d_local = d_features[:, :, C:C + 3 * PV].reshape(rows_q, head_count, PV, 3)
    d_lengths = d_features[:, :, C + 3 * PV:C + 4 * PV]
    d_pair = d_features[:, :, C + 4 * PV:].astype(jnp.bfloat16)
    d_local = d_local + (d_lengths / lengths)[..., None] * local_pts
    d_points = rotate(d_local, rotation).astype(jnp.bfloat16).reshape(rows_q, head_count, 3 * PV)
    d_attention = product('qhc,khc->qhk', d_attended, values_all) + product('qhe,khe->qhk', d_points, vp_all) + product('qhc,qkc->qhk', d_pair, pair)
    row_total = lax.optimization_barrier(jnp.sum(attention * d_attention, axis=-1, keepdims=True))
    score_b = (LOGIT_SCALE * attention * (d_attention - row_total)).astype(jnp.bfloat16)
    d_query = product('qhk,khc->qhc', score_b, keys_all) / math.sqrt(C)
    score_rows = lax.optimization_barrier(jnp.sum(score_b.astype(jnp.float32), axis=-1))[:, :, None]
    d_qpts = point_gain * (product('qhk,khe->qhe', score_b, kp_all) - score_rows * query_pts.astype(jnp.float32))
    d_qlocal = unrotate(d_qpts.reshape(rows_q, head_count, PQ, 3), rotation).astype(jnp.bfloat16).reshape(rows_q, -1)
    grad_part = jnp.dot(d_query.astype(jnp.bfloat16).reshape(rows_q, -1), jnp.transpose(w_query), preferred_element_type=jnp.float32)
    grad_part = grad_part + jnp.dot(d_qlocal, jnp.transpose(w_query_points), preferred_element_type=jnp.float32)
    query_side = jnp.concatenate([query_b.reshape(rows_q, -1), query_pts.reshape(rows_q, -1), d_attended.reshape(rows_q, -1), d_points.reshape(rows_q, -1)], axis=1)
    return (output_part, grad_part, query_side, attention_b, score_b)

def key_terms(attention_b, score_b, query_side, key_points, point_gain, head_count):
    count_q = query_side.shape[0]
    count_k = key_points.shape[0]
    side_parts = split_columns(query_side, [head_count * C, head_count * 3 * PQ, head_count * C, head_count * 3 * PV], 1)
    query_b = side_parts[0].reshape(count_q, head_count, C)
    query_pts = side_parts[1].reshape(count_q, head_count, 3 * PQ)
    grad_att = side_parts[2].reshape(count_q, head_count, C)
    grad_pts = side_parts[3].reshape(count_q, head_count, 3 * PV)
    d_key = product('qhk,qhc->khc', score_b, query_b) / math.sqrt(C)
    score_sum = lax.optimization_barrier(jnp.sum(score_b.astype(jnp.float32), axis=0))
    d_kpts = point_gain * (product('qhk,qhe->khe', score_b, query_pts) - jnp.transpose(score_sum)[:, :, None] * key_points.astype(jnp.float32))
    d_value = product('qhk,qhc->khc', attention_b, grad_att)
    d_vpts = product('qhk,qhe->khe', attention_b, grad_pts)
    return jnp.concatenate([d_key.reshape(count_k, -1), d_value.reshape(count_k, -1), d_kpts.reshape(count_k, -1), d_vpts.reshape(count_k, -1)], axis=1)

def key_finish(key_rows, key_frames, w_key, w_value, w_key_points, w_value_points, head_count):
    rows_k = key_rows.shape[0]
    rotation, offset = frame_parts(key_frames)
    pieces = split_columns(key_rows, [head_count * C, head_count * C, head_count * 3 * PQ, head_count * 3 * PV], 1)
    kp_local = unrotate(pieces[2].reshape(rows_k, head_count, PQ, 3), rotation).astype(jnp.bfloat16).reshape(rows_k, -1)
    vp_local = unrotate(pieces[3].reshape(rows_k, head_count, PV, 3), rotation).astype(jnp.bfloat16).reshape(rows_k, -1)
    result = jnp.dot(pieces[0].astype(jnp.bfloat16), jnp.transpose(w_key), preferred_element_type=jnp.float32)
    result = result + jnp.dot(pieces[1].astype(jnp.bfloat16), jnp.transpose(w_value), preferred_element_type=jnp.float32)
    result = result + jnp.dot(kp_local, jnp.transpose(w_key_points), preferred_element_type=jnp.float32)
    return result + jnp.dot(vp_local, jnp.transpose(w_value_points), preferred_element_type=jnp.float32)

def reference(query_single, key_single, pair, query_frames, key_frames, w_query, w_key, w_value, w_query_points, w_key_points, w_value_points, head_weight, bias_weight, w_out, d_out):
    head_count = head_weight.shape[0]
    total_q = query_single.shape[0]
    total_keys = key_single.shape[0]
    keys_b, values_b, key_pts, value_pts = key_side(key_single, key_frames, w_key, w_value, w_key_points, w_value_points, head_count)
    keys_all = keys_b.reshape(total_keys, head_count, C)
    values_all = values_b.reshape(total_keys, head_count, C)
    kp_all = key_pts.reshape(total_keys, head_count, 3 * PQ)
    vp_all = value_pts.reshape(total_keys, head_count, 3 * PV)
    point_gain = (jax.nn.softplus(head_weight) * point_scale(PQ))[None, :, None]
    block_rows = math.gcd(total_q, 32)
    block_count = total_q // block_rows
    blocks_in = (query_single.reshape(block_count, block_rows, -1), pair.reshape(block_count, block_rows, total_keys, -1), jnp.transpose(query_frames.reshape(12, block_count, block_rows), (1, 0, 2)), d_out.reshape(block_count, block_rows, -1))

    def one_block(carry, blocks):
        single_blk, pair_blk, frames_blk, cotangent_blk = blocks
        output_part, grad_part, query_side, attention_b, score_b = query_pass(single_blk, pair_blk, frames_blk, w_query, w_query_points, head_weight, bias_weight, w_out, cotangent_blk, keys_all, values_all, kp_all, vp_all)
        terms = key_terms(attention_b, score_b, query_side, kp_all, point_gain, head_count)
        return (carry + terms, (output_part.astype(jnp.bfloat16), grad_part))
    width_all = head_count * (2 * C + 3 * PQ + 3 * PV)
    key_rows, results = lax.scan(one_block, jnp.zeros((total_keys, width_all), jnp.float32), blocks_in)
    outputs, grads = results
    grad_keys = key_finish(key_rows, key_frames, w_key, w_value, w_key_points, w_value_points, head_count)
    return (outputs.reshape(total_q, -1), grads.reshape(total_q, -1), grad_keys)
```

```python
import math

import jax
import jax.numpy as jnp
from jax import lax
from jax.sharding import PartitionSpec as P

C = 16
PQ = 4
PV = 8


LOGIT_SCALE = math.sqrt(1.0 / 3.0)


def point_scale(points):
    return math.sqrt(2.0 / (9.0 * points))


def product(form, former, latter):
    return jnp.einsum(form, former, latter, preferred_element_type=jnp.float32)


def frame_parts(frames):
    columns = frames.shape[1]
    return (frames[:9].reshape(3, 3, columns), frames[9:12])


def rotate(vectors, rotation):
    return jnp.einsum("xyn,nhpy->nhpx", rotation, vectors, precision=lax.Precision.HIGHEST)


def unrotate(vectors, rotation):
    return jnp.einsum("xyn,nhpx->nhpy", rotation, vectors, precision=lax.Precision.HIGHEST)


def split_columns(packed, extents, axis_index):
    pieces = []
    cursor = 0
    for extent in extents:
        pieces.append(lax.slice_in_dim(packed, cursor, cursor + extent, axis=axis_index))
        cursor = cursor + extent
    return pieces


def key_side(key_single, key_frames, w_key, w_value, w_key_points, w_value_points, head_count):
    rows_k = key_single.shape[0]
    rotation, offset = frame_parts(key_frames)
    offset_rows = jnp.transpose(offset)[:, None, None, :]
    keys_b = jnp.dot(key_single, w_key, preferred_element_type=jnp.float32).astype(jnp.bfloat16)
    values_b = jnp.dot(key_single, w_value, preferred_element_type=jnp.float32).astype(jnp.bfloat16)
    local_k = jnp.dot(key_single, w_key_points, preferred_element_type=jnp.float32).reshape(
        rows_k, head_count, PQ, 3
    )
    key_pts = (rotate(local_k, rotation) + offset_rows).astype(jnp.bfloat16).reshape(rows_k, -1)
    local_v = jnp.dot(key_single, w_value_points, preferred_element_type=jnp.float32).reshape(
        rows_k, head_count, PV, 3
    )
    value_pts = (rotate(local_v, rotation) + offset_rows).astype(jnp.bfloat16).reshape(rows_k, -1)
    return (keys_b, values_b, key_pts, value_pts)


def query_pass(
    query_single,
    pair,
    query_frames,
    w_query,
    w_query_points,
    head_weight,
    bias_weight,
    w_out,
    d_out,
    keys_all,
    values_all,
    kp_all,
    vp_all,
):
    rows_q = query_single.shape[0]
    head_count = head_weight.shape[0]
    rotation, offset = frame_parts(query_frames)
    offset_rows = jnp.transpose(offset)[:, None, None, :]
    point_gain = (jax.nn.softplus(head_weight) * point_scale(PQ))[None, :, None]
    query_b = (
        jnp.dot(query_single, w_query, preferred_element_type=jnp.float32)
        .astype(jnp.bfloat16)
        .reshape(rows_q, head_count, C)
    )
    local_q = jnp.dot(query_single, w_query_points, preferred_element_type=jnp.float32).reshape(
        rows_q, head_count, PQ, 3
    )
    query_pts = (
        (rotate(local_q, rotation) + offset_rows)
        .astype(jnp.bfloat16)
        .reshape(rows_q, head_count, 3 * PQ)
    )
    query_sq = jnp.sum(jnp.square(query_pts.astype(jnp.float32)), axis=-1)
    key_sq = jnp.sum(jnp.square(kp_all.astype(jnp.float32)), axis=-1)
    pair_bias = product("hc,qkc->qhk", bias_weight, pair)
    distance = (
        query_sq[:, :, None]
        + jnp.transpose(key_sq)[None, :, :]
        - 2.0 * product("qhe,khe->qhk", query_pts, kp_all)
    )
    logits = LOGIT_SCALE * (
        product("qhc,khc->qhk", query_b, keys_all) / math.sqrt(C)
        + pair_bias
        - 0.5 * point_gain * distance
    )
    attention = jax.nn.softmax(logits, axis=-1)
    attention_b = attention.astype(jnp.bfloat16)
    attended = product("qhk,khc->qhc", attention_b, values_all)
    point_sum = product("qhk,khe->qhe", attention_b, vp_all).reshape(rows_q, head_count, PV, 3)
    pair_out = product("qhk,qkc->qhc", attention_b, pair)
    local_pts = unrotate(point_sum - offset_rows, rotation)
    lengths = jnp.sqrt(1.0 + jnp.sum(jnp.square(local_pts), axis=-1))
    features = jnp.concatenate(
        [attended, local_pts.reshape(rows_q, head_count, 3 * PV), lengths, pair_out], axis=-1
    )
    features = features.astype(jnp.bfloat16).reshape(rows_q, -1)
    output_part = jnp.dot(features, w_out, preferred_element_type=jnp.float32)
    d_features = jnp.dot(d_out, jnp.transpose(w_out), preferred_element_type=jnp.float32).reshape(
        rows_q, head_count, -1
    )
    d_attended = d_features[:, :, :C].astype(jnp.bfloat16)
    d_local = d_features[:, :, C : C + 3 * PV].reshape(rows_q, head_count, PV, 3)
    d_lengths = d_features[:, :, C + 3 * PV : C + 4 * PV]
    d_pair = d_features[:, :, C + 4 * PV :].astype(jnp.bfloat16)
    d_local = d_local + (d_lengths / lengths)[..., None] * local_pts
    d_points = rotate(d_local, rotation).astype(jnp.bfloat16).reshape(rows_q, head_count, 3 * PV)
    d_attention = (
        product("qhc,khc->qhk", d_attended, values_all)
        + product("qhe,khe->qhk", d_points, vp_all)
        + product("qhc,qkc->qhk", d_pair, pair)
    )
    row_total = jnp.sum(attention * d_attention, axis=-1, keepdims=True)
    score_b = (LOGIT_SCALE * attention * (d_attention - row_total)).astype(jnp.bfloat16)
    d_query = product("qhk,khc->qhc", score_b, keys_all) / math.sqrt(C)
    score_rows = jnp.sum(score_b.astype(jnp.float32), axis=-1)[:, :, None]
    d_qpts = point_gain * (
        product("qhk,khe->qhe", score_b, kp_all) - score_rows * query_pts.astype(jnp.float32)
    )
    d_qlocal = (
        unrotate(d_qpts.reshape(rows_q, head_count, PQ, 3), rotation)
        .astype(jnp.bfloat16)
        .reshape(rows_q, -1)
    )
    grad_part = jnp.dot(
        d_query.astype(jnp.bfloat16).reshape(rows_q, -1),
        jnp.transpose(w_query),
        preferred_element_type=jnp.float32,
    )
    grad_part = grad_part + jnp.dot(
        d_qlocal, jnp.transpose(w_query_points), preferred_element_type=jnp.float32
    )
    query_side = jnp.concatenate(
        [
            query_b.reshape(rows_q, -1),
            query_pts.reshape(rows_q, -1),
            d_attended.reshape(rows_q, -1),
            d_points.reshape(rows_q, -1),
        ],
        axis=1,
    )
    return (output_part, grad_part, query_side, attention_b, score_b)


def key_terms(attention_b, score_b, query_side, key_points, point_gain, head_count):
    count_q = query_side.shape[0]
    count_k = key_points.shape[0]
    side_parts = split_columns(
        query_side, [head_count * C, head_count * 3 * PQ, head_count * C, head_count * 3 * PV], 1
    )
    query_b = side_parts[0].reshape(count_q, head_count, C)
    query_pts = side_parts[1].reshape(count_q, head_count, 3 * PQ)
    grad_att = side_parts[2].reshape(count_q, head_count, C)
    grad_pts = side_parts[3].reshape(count_q, head_count, 3 * PV)
    d_key = product("qhk,qhc->khc", score_b, query_b) / math.sqrt(C)
    score_sum = jnp.sum(score_b.astype(jnp.float32), axis=0)
    d_kpts = point_gain * (
        product("qhk,qhe->khe", score_b, query_pts)
        - jnp.transpose(score_sum)[:, :, None] * key_points.astype(jnp.float32)
    )
    d_value = product("qhk,qhc->khc", attention_b, grad_att)
    d_vpts = product("qhk,qhe->khe", attention_b, grad_pts)
    return jnp.concatenate(
        [
            d_key.reshape(count_k, -1),
            d_value.reshape(count_k, -1),
            d_kpts.reshape(count_k, -1),
            d_vpts.reshape(count_k, -1),
        ],
        axis=1,
    )


def key_finish(key_rows, key_frames, w_key, w_value, w_key_points, w_value_points, head_count):
    rows_k = key_rows.shape[0]
    rotation, offset = frame_parts(key_frames)
    pieces = split_columns(
        key_rows, [head_count * C, head_count * C, head_count * 3 * PQ, head_count * 3 * PV], 1
    )
    kp_local = (
        unrotate(pieces[2].reshape(rows_k, head_count, PQ, 3), rotation)
        .astype(jnp.bfloat16)
        .reshape(rows_k, -1)
    )
    vp_local = (
        unrotate(pieces[3].reshape(rows_k, head_count, PV, 3), rotation)
        .astype(jnp.bfloat16)
        .reshape(rows_k, -1)
    )
    result = jnp.dot(
        pieces[0].astype(jnp.bfloat16), jnp.transpose(w_key), preferred_element_type=jnp.float32
    )
    result = result + jnp.dot(
        pieces[1].astype(jnp.bfloat16), jnp.transpose(w_value), preferred_element_type=jnp.float32
    )
    result = result + jnp.dot(
        kp_local, jnp.transpose(w_key_points), preferred_element_type=jnp.float32
    )
    return result + jnp.dot(
        vp_local, jnp.transpose(w_value_points), preferred_element_type=jnp.float32
    )


def shards(
    query_single,
    key_single,
    pair,
    query_frames,
    key_frames,
    w_query,
    w_key,
    w_value,
    w_query_points,
    w_key_points,
    w_value_points,
    head_weight,
    bias_weight,
    w_out,
    d_out,
):
    head_count = head_weight.shape[0]
    keys_b, values_b, key_pts, value_pts = key_side(
        key_single, key_frames, w_key, w_value, w_key_points, w_value_points, head_count
    )
    packed = jnp.concatenate([keys_b, values_b, key_pts, value_pts], axis=1)
    gathered = lax.all_gather(packed, "row", axis=0, tiled=True)
    total_keys = gathered.shape[0]
    pieces = split_columns(
        gathered, [head_count * C, head_count * C, head_count * 3 * PQ, head_count * 3 * PV], 1
    )
    keys_all = pieces[0].reshape(total_keys, head_count, C)
    values_all = pieces[1].reshape(total_keys, head_count, C)
    kp_all = pieces[2].reshape(total_keys, head_count, 3 * PQ)
    vp_all = pieces[3].reshape(total_keys, head_count, 3 * PV)
    output_part, grad_part, query_side, attention_b, score_b = query_pass(
        query_single,
        pair,
        query_frames,
        w_query,
        w_query_points,
        head_weight,
        bias_weight,
        w_out,
        d_out,
        keys_all,
        values_all,
        kp_all,
        vp_all,
    )
    output = lax.psum(output_part, "head").astype(jnp.bfloat16)
    point_gain = (jax.nn.softplus(head_weight) * point_scale(PQ))[None, :, None]
    scores = jnp.concatenate([attention_b, score_b], axis=1)
    rows_n = lax.axis_size("row")
    local_k = key_single.shape[0]
    scores = scores.reshape(2 * head_count, rows_n, local_k)
    scores = lax.all_to_all(scores, "row", split_axis=1, concat_axis=1, tiled=True)
    scores = jnp.transpose(scores, (1, 0, 2))
    side_all = lax.all_gather(query_side, "row", axis=0, tiled=True)
    key_rows = key_terms(
        scores[:, :head_count], scores[:, head_count:], side_all,
        key_pts.reshape(local_k, head_count, 3 * PQ), point_gain, head_count,
    )
    grad_keys_part = key_finish(
        key_rows, key_frames, w_key, w_value, w_key_points, w_value_points, head_count
    )
    grad_query, grad_keys = lax.psum((grad_part, grad_keys_part), "head")
    return (output, grad_query, grad_keys)


def solution(mesh):
    return jax.shard_map(
        shards,
        mesh=mesh,
        in_specs=(
            P("row", None),
            P("row", None),
            P("row", None, None),
            P(None, "row"),
            P(None, "row"),
            P(None, "head"),
            P(None, "head"),
            P(None, "head"),
            P(None, "head"),
            P(None, "head"),
            P(None, "head"),
            P("head"),
            P("head", None),
            P("head", None),
            P("row", None),
        ),
        out_specs=(P("row", None), P("row", None), P("row", None)),
        check_vma=False,
    )
```

```python
import functools
import math

import jax
import jax.numpy as jnp
from jax import lax
from jax.experimental import pallas as pl
from jax.experimental.pallas import tpu as pltpu
from jax.sharding import PartitionSpec as P

NY, NZ, NX = 4, 8, 4
ROWS = NY * NZ * NX
LK = 64
K = ROWS * LK
SIZES = (NY, NZ, NX)
LOGIT_SCALE = math.sqrt(1.0 / 3.0)
POINT_SCALE = math.sqrt(2.0 / 36.0)
MESH = pl.DeviceIdType.MESH
BF, F32 = jnp.bfloat16, jnp.float32

STREAMS = (
    (0, 0, 16, (2, 0, 1)),
    (0, 16, 32, (0, 1, 2)),
    (0, 48, 16, (1, 2, 0)),
    (1, 0, 16, (2, 0, 1)),
    (1, 16, 16, (0, 1, 2)),
    (1, 32, 32, (1, 2, 0)),
)
ROUNDS = 8


def nt(a, b):
    return lax.dot_general(a, b, (((1,), (1,)), ((), ())), preferred_element_type=F32)


def nn(a, b):
    return lax.dot_general(a, b, (((1,), (0,)), ((), ())), preferred_element_type=F32)


def tn(a, b, precision=None):
    return lax.dot_general(
        a, b, (((0,), (0,)), ((), ())), preferred_element_type=F32, precision=precision
    )


def iotas(shape):
    return (
        lax.broadcasted_iota(jnp.int32, shape, 0),
        lax.broadcasted_iota(jnp.int32, shape, 1),
    )


def third(value):
    return lax.shift_right_logical(value * 43, 7)


def within(lane, start, count):
    return (lane >= start) & (lane < start + count)


SHIFTS = (0, 1, 2, -1, -2)


def selection():
    j, l = iotas((12, 128))
    x = l - 3 * third(l)
    parts = []
    for d in SHIFTS:
        ok = (x + d >= 0) & (x + d < 3)
        parts.append(ok & (j == 4 * x + d))
    parts.append(j == 9 + x)
    for d in SHIFTS[1:]:
        ok = (x + d >= 0) & (x + d < 3)
        parts.append(ok & (j == 4 * x + 3 * d))
    return jnp.concatenate([jnp.where(p, 1.0, 0.0) for p in parts], axis=1)


def part(pat, i):
    return pat[:, 128 * i : 128 * i + 128]


def shifted(v, d):
    return v if d == 0 else pltpu.roll(v, (-d) % 128, 1)


def rotated(v, pat):
    return sum(part(pat, i) * shifted(v, d) for i, d in enumerate(SHIFTS))


def unrotated(v, pat):
    out = part(pat, 0) * v
    for i, d in enumerate(SHIFTS[1:]):
        out = out + part(pat, 6 + i) * shifted(v, d)
    return out


def softplus(x):
    return jnp.maximum(x, 0.0) + jnp.log1p(jnp.exp(-jnp.abs(x)))


def by_head(index, values):
    return jnp.where(index == 0, values[0], jnp.where(index == 1, values[1], values[2]))


def mask_k(r, l):
    return within(l, 16 * r, 16) & (r < 3), within(l, 48 + 12 * r, 12) & (r < 3)


def mask_v(r, l):
    return (within(l, 16 * r, 16) | within(l, 48 + 24 * r, 24)) & (r < 3)


def kernel(
    qs, ks, pair, qfr, kfr, w_q, w_k, w_v, w_qp, w_kp, w_vp, hw, bw, w_o, d_o,
    o_out, o_gq, o_gk,
    buf_k, buf_v, pair_s, wq_s, wk_s, wv_s, wp_s, lhs_s, pb_s, att_s, da_s, msg, recv, recv_f,
    pat_s, part_s, got_s,
    pair_sem, send_sem, recv_sem, a2a_send, a2a_recv, own_sem, ex_send, ex_recv,
):
    row = lax.axis_index("row")
    core = lax.axis_index("head")
    coords = (row // (NZ * NX), (row // NX) % NZ, row % NX)

    def neighbour(axis, step):
        moved = list(coords)
        moved[axis] = (coords[axis] + step + SIZES[axis]) % SIZES[axis]
        return (moved[0] * NZ + moved[1]) * NX + moved[2]

    barrier = pltpu.get_barrier_semaphore()
    for axis in range(3):
        for step in (1, -1):
            pl.semaphore_signal(
                barrier, inc=1, device_id=(neighbour(axis, step), core), device_id_type=MESH
            )
    pl.semaphore_signal(barrier, inc=1, device_id=(row, 1 - core), device_id_type=MESH)
    pair_copy = pltpu.make_async_copy(pair.at[0], pair_s, pair_sem)
    pair_copy.start()

    wk_s[...] = jnp.zeros_like(wk_s)
    wk_s[:, 0:48] = w_k[...]
    wk_s[:, 48:84] = w_kp[...]
    wv_s[...] = jnp.zeros_like(wv_s)
    wv_s[:, 0:48] = w_v[...]
    wv_s[:, 48:120] = w_vp[...]
    select = selection()
    pat = tn(kfr[...], select, lax.Precision.HIGHEST)
    pat_s[...] = pat
    r64, l64 = iotas((LK, 128))
    feat = nn(ks[...], wk_s[...])
    k_rows = jnp.where(
        l64 < 48, feat, jnp.where(l64 < 84, rotated(feat, pat) + part(pat, 5), 0.0)
    ).astype(BF)
    k_full = k_rows.astype(F32)
    square = k_full * k_full
    for h in range(3):
        total = jnp.sum(
            jnp.where(within(l64, 48 + 12 * h, 12), square, 0.0), axis=1, keepdims=True
        )
        high = total.astype(BF).astype(F32)
        middle = (total - high).astype(BF).astype(F32)
        low = total - high - middle
        at = 84 + 3 * h
        k_full = jnp.where(
            l64 == at, high, jnp.where(l64 == at + 1, middle, jnp.where(l64 == at + 2, low, k_full))
        )
    feat = nn(ks[...], wv_s[...])
    v_rows = jnp.where(
        l64 < 48, feat, jnp.where(l64 < 120, rotated(feat, pat) + part(pat, 5), 0.0)
    ).astype(BF)
    mine = (pl.ds(coords[0], 1), pl.ds(coords[1], 1), pl.ds(coords[2], 1))
    buf_k[mine] = k_full.astype(BF).reshape(1, 1, 1, LK, 128)
    buf_v[mine] = v_rows.reshape(1, 1, 1, LK, 128)

    bufs = (buf_k, buf_v)

    def copies(s, rnd):
        which, first, count, order = STREAMS[s]
        left = rnd
        for phase, axis in enumerate(order):
            rounds = SIZES[axis] // 2
            if left < rounds:
                break
            left -= rounds
        out = []
        for direction, step in enumerate((1, -1)):
            at = [pl.ds(c, 1) for c in coords]
            for done in order[:phase]:
                at[done] = pl.ds(0, SIZES[done])
            at[axis] = pl.ds((coords[axis] - step * left + SIZES[axis]) % SIZES[axis], 1)
            if left == rounds - 1:
                if phase == 0:
                    if direction != s % 2:
                        continue
                else:
                    split = order[0]
                    at[split] = pl.ds(direction * (SIZES[split] // 2), SIZES[split] // 2)
            where = bufs[which].at[at[0], at[1], at[2], pl.ds(first, count)]
            out.append(
                pltpu.make_async_remote_copy(
                    src_ref=where,
                    dst_ref=where,
                    send_sem=send_sem.at[s, rnd, direction],
                    recv_sem=recv_sem.at[s, rnd, direction],
                    device_id=(neighbour(axis, step), core),
                    device_id_type=MESH,
                )
            )
        return out

    pl.semaphore_wait(barrier, 7)

    def start_round(s, rnd):
        for copy in copies(s, rnd):
            copy.start()

    def end_round(s, rnd):
        for copy in copies(s, rnd):
            copy.wait_recv()

    for s in range(6):
        start_round(s, 0)

    wq_s[...] = jnp.zeros_like(wq_s)
    wq_s[:, 0:48] = w_q[...]
    wq_s[:, 48:84] = w_qp[...]
    pat_q = tn(qfr[...], select, lax.Precision.HIGHEST)
    _, l1 = iotas((1, 128))
    x1 = l1 - 3 * third(l1)
    feat = nn(qs[...], wq_s[...])
    q_row = jnp.where(
        l1 < 48, feat, jnp.where(l1 < 84, rotated(feat, pat_q) + part(pat_q, 5), 0.0)
    )
    q_row = q_row.astype(BF).astype(F32)
    r8, l8 = iotas((8, 128))
    raw = [hw[0], hw[1], hw[2]]
    gain = (softplus(by_head(r8, raw)) * POINT_SCALE)[:, 0:1]
    keys8, points8 = mask_k(r8, l8)
    values8 = mask_v(r8, l8)
    q8 = jnp.broadcast_to(q_row, (8, 128))
    q_square = jnp.sum(jnp.where(points8, q8 * q8, 0.0), axis=1, keepdims=True)
    lhs_q = jnp.concatenate(
        [
            jnp.where(keys8, q8, 0.0),
            jnp.where(points8, q8, jnp.where(within(l8, 84 + 3 * r8, 3) & (r8 < 3), -0.5, 0.0)),
        ],
        axis=0,
    ).astype(BF)

    i256, _ = iotas((256, 1))
    i = i256 & 127
    j = i - 48
    head = lax.shift_right_logical(j * 43, 10)
    point = third(j)
    p_head = lax.shift_right_logical(point, 3)
    source = jnp.where(
        i256 < 128,
        jnp.where(i < 48, 176 * lax.shift_right_logical(i, 4) + (i & 15), 152 * head + 16 + j),
        176 * p_head + 40 + (point & 7),
    )
    valid = (i < 120) & ((i256 < 128) | (i >= 48))
    source = jnp.where(valid, source, -1)
    _, lane_o = iotas((256, 528))
    pick = jnp.where(lane_o == source, 1.0, 0.0).astype(BF)
    wp_s[...] = nn(pick, w_o[...]).astype(BF)
    d_feat = nt(d_o[...], wp_s[...])
    lhs_s[...] = jnp.zeros_like(lhs_s)
    lhs_s[0:3, :] = bw[...].astype(F32)
    for h in range(3):
        lhs_s[8 + h : 9 + h, :] = nt(d_o[...], w_o[176 * h + 48 : 176 * h + 176, :])
    lhs_p = lhs_s[...].astype(BF)
    pair_copy.wait()

    def pair_step(g, _):
        at = pl.multiple_of(g * 1024, 1024)
        pb_s[:, pl.ds(at, 1024)] = nt(lhs_p, pair_s[pl.ds(at, 1024), :])
        return 0

    for rnd in range(1, ROUNDS + 1):
        lax.fori_loop(rnd - 1, rnd, pair_step, 0)
        for s in range(6):
            end_round(s, rnd - 1)
            if rnd < ROUNDS:
                start_round(s, rnd)

    def chunk(ref, g):
        return ref[pl.ds(g // 2, 1), pl.ds((g % 2) * 4, 4)].reshape(1024, 128)

    def logit_step(g, top):
        at = pl.multiple_of(g * 1024, 1024)
        both = nt(lhs_q, chunk(buf_k, g))
        logits = LOGIT_SCALE * (
            both[0:8] * 0.25
            + pb_s[0:8, pl.ds(at, 1024)]
            + gain * (both[8:16] - 0.5 * q_square)
        )
        att_s[:, pl.ds(at, 1024)] = logits
        return jnp.maximum(top, jnp.max(logits, axis=1, keepdims=True))

    top = lax.fori_loop(0, 8, logit_step, jnp.full((8, 1), -3.0e38, F32))

    def exp_step(g, total):
        at = pl.multiple_of(g * 1024, 1024)
        e = jnp.exp(att_s[:, pl.ds(at, 1024)] - top)
        att_s[:, pl.ds(at, 1024)] = e
        return total + jnp.sum(e, axis=1, keepdims=True)

    total = lax.fori_loop(0, 8, exp_step, jnp.zeros((8, 1), F32))

    def attend_step(g, carry):
        acc_v, acc_p = carry
        at = pl.multiple_of(g * 1024, 1024)
        a = att_s[:, pl.ds(at, 1024)] / total
        att_s[:, pl.ds(at, 1024)] = a
        a = a.astype(BF)
        return (
            acc_v + nn(a, chunk(buf_v, g)),
            acc_p + nn(a, pair_s[pl.ds(at, 1024), :]),
        )

    zero8 = jnp.zeros((8, 128), F32)
    acc_v, acc_p = lax.fori_loop(0, 8, attend_step, (zero8, zero8))
    row_v = jnp.sum(jnp.where(values8, acc_v, 0.0), axis=0, keepdims=True)
    is_point = within(l1, 48, 72)
    local = jnp.where(is_point, unrotated(jnp.where(is_point, row_v - part(pat_q, 5), 0.0), pat_q), 0.0)
    squares = local * local
    norm = squares
    for d in SHIFTS[1:]:
        norm = norm + jnp.where((x1 + d >= 0) & (x1 + d < 3), shifted(squares, d), 0.0)
    lengths = jnp.sqrt(1.0 + norm)
    f_v = jnp.where(l1 < 48, row_v, local).astype(BF)
    f_len = jnp.where(is_point & (x1 == 0), lengths, 0.0).astype(BF)
    out_row = nn(f_v, wp_s[0:128, :]) + nn(f_len, wp_s[128:256, :])
    for h in range(3):
        out_row = out_row + nn(
            acc_p[h : h + 1, :].astype(BF), w_o[176 * h + 48 : 176 * h + 176, :]
        )
    part_s[64:65, :] = out_row

    d_local = d_feat[:, 0:128] + d_feat[:, 128:256] / lengths * local
    d_local = jnp.where(is_point, d_local, 0.0)
    side_v = jnp.where(
        l1 < 48, d_feat[:, 0:128], jnp.where(is_point, rotated(d_local, pat_q), 0.0)
    )
    side_v8 = jnp.broadcast_to(side_v, (8, 128))
    lhs_v = jnp.where(values8, side_v8, 0.0).astype(BF)

    def grad_step(g, carry):
        at = pl.multiple_of(g * 1024, 1024)
        d_att = nt(lhs_v, chunk(buf_v, g)) + pb_s[8:16, pl.ds(at, 1024)]
        da_s[:, pl.ds(at, 1024)] = d_att
        return carry + jnp.sum(att_s[:, pl.ds(at, 1024)] * d_att, axis=1, keepdims=True)

    row_total = lax.fori_loop(0, 8, grad_step, jnp.zeros((8, 1), F32))
    side = jnp.where(r8 == 6, q8, jnp.where(r8 == 7, side_v8, 0.0))
    side = jnp.concatenate([side] * 8, axis=1)
    rc, _ = iotas((8, 1024))

    def score_step(g, carry):
        acc, sums = carry
        at = pl.multiple_of(g * 1024, 1024)
        a = att_s[:, pl.ds(at, 1024)]
        score = LOGIT_SCALE * a * (da_s[:, pl.ds(at, 1024)] - row_total)
        out = jnp.where(rc < 3, a, jnp.where(rc < 6, pltpu.roll(score, 3, 0), side))
        msg[:, pl.ds(at, 1024)] = out.astype(BF)
        score = score.astype(BF)
        acc = acc + nn(score, chunk(buf_k, g))
        return acc, sums + jnp.sum(score.astype(F32), axis=1, keepdims=True)

    acc_k, score_rows = lax.fori_loop(0, 8, score_step, (zero8, jnp.zeros((8, 1), F32)))

    def tile(device):
        return msg.at[:, pl.ds(pl.multiple_of((device // 2) * 128, 128), 128)]

    def send_step(i, _):
        target = (row + i) % ROWS
        pltpu.make_async_remote_copy(
            src_ref=tile(target),
            dst_ref=recv.at[row],
            send_sem=a2a_send,
            recv_sem=a2a_recv,
            device_id=(target, core),
            device_id_type=MESH,
        ).start()
        return 0

    own = pltpu.make_async_copy(tile(row), recv.at[row], own_sem)
    own.start()
    lax.fori_loop(1, ROWS, send_step, 0)

    q_terms = jnp.where(keys8, acc_k * 0.25, 0.0) + jnp.where(
        points8, gain * (acc_k - score_rows * q8), 0.0
    )
    d_q = jnp.sum(q_terms, axis=0, keepdims=True)
    d_q = jnp.where(l1 < 48, d_q, jnp.where(l1 < 84, unrotated(d_q, pat_q), 0.0)).astype(BF)
    part_s[72:73, :] = nt(d_q, wq_s[...])

    own.wait()
    everyone = recv.at[pl.ds(0, ROWS - 1)]
    pltpu.make_async_copy(everyone, everyone, a2a_recv).wait()

    def unpack_step(i, _):
        at = pl.multiple_of(i * 64, 64)
        recv_f[pl.ds(at, 64), :] = recv[pl.ds(i * 8, 8)].astype(F32).reshape(64, 128)
        return 0

    lax.fori_loop(0, ROWS // 8, unpack_step, 0)

    def every(i):
        return recv_f[pl.ds(i, ROWS, stride=8), :]

    side_k, side_v = every(6), every(7)
    _, l128 = iotas((ROWS, 128))
    out_k = out_v = sums = jnp.zeros((128, 128), F32)
    for h in range(3):
        keys_h = within(l128, 16 * h, 16)
        points_h = within(l128, 48 + 12 * h, 12)
        vpoints_h = within(l128, 48 + 24 * h, 24)
        att_h, score_h = every(h).astype(BF), every(3 + h).astype(BF)
        out_v = out_v + tn(att_h, jnp.where(keys_h | vpoints_h, side_v, 0.0).astype(BF))
        out_k = out_k + tn(score_h, jnp.where(keys_h | points_h, side_k, 0.0).astype(BF))
        sums = sums + tn(score_h, jnp.where(points_h, 1.0, 0.0).astype(BF))
    odd = row % 2 == 1

    def mine_of(x):
        return jnp.where(odd, x[64:128], x[0:64])

    out_k, out_v, sums = mine_of(out_k), mine_of(out_v), mine_of(sums)
    pat = pat_s[...]
    kf = buf_k[mine].reshape(LK, 128).astype(F32)
    gain_l = softplus(by_head(jnp.where(l1 < 60, 0, jnp.where(l1 < 72, 1, 2)), raw)) * POINT_SCALE
    d_points = jnp.where(within(l64, 48, 36), gain_l * (out_k - sums * kf), 0.0)
    d_k = jnp.where(l64 < 48, out_k * 0.25, jnp.where(l64 < 84, unrotated(d_points, pat), 0.0))
    d_v = jnp.where(l64 < 48, out_v, jnp.where(l64 < 120, unrotated(out_v, pat), 0.0))
    part_s[0:64, :] = nt(d_k.astype(BF), wk_s[...]) + nt(d_v.astype(BF), wv_s[...])

    exchange = pltpu.make_async_remote_copy(
        src_ref=part_s,
        dst_ref=got_s,
        send_sem=ex_send,
        recv_sem=ex_recv,
        device_id=(row, 1 - core),
        device_id_type=MESH,
    )
    exchange.start()
    for s in range(6):
        for rnd in range(ROUNDS):
            for copy in copies(s, rnd):
                copy.wait_send()
    pltpu.make_async_copy(everyone, everyone, a2a_send).wait()
    exchange.wait()
    o_gk[...] = part_s[0:64, :] + got_s[0:64, :]
    o_out[...] = (part_s[64:65, :] + got_s[64:65, :]).astype(BF)
    o_gq[...] = part_s[72:73, :] + got_s[72:73, :]


def shards(
    query_single, key_single, pair, query_frames, key_frames, w_query, w_key, w_value,
    w_query_points, w_key_points, w_value_points, head_weight, bias_weight, w_out, d_out,
):
    vmem = pl.BlockSpec(memory_space=pltpu.VMEM)
    specs = [vmem] * 15
    specs[2] = pl.BlockSpec(memory_space=pl.ANY)
    specs[11] = pl.BlockSpec(memory_space=pltpu.SMEM)
    dma = pltpu.SemaphoreType.DMA
    return pl.pallas_call(
        kernel,
        out_shape=(
            jax.ShapeDtypeStruct((1, 384), BF),
            jax.ShapeDtypeStruct((1, 384), F32),
            jax.ShapeDtypeStruct((LK, 384), F32),
        ),
        in_specs=specs,
        out_specs=(vmem, vmem, vmem),
        scratch_shapes=[
            pltpu.VMEM((NY, NZ, NX, LK, 128), BF),
            pltpu.VMEM((NY, NZ, NX, LK, 128), BF),
            pltpu.VMEM((K, 128), BF),
            pltpu.VMEM((384, 128), BF),
            pltpu.VMEM((384, 128), BF),
            pltpu.VMEM((384, 128), BF),
            pltpu.VMEM((256, 384), BF),
            pltpu.VMEM((16, 128), F32),
            pltpu.VMEM((16, K), F32),
            pltpu.VMEM((8, K), F32),
            pltpu.VMEM((8, K), F32),
            pltpu.VMEM((8, K), BF),
            pltpu.VMEM((ROWS, 8, 128), BF),
            pltpu.VMEM((ROWS * 8, 128), F32),
            pltpu.VMEM((LK, 1280), F32),
            pltpu.VMEM((80, 384), F32),
            pltpu.VMEM((80, 384), F32),
            dma, dma((6, ROUNDS, 2)), dma((6, ROUNDS, 2)), dma, dma, dma, dma, dma,
        ],
        compiler_params=pltpu.CompilerParams(
            collective_id=0, has_side_effects=True, vmem_limit_bytes=48 * 1024 * 1024
        ),
    )(
        query_single, key_single, pair, query_frames, key_frames, w_query, w_key, w_value,
        w_query_points, w_key_points, w_value_points, head_weight, bias_weight, w_out, d_out,
    )


def solution(mesh):
    return jax.shard_map(
        shards,
        mesh=mesh,
        in_specs=(
            P("row", None),
            P("row", None),
            P("row", None, None),
            P(None, "row"),
            P(None, "row"),
            P(None, "head"),
            P(None, "head"),
            P(None, "head"),
            P(None, "head"),
            P(None, "head"),
            P(None, "head"),
            P("head"),
            P("head", None),
            P("head", None),
            P("row", None),
        ),
        out_specs=(P("row", None), P("row", None), P("row", None)),
        check_vma=False,
    )
```

```python
import functools
import math

import jax
import jax.numpy as jnp
from jax import lax
from jax.experimental import pallas as pl
from jax.experimental.pallas import tpu as pltpu
from jax.sharding import PartitionSpec as P

NY, NZ, NX = 4, 8, 4
ROWS = NY * NZ * NX
LK = 64
K = ROWS * LK
SIZES = (NY, NZ, NX)
LOGIT_SCALE = math.sqrt(1.0 / 3.0)
POINT_SCALE = math.sqrt(2.0 / 36.0)
MESH = pl.DeviceIdType.MESH
BF, F32 = jnp.bfloat16, jnp.float32

STREAMS = (
    (0, 0, 16, (2, 0, 1)),
    (0, 16, 32, (0, 1, 2)),
    (0, 48, 16, (1, 2, 0)),
    (1, 0, 16, (2, 0, 1)),
    (1, 16, 16, (0, 1, 2)),
    (1, 32, 32, (1, 2, 0)),
)
ROUNDS = 8


def nt(a, b):
    return lax.dot_general(a, b, (((1,), (1,)), ((), ())), preferred_element_type=F32)


def nn(a, b):
    return lax.dot_general(a, b, (((1,), (0,)), ((), ())), preferred_element_type=F32)


def tn(a, b, precision=None):
    return lax.dot_general(
        a, b, (((0,), (0,)), ((), ())), preferred_element_type=F32, precision=precision
    )


def iotas(shape):
    return (
        lax.broadcasted_iota(jnp.int32, shape, 0),
        lax.broadcasted_iota(jnp.int32, shape, 1),
    )


def third(value):
    return lax.shift_right_logical(value * 43, 7)


def within(lane, start, count):
    return (lane >= start) & (lane < start + count)


SHIFTS = (0, 1, 2, -1, -2)


def selection():
    j, l = iotas((12, 128))
    x = l - 3 * third(l)
    parts = []
    for d in SHIFTS:
        ok = (x + d >= 0) & (x + d < 3)
        parts.append(ok & (j == 4 * x + d))
    parts.append(j == 9 + x)
    for d in SHIFTS[1:]:
        ok = (x + d >= 0) & (x + d < 3)
        parts.append(ok & (j == 4 * x + 3 * d))
    return jnp.concatenate([jnp.where(p, 1.0, 0.0) for p in parts], axis=1)


def part(pat, i):
    return pat[:, 128 * i : 128 * i + 128]


def shifted(v, d):
    return v if d == 0 else pltpu.roll(v, (-d) % 128, 1)


def rotated(v, pat):
    return sum(part(pat, i) * shifted(v, d) for i, d in enumerate(SHIFTS))


def unrotated(v, pat):
    out = part(pat, 0) * v
    for i, d in enumerate(SHIFTS[1:]):
        out = out + part(pat, 6 + i) * shifted(v, d)
    return out


def softplus(x):
    return jnp.maximum(x, 0.0) + jnp.log1p(jnp.exp(-jnp.abs(x)))


def by_head(index, values):
    return jnp.where(index == 0, values[0], jnp.where(index == 1, values[1], values[2]))


def mask_k(r, l):
    return within(l, 16 * r, 16) & (r < 3), within(l, 48 + 12 * r, 12) & (r < 3)


def mask_v(r, l):
    return (within(l, 16 * r, 16) | within(l, 48 + 24 * r, 24)) & (r < 3)


def kernel(
    qs_h, ks_h, pair, qfr_h, kfr_h, w_q_h, w_k_h, w_v_h, w_qp_h, w_kp_h, w_vp_h, hw_h, bw_h,
    w_o_h, d_o_h,
    o_out, o_gq, o_gk,
    qs, ks, qfr, kfr, w_q, w_k, w_v, w_qp, w_kp, w_vp, hw, bw, w_o, d_o, in_sem,
    buf_k, buf_v, pair_s, wq_s, wk_s, wv_s, wp_s, lhs_s, pb_s, att_s, da_s, msg, recv, recv_f,
    pat_s, part_s, got_s,
    pair_sem, send_sem, recv_sem, a2a_send, a2a_recv, own_sem, ex_send, ex_recv,
):
    row = lax.axis_index("row")
    core = lax.axis_index("head")
    loads = [
        pltpu.make_async_copy(src, dst, in_sem.at[n])
        for n, (src, dst) in enumerate(
            (
                (ks_h, ks), (kfr_h, kfr), (w_k_h, w_k), (w_kp_h, w_kp), (w_v_h, w_v), (w_vp_h, w_vp),
                (qs_h, qs), (qfr_h, qfr), (w_q_h, w_q), (w_qp_h, w_qp), (hw_h, hw), (bw_h, bw),
                (w_o_h, w_o), (d_o_h, d_o),
            )
        )
    ]
    for load in loads:
        load.start()
    coords = (row // (NZ * NX), (row // NX) % NZ, row % NX)

    def neighbour(axis, step):
        moved = list(coords)
        moved[axis] = (coords[axis] + step + SIZES[axis]) % SIZES[axis]
        return (moved[0] * NZ + moved[1]) * NX + moved[2]

    barrier = pltpu.get_barrier_semaphore()
    for axis in range(3):
        for step in (1, -1):
            pl.semaphore_signal(
                barrier, inc=1, device_id=(neighbour(axis, step), core), device_id_type=MESH
            )
    pl.semaphore_signal(barrier, inc=1, device_id=(row, 1 - core), device_id_type=MESH)
    pair_copy = pltpu.make_async_copy(pair.at[0], pair_s, pair_sem)
    pair_copy.start()

    select = selection()
    for load in loads[:6]:
        load.wait()
    wk_s[...] = jnp.zeros_like(wk_s)
    wk_s[0:48, :] = w_k[...]
    wk_s[48:84, :] = w_kp[...]
    wv_s[...] = jnp.zeros_like(wv_s)
    wv_s[0:48, :] = w_v[...]
    wv_s[48:120, :] = w_vp[...]
    pat = tn(kfr[...], select, lax.Precision.HIGHEST)
    pat_s[...] = pat
    r64, l64 = iotas((LK, 128))
    feat = nt(ks[...], wk_s[...])
    k_rows = jnp.where(
        l64 < 48, feat, jnp.where(l64 < 84, rotated(feat, pat) + part(pat, 5), 0.0)
    ).astype(BF)
    k_full = k_rows.astype(F32)
    square = k_full * k_full
    for h in range(3):
        total = jnp.sum(
            jnp.where(within(l64, 48 + 12 * h, 12), square, 0.0), axis=1, keepdims=True
        )
        high = total.astype(BF).astype(F32)
        middle = (total - high).astype(BF).astype(F32)
        low = total - high - middle
        at = 84 + 3 * h
        k_full = jnp.where(
            l64 == at, high, jnp.where(l64 == at + 1, middle, jnp.where(l64 == at + 2, low, k_full))
        )
    feat = nt(ks[...], wv_s[...])
    v_rows = jnp.where(
        l64 < 48, feat, jnp.where(l64 < 120, rotated(feat, pat) + part(pat, 5), 0.0)
    ).astype(BF)
    mine = (pl.ds(coords[0], 1), pl.ds(coords[1], 1), pl.ds(coords[2], 1))
    buf_k[mine] = k_full.astype(BF).reshape(1, 1, 1, LK, 128)
    buf_v[mine] = v_rows.reshape(1, 1, 1, LK, 128)

    bufs = (buf_k, buf_v)

    def copies(s, rnd):
        which, first, count, order = STREAMS[s]
        left = rnd
        for phase, axis in enumerate(order):
            rounds = SIZES[axis] // 2
            if left < rounds:
                break
            left -= rounds
        out = []
        for direction, step in enumerate((1, -1)):
            at = [pl.ds(c, 1) for c in coords]
            for done in order[:phase]:
                at[done] = pl.ds(0, SIZES[done])
            at[axis] = pl.ds((coords[axis] - step * left + SIZES[axis]) % SIZES[axis], 1)
            if left == rounds - 1:
                if phase == 0:
                    if direction != s % 2:
                        continue
                else:
                    split = order[0]
                    at[split] = pl.ds(direction * (SIZES[split] // 2), SIZES[split] // 2)
            where = bufs[which].at[at[0], at[1], at[2], pl.ds(first, count)]
            out.append(
                pltpu.make_async_remote_copy(
                    src_ref=where,
                    dst_ref=where,
                    send_sem=send_sem.at[s, rnd, direction],
                    recv_sem=recv_sem.at[s, rnd, direction],
                    device_id=(neighbour(axis, step), core),
                    device_id_type=MESH,
                )
            )
        return out

    pl.semaphore_wait(barrier, 7)

    def start_round(s, rnd):
        for copy in copies(s, rnd):
            copy.start()

    def end_round(s, rnd):
        for copy in copies(s, rnd):
            copy.wait_recv()

    for s in range(6):
        start_round(s, 0)

    for load in loads[6:]:
        load.wait()
    wq_s[...] = jnp.zeros_like(wq_s)
    wq_s[0:48, :] = w_q[...]
    wq_s[48:84, :] = w_qp[...]
    pat_q = lax.dot_general(
        qfr[...], select, (((1,), (0,)), ((), ())),
        preferred_element_type=F32, precision=lax.Precision.HIGHEST,
    )
    _, l1 = iotas((1, 128))
    x1 = l1 - 3 * third(l1)
    feat = nt(qs[...], wq_s[...])
    q_row = jnp.where(
        l1 < 48, feat, jnp.where(l1 < 84, rotated(feat, pat_q) + part(pat_q, 5), 0.0)
    )
    q_row = q_row.astype(BF).astype(F32)
    r8, l8 = iotas((8, 128))
    raw = [hw[0], hw[1], hw[2]]
    gain = (softplus(by_head(r8, raw)) * POINT_SCALE)[:, 0:1]
    keys8, points8 = mask_k(r8, l8)
    values8 = mask_v(r8, l8)
    q8 = jnp.broadcast_to(q_row, (8, 128))
    q_square = jnp.sum(jnp.where(points8, q8 * q8, 0.0), axis=1, keepdims=True)
    lhs_q = jnp.concatenate(
        [
            jnp.where(keys8, q8, 0.0),
            jnp.where(points8, q8, jnp.where(within(l8, 84 + 3 * r8, 3) & (r8 < 3), -0.5, 0.0)),
        ],
        axis=0,
    ).astype(BF)

    i256, _ = iotas((256, 1))
    i = i256 & 127
    j = i - 48
    head = lax.shift_right_logical(j * 43, 10)
    point = third(j)
    p_head = lax.shift_right_logical(point, 3)
    source = jnp.where(
        i256 < 128,
        jnp.where(i < 48, 176 * lax.shift_right_logical(i, 4) + (i & 15), 152 * head + 16 + j),
        176 * p_head + 40 + (point & 7),
    )
    valid = (i < 120) & ((i256 < 128) | (i >= 48))
    source = jnp.where(valid, source, -1)
    _, lane_o = iotas((256, 528))
    pick = jnp.where(lane_o == source, 1.0, 0.0).astype(BF)
    wp_s[...] = nn(pick, w_o[...]).astype(BF)
    d_feat = nt(d_o[...], wp_s[...])
    lhs_s[...] = jnp.zeros_like(lhs_s)
    lhs_s[0:3, :] = bw[...].astype(F32)
    for h in range(3):
        lhs_s[8 + h : 9 + h, :] = nt(d_o[...], w_o[176 * h + 48 : 176 * h + 176, :])
    lhs_p = lhs_s[...].astype(BF)
    pair_copy.wait()

    def pair_step(g, _):
        at = pl.multiple_of(g * 1024, 1024)
        pb_s[:, pl.ds(at, 1024)] = nt(lhs_p, pair_s[pl.ds(at, 1024), :])
        return 0

    for rnd in range(1, ROUNDS + 1):
        lax.fori_loop(rnd - 1, rnd, pair_step, 0)
        for s in range(6):
            end_round(s, rnd - 1)
            if rnd < ROUNDS:
                start_round(s, rnd)

    def chunk(ref, g):
        return ref[pl.ds(g // 2, 1), pl.ds((g % 2) * 4, 4)].reshape(1024, 128)

    def logit_step(g, top):
        at = pl.multiple_of(g * 1024, 1024)
        both = nt(lhs_q, chunk(buf_k, g))
        logits = LOGIT_SCALE * (
            both[0:8] * 0.25
            + pb_s[0:8, pl.ds(at, 1024)]
            + gain * (both[8:16] - 0.5 * q_square)
        )
        att_s[:, pl.ds(at, 1024)] = logits
        return jnp.maximum(top, jnp.max(logits, axis=1, keepdims=True))

    top = lax.fori_loop(0, 8, logit_step, jnp.full((8, 1), -3.0e38, F32))

    def exp_step(g, total):
        at = pl.multiple_of(g * 1024, 1024)
        e = jnp.exp(att_s[:, pl.ds(at, 1024)] - top)
        att_s[:, pl.ds(at, 1024)] = e
        return total + jnp.sum(e, axis=1, keepdims=True)

    total = lax.fori_loop(0, 8, exp_step, jnp.zeros((8, 1), F32))

    def attend_step(g, carry):
        acc_v, acc_p = carry
        at = pl.multiple_of(g * 1024, 1024)
        a = att_s[:, pl.ds(at, 1024)] / total
        att_s[:, pl.ds(at, 1024)] = a
        a = a.astype(BF)
        return (
            acc_v + nn(a, chunk(buf_v, g)),
            acc_p + nn(a, pair_s[pl.ds(at, 1024), :]),
        )

    zero8 = jnp.zeros((8, 128), F32)
    acc_v, acc_p = lax.fori_loop(0, 8, attend_step, (zero8, zero8))
    row_v = jnp.sum(jnp.where(values8, acc_v, 0.0), axis=0, keepdims=True)
    is_point = within(l1, 48, 72)
    local = jnp.where(is_point, unrotated(jnp.where(is_point, row_v - part(pat_q, 5), 0.0), pat_q), 0.0)
    squares = local * local
    norm = squares
    for d in SHIFTS[1:]:
        norm = norm + jnp.where((x1 + d >= 0) & (x1 + d < 3), shifted(squares, d), 0.0)
    lengths = jnp.sqrt(1.0 + norm)
    f_v = jnp.where(l1 < 48, row_v, local).astype(BF)
    f_len = jnp.where(is_point & (x1 == 0), lengths, 0.0).astype(BF)
    out_row = nn(f_v, wp_s[0:128, :]) + nn(f_len, wp_s[128:256, :])
    for h in range(3):
        out_row = out_row + nn(
            acc_p[h : h + 1, :].astype(BF), w_o[176 * h + 48 : 176 * h + 176, :]
        )
    part_s[64:65, :] = out_row

    d_local = d_feat[:, 0:128] + d_feat[:, 128:256] / lengths * local
    d_local = jnp.where(is_point, d_local, 0.0)
    side_v = jnp.where(
        l1 < 48, d_feat[:, 0:128], jnp.where(is_point, rotated(d_local, pat_q), 0.0)
    )
    side_v8 = jnp.broadcast_to(side_v, (8, 128))
    lhs_v = jnp.where(values8, side_v8, 0.0).astype(BF)

    def grad_step(g, carry):
        at = pl.multiple_of(g * 1024, 1024)
        d_att = nt(lhs_v, chunk(buf_v, g)) + pb_s[8:16, pl.ds(at, 1024)]
        da_s[:, pl.ds(at, 1024)] = d_att
        return carry + jnp.sum(att_s[:, pl.ds(at, 1024)] * d_att, axis=1, keepdims=True)

    row_total = lax.fori_loop(0, 8, grad_step, jnp.zeros((8, 1), F32))
    side = jnp.where(r8 == 6, q8, jnp.where(r8 == 7, side_v8, 0.0))
    side = jnp.concatenate([side] * 8, axis=1)
    rc, _ = iotas((8, 1024))

    def score_step(g, carry):
        acc, sums = carry
        at = pl.multiple_of(g * 1024, 1024)
        a = att_s[:, pl.ds(at, 1024)]
        score = LOGIT_SCALE * a * (da_s[:, pl.ds(at, 1024)] - row_total)
        out = jnp.where(rc < 3, a, jnp.where(rc < 6, pltpu.roll(score, 3, 0), side))
        msg[:, pl.ds(at, 1024)] = out.astype(BF)
        score = score.astype(BF)
        acc = acc + nn(score, chunk(buf_k, g))
        return acc, sums + jnp.sum(score.astype(F32), axis=1, keepdims=True)

    acc_k, score_rows = lax.fori_loop(0, 8, score_step, (zero8, jnp.zeros((8, 1), F32)))

    def tile(device):
        return msg.at[:, pl.ds(pl.multiple_of((device // 2) * 128, 128), 128)]

    def send_step(i, _):
        target = (row + i) % ROWS
        pltpu.make_async_remote_copy(
            src_ref=tile(target),
            dst_ref=recv.at[row],
            send_sem=a2a_send,
            recv_sem=a2a_recv,
            device_id=(target, core),
            device_id_type=MESH,
        ).start()
        return 0

    own = pltpu.make_async_copy(tile(row), recv.at[row], own_sem)
    own.start()
    lax.fori_loop(1, ROWS, send_step, 0)

    q_terms = jnp.where(keys8, acc_k * 0.25, 0.0) + jnp.where(
        points8, gain * (acc_k - score_rows * q8), 0.0
    )
    d_q = jnp.sum(q_terms, axis=0, keepdims=True)
    d_q = jnp.where(l1 < 48, d_q, jnp.where(l1 < 84, unrotated(d_q, pat_q), 0.0)).astype(BF)
    part_s[72:73, :] = nn(d_q, wq_s[...])

    own.wait()
    everyone = recv.at[pl.ds(0, ROWS - 1)]
    pltpu.make_async_copy(everyone, everyone, a2a_recv).wait()

    def unpack_step(i, _):
        at = pl.multiple_of(i * 64, 64)
        recv_f[pl.ds(at, 64), :] = recv[pl.ds(i * 8, 8)].astype(F32).reshape(64, 128)
        return 0

    lax.fori_loop(0, ROWS // 8, unpack_step, 0)

    def every(i):
        return recv_f[pl.ds(i, ROWS, stride=8), :]

    side_k, side_v = every(6), every(7)
    _, l128 = iotas((ROWS, 128))
    out_k = out_v = sums = jnp.zeros((128, 128), F32)
    for h in range(3):
        keys_h = within(l128, 16 * h, 16)
        points_h = within(l128, 48 + 12 * h, 12)
        vpoints_h = within(l128, 48 + 24 * h, 24)
        att_h, score_h = every(h).astype(BF), every(3 + h).astype(BF)
        out_v = out_v + tn(att_h, jnp.where(keys_h | vpoints_h, side_v, 0.0).astype(BF))
        out_k = out_k + tn(score_h, jnp.where(keys_h | points_h, side_k, 0.0).astype(BF))
        sums = sums + tn(score_h, jnp.where(points_h, 1.0, 0.0).astype(BF))
    odd = row % 2 == 1

    def mine_of(x):
        return jnp.where(odd, x[64:128], x[0:64])

    out_k, out_v, sums = mine_of(out_k), mine_of(out_v), mine_of(sums)
    pat = pat_s[...]
    kf = buf_k[mine].reshape(LK, 128).astype(F32)
    gain_l = softplus(by_head(jnp.where(l1 < 60, 0, jnp.where(l1 < 72, 1, 2)), raw)) * POINT_SCALE
    d_points = jnp.where(within(l64, 48, 36), gain_l * (out_k - sums * kf), 0.0)
    d_k = jnp.where(l64 < 48, out_k * 0.25, jnp.where(l64 < 84, unrotated(d_points, pat), 0.0))
    d_v = jnp.where(l64 < 48, out_v, jnp.where(l64 < 120, unrotated(out_v, pat), 0.0))
    part_s[0:64, :] = nn(d_k.astype(BF), wk_s[...]) + nn(d_v.astype(BF), wv_s[...])

    exchange = pltpu.make_async_remote_copy(
        src_ref=part_s,
        dst_ref=got_s,
        send_sem=ex_send,
        recv_sem=ex_recv,
        device_id=(row, 1 - core),
        device_id_type=MESH,
    )
    exchange.start()
    for s in range(6):
        for rnd in range(ROUNDS):
            for copy in copies(s, rnd):
                copy.wait_send()
    pltpu.make_async_copy(everyone, everyone, a2a_send).wait()
    exchange.wait()
    o_gk[...] = part_s[0:64, :] + got_s[0:64, :]
    o_out[...] = (part_s[64:65, :] + got_s[64:65, :]).astype(BF)
    o_gq[...] = part_s[72:73, :] + got_s[72:73, :]


def shards(
    query_single, key_single, pair, query_frames, key_frames, w_query, w_key, w_value,
    w_query_points, w_key_points, w_value_points, head_weight, bias_weight, w_out, d_out,
):
    vmem = pl.BlockSpec(memory_space=pltpu.VMEM)
    specs = [pl.BlockSpec(memory_space=pltpu.HBM)] * 15
    dma = pltpu.SemaphoreType.DMA
    return pl.pallas_call(
        kernel,
        out_shape=(
            jax.ShapeDtypeStruct((1, 384), BF),
            jax.ShapeDtypeStruct((1, 384), F32),
            jax.ShapeDtypeStruct((LK, 384), F32),
        ),
        in_specs=specs,
        out_specs=(vmem, vmem, vmem),
        scratch_shapes=[
            pltpu.VMEM((1, 384), BF),
            pltpu.VMEM((LK, 384), BF),
            pltpu.VMEM((1, 12), F32),
            pltpu.VMEM((12, LK), F32),
            pltpu.VMEM((48, 384), BF),
            pltpu.VMEM((48, 384), BF),
            pltpu.VMEM((48, 384), BF),
            pltpu.VMEM((36, 384), BF),
            pltpu.VMEM((36, 384), BF),
            pltpu.VMEM((72, 384), BF),
            pltpu.SMEM((3,), F32),
            pltpu.VMEM((3, 128), BF),
            pltpu.VMEM((528, 384), BF),
            pltpu.VMEM((1, 384), BF),
            pltpu.SemaphoreType.DMA((14,)),
            pltpu.VMEM((NY, NZ, NX, LK, 128), BF),
            pltpu.VMEM((NY, NZ, NX, LK, 128), BF),
            pltpu.VMEM((K, 128), BF),
            pltpu.VMEM((128, 384), BF),
            pltpu.VMEM((128, 384), BF),
            pltpu.VMEM((128, 384), BF),
            pltpu.VMEM((256, 384), BF),
            pltpu.VMEM((16, 128), F32),
            pltpu.VMEM((16, K), F32),
            pltpu.VMEM((8, K), F32),
            pltpu.VMEM((8, K), F32),
            pltpu.VMEM((8, K), BF),
            pltpu.VMEM((ROWS, 8, 128), BF),
            pltpu.VMEM((ROWS * 8, 128), F32),
            pltpu.VMEM((LK, 1280), F32),
            pltpu.VMEM((80, 384), F32),
            pltpu.VMEM((80, 384), F32),
            dma, dma((6, ROUNDS, 2)), dma((6, ROUNDS, 2)), dma, dma, dma, dma, dma,
        ],
        compiler_params=pltpu.CompilerParams(
            collective_id=0, has_side_effects=True, vmem_limit_bytes=67043328
        ),
    )(
        query_single, key_single, pair, query_frames.T, key_frames, w_query.T, w_key.T, w_value.T,
        w_query_points.T, w_key_points.T, w_value_points.T, head_weight, bias_weight, w_out, d_out,
    )


def solution(mesh):
    return jax.shard_map(
        shards,
        mesh=mesh,
        in_specs=(
            P("row", None),
            P("row", None),
            P("row", None, None),
            P(None, "row"),
            P(None, "row"),
            P(None, "head"),
            P(None, "head"),
            P(None, "head"),
            P(None, "head"),
            P(None, "head"),
            P(None, "head"),
            P("head"),
            P("head", None),
            P("head", None),
            P("row", None),
        ),
        out_specs=(P("row", None), P("row", None), P("row", None)),
        check_vma=False,
    )
```

```python
import functools
import math

import jax
import jax.numpy as jnp
from jax import lax
from jax.experimental import pallas as pl
from jax.experimental.pallas import tpu as pltpu
from jax.sharding import PartitionSpec as P

NY, NZ, NX = 4, 8, 4
ROWS = NY * NZ * NX
LK = 64
K = ROWS * LK
SIZES = (NY, NZ, NX)
LOGIT_SCALE = math.sqrt(1.0 / 3.0)
POINT_SCALE = math.sqrt(2.0 / 36.0)
MESH = pl.DeviceIdType.MESH
BF, F32 = jnp.bfloat16, jnp.float32

STREAMS = (
    (0, 0, 32, (0, 1, 2)),
    (0, 32, 32, (2, 1, 0)),
    (1, 0, 32, (0, 1, 2)),
    (1, 32, 32, (2, 1, 0)),
)
SLOTS = 7


def gather_plan():
    plan = []

    def add(rnd, name, needs, axis, step, offsets, half=None):
        plan.append((rnd, name, needs, axis, step, offsets, half))

    for sign, mark in ((1, "+"), (-1, "-")):
        add(0, "a" + mark, (), 0, sign, (0, 0, 0))
    add(0, "b", (), 0, 2, (0, 0, 0))
    first = ("a+", "a-", "b")
    for k in range(NZ // 2):
        for sign, mark in ((1, "+"), (-1, "-")):
            needs = first if k == 0 else ("c%d%s" % (k - 1, mark),)
            half = "blocks" if k == NZ // 2 - 1 else None
            add(1 + k, "c%d%s" % (k, mark), needs, 1, sign, (None, -sign * k, 0), half)
    for k in range(NZ // 2 + 1):
        for side in (1, -1) if 0 < k < NZ // 2 else (1,):
            offset = -side * k
            if k == 0:
                needs = first
            elif k == NZ // 2:
                needs = ("c%d+" % (k - 1), "c%d-" % (k - 1))
            else:
                needs = ("c%d%s" % (k - 1, "+" if side == 1 else "-"),)
            for sign, mark in ((1, "+"), (-1, "-")):
                name = "%d%s" % (offset, mark)
                add(1 + k, "d" + name, needs, 2, sign, (None, offset, 0))
                if k < NZ // 2:
                    add(2 + k, "e" + name, ("d" + name,), 2, sign, (None, offset, -sign), "blocks")
            if k == NZ // 2:
                add(1 + k, "e%d" % offset, needs, 2, 2, (None, offset, 0))
    return sorted(plan, key=lambda item: (item[0], item[1]))


PLAN = gather_plan()
NUMBER = {item[1]: n for n, item in enumerate(PLAN)}


def nt(a, b):
    return lax.dot_general(a, b, (((1,), (1,)), ((), ())), preferred_element_type=F32)


def nn(a, b):
    return lax.dot_general(a, b, (((1,), (0,)), ((), ())), preferred_element_type=F32)


def tn(a, b, precision=None):
    return lax.dot_general(
        a, b, (((0,), (0,)), ((), ())), preferred_element_type=F32, precision=precision
    )


def iotas(shape):
    return (
        lax.broadcasted_iota(jnp.int32, shape, 0),
        lax.broadcasted_iota(jnp.int32, shape, 1),
    )


def third(value):
    return lax.shift_right_logical(value * 43, 7)


def within(lane, start, count):
    return (lane >= start) & (lane < start + count)


SHIFTS = (0, 1, 2, -1, -2)


def selection():
    j, l = iotas((12, 128))
    x = l - 3 * third(l)
    parts = []
    for d in SHIFTS:
        ok = (x + d >= 0) & (x + d < 3)
        parts.append(ok & (j == 4 * x + d))
    parts.append(j == 9 + x)
    for d in SHIFTS[1:]:
        ok = (x + d >= 0) & (x + d < 3)
        parts.append(ok & (j == 4 * x + 3 * d))
    return jnp.concatenate([jnp.where(p, 1.0, 0.0) for p in parts], axis=1)


def part(pat, i):
    return pat[:, 128 * i : 128 * i + 128]


def shifted(v, d):
    return v if d == 0 else pltpu.roll(v, (-d) % 128, 1)


def rotated(v, pat):
    return sum(part(pat, i) * shifted(v, d) for i, d in enumerate(SHIFTS))


def unrotated(v, pat):
    out = part(pat, 0) * v
    for i, d in enumerate(SHIFTS[1:]):
        out = out + part(pat, 6 + i) * shifted(v, d)
    return out


def softplus(x):
    return jnp.maximum(x, 0.0) + jnp.log1p(jnp.exp(-jnp.abs(x)))


def by_head(index, values):
    return jnp.where(index == 0, values[0], jnp.where(index == 1, values[1], values[2]))


def mask_k(r, l):
    return within(l, 16 * r, 16) & (r < 3), within(l, 48 + 12 * r, 12) & (r < 3)


def mask_v(r, l):
    return (within(l, 16 * r, 16) | within(l, 48 + 24 * r, 24)) & (r < 3)


def kernel(
    qs_h, ks_h, pair, qfr_h, kfr_h, w_q_h, w_k_h, w_v_h, w_qp_h, w_kp_h, w_vp_h, hw_h, bw_h,
    w_o_h, d_o_h,
    o_sum,
    qs, ks, qfr, kfr, w_q, w_k, w_v, w_qp, w_kp, w_vp, hw, bw, w_o, d_o, in_sem,
    buf_k, buf_v, pair_s, wq_s, wk_s, wv_s, wp_s, lhs_s, pb_s, att_s, da_s, msg_a, msg_s, recv_a, recv_s, unpack_a, unpack_s,
    pat_s, part_s, got_s,
    pair_sem, send_sem, recv_sem, a_send, a_recv, s_send, s_recv, own_sem, ex_send, ex_recv,
):
    row = lax.axis_index("row")
    core = lax.axis_index("head")
    loads = [
        pltpu.make_async_copy(src, dst, in_sem.at[n])
        for n, (src, dst) in enumerate(
            (
                (ks_h, ks), (kfr_h, kfr), (w_k_h, w_k), (w_kp_h, w_kp), (w_v_h, w_v), (w_vp_h, w_vp),
                (qs_h, qs), (qfr_h, qfr), (w_q_h, w_q), (w_qp_h, w_qp), (hw_h, hw), (bw_h, bw),
                (w_o_h, w_o), (d_o_h, d_o),
            )
        )
    ]
    for load in loads:
        load.start()
    coords = (row // (NZ * NX), (row // NX) % NZ, row % NX)

    def neighbour(axis, step):
        moved = list(coords)
        moved[axis] = (coords[axis] + step + SIZES[axis]) % SIZES[axis]
        return (moved[0] * NZ + moved[1]) * NX + moved[2]

    barrier = pltpu.get_barrier_semaphore()
    for axis, steps in ((0, (1, -1, 2)), (1, (1, -1)), (2, (1, -1, 2))):
        for step in steps:
            pl.semaphore_signal(
                barrier, inc=1, device_id=(neighbour(axis, step), core), device_id_type=MESH
            )
    pl.semaphore_signal(barrier, inc=1, device_id=(row, 1 - core), device_id_type=MESH)
    pair_copy = pltpu.make_async_copy(pair.at[0], pair_s, pair_sem)
    pair_copy.start()

    select = selection()
    for load in loads[:6]:
        load.wait()
    wk_s[...] = jnp.zeros_like(wk_s)
    wk_s[0:48, :] = w_k[...]
    wk_s[48:84, :] = w_kp[...]
    wv_s[...] = jnp.zeros_like(wv_s)
    wv_s[0:48, :] = w_v[...]
    wv_s[48:120, :] = w_vp[...]
    pat = tn(kfr[...], select, lax.Precision.HIGHEST)
    pat_s[...] = pat
    r64, l64 = iotas((LK, 128))
    feat = nt(ks[...], wk_s[...])
    k_rows = jnp.where(
        l64 < 48, feat, jnp.where(l64 < 84, rotated(feat, pat) + part(pat, 5), 0.0)
    ).astype(BF)
    k_full = k_rows.astype(F32)
    square = k_full * k_full
    for h in range(3):
        total = jnp.sum(
            jnp.where(within(l64, 48 + 12 * h, 12), square, 0.0), axis=1, keepdims=True
        )
        high = total.astype(BF).astype(F32)
        middle = (total - high).astype(BF).astype(F32)
        low = total - high - middle
        at = 84 + 3 * h
        k_full = jnp.where(
            l64 == at, high, jnp.where(l64 == at + 1, middle, jnp.where(l64 == at + 2, low, k_full))
        )
    feat = nt(ks[...], wv_s[...])
    v_rows = jnp.where(
        l64 < 48, feat, jnp.where(l64 < 120, rotated(feat, pat) + part(pat, 5), 0.0)
    ).astype(BF)
    mine = (pl.ds(coords[0], 1), pl.ds(coords[1], 1), pl.ds(coords[2], 1))
    buf_k[mine] = k_full.astype(BF).reshape(1, 1, 1, LK, 128)
    buf_v[mine] = v_rows.reshape(1, 1, 1, LK, 128)

    bufs = (buf_k, buf_v)

    seen = [set() for _ in STREAMS]

    def gather_copy(s, item):
        which, start, count, order = STREAMS[s]
        _, name, _, axis, step, offsets, half = item
        at = [None] * 3
        for a, offset in zip(order, offsets):
            if offset is None:
                at[a] = pl.ds(0, SIZES[a])
            elif offset == 0:
                at[a] = pl.ds(coords[a], 1)
            else:
                at[a] = pl.ds((coords[a] + offset + SIZES[a]) % SIZES[a], 1)
        second = 0 if step == 1 else 1
        if half == "blocks":
            a = order[0]
            at[a] = pl.ds(second * (SIZES[a] // 2), SIZES[a] // 2)
        where = bufs[which].at[at[0], at[1], at[2], pl.ds(start, count)]
        n = NUMBER[name]
        return pltpu.make_async_remote_copy(
            src_ref=where,
            dst_ref=where,
            send_sem=send_sem.at[s, n],
            recv_sem=recv_sem.at[s, n],
            device_id=(neighbour(order[axis], step), core),
            device_id_type=MESH,
        )

    def arrive(s, name):
        if name not in seen[s]:
            seen[s].add(name)
            gather_copy(s, PLAN[NUMBER[name]]).wait_recv()

    def gather_round(s, rnd):
        for item in PLAN:
            if item[0] == rnd:
                for name in item[2]:
                    arrive(s, name)
                gather_copy(s, item).start()
        if rnd == SLOTS - 1:
            for item in PLAN:
                arrive(s, item[1])

    def gather_slot(slot):
        for s in range(4):
            gather_round(s, slot)

    pl.semaphore_wait(barrier, 9)
    gather_slot(0)

    for load in loads[6:]:
        load.wait()
    wq_s[...] = jnp.zeros_like(wq_s)
    wq_s[0:48, :] = w_q[...]
    wq_s[48:84, :] = w_qp[...]
    pat_q = lax.dot_general(
        qfr[...], select, (((1,), (0,)), ((), ())),
        preferred_element_type=F32, precision=lax.Precision.HIGHEST,
    )
    _, l1 = iotas((1, 128))
    x1 = l1 - 3 * third(l1)
    feat = nt(qs[...], wq_s[...])
    q_row = jnp.where(
        l1 < 48, feat, jnp.where(l1 < 84, rotated(feat, pat_q) + part(pat_q, 5), 0.0)
    )
    q_row = q_row.astype(BF).astype(F32)
    r8, l8 = iotas((8, 128))
    raw = [hw[0], hw[1], hw[2]]
    gain = (softplus(by_head(r8, raw)) * POINT_SCALE)[:, 0:1]
    keys8, points8 = mask_k(r8, l8)
    values8 = mask_v(r8, l8)
    q8 = jnp.broadcast_to(q_row, (8, 128))
    q_square = jnp.sum(jnp.where(points8, q8 * q8, 0.0), axis=1, keepdims=True)
    lhs_q = jnp.concatenate(
        [
            jnp.where(keys8, q8, 0.0),
            jnp.where(points8, q8, jnp.where(within(l8, 84 + 3 * r8, 3) & (r8 < 3), -0.5, 0.0)),
        ],
        axis=0,
    ).astype(BF)

    i256, _ = iotas((256, 1))
    i = i256 & 127
    j = i - 48
    head = lax.shift_right_logical(j * 43, 10)
    point = third(j)
    p_head = lax.shift_right_logical(point, 3)
    source = jnp.where(
        i256 < 128,
        jnp.where(i < 48, 176 * lax.shift_right_logical(i, 4) + (i & 15), 152 * head + 16 + j),
        176 * p_head + 40 + (point & 7),
    )
    valid = (i < 120) & ((i256 < 128) | (i >= 48))
    source = jnp.where(valid, source, -1)
    _, lane_o = iotas((256, 528))
    pick = jnp.where(lane_o == source, 1.0, 0.0).astype(BF)
    wp_s[...] = nn(pick, w_o[...]).astype(BF)
    d_feat = nt(d_o[...], wp_s[...])
    lhs_s[...] = jnp.zeros_like(lhs_s)
    lhs_s[0:3, :] = bw[...].astype(F32)
    for h in range(3):
        lhs_s[8 + h : 9 + h, :] = nt(d_o[...], w_o[176 * h + 48 : 176 * h + 176, :])
    lhs_p = lhs_s[...].astype(BF)
    pair_copy.wait()

    def pair_step(g, _):
        at = pl.multiple_of(g * 1024, 1024)
        pb_s[:, pl.ds(at, 1024)] = nt(lhs_p, pair_s[pl.ds(at, 1024), :])
        return 0

    for slot in range(1, SLOTS - 1):
        lax.fori_loop((slot - 1) * 8 // (SLOTS - 2), slot * 8 // (SLOTS - 2), pair_step, 0)
        gather_slot(slot)
    gather_slot(SLOTS - 1)

    def chunk(ref, g):
        return ref[pl.ds(g // 2, 1), pl.ds((g % 2) * 4, 4)].reshape(1024, 128)

    def logit_step(g, top):
        at = pl.multiple_of(g * 1024, 1024)
        both = nt(lhs_q, chunk(buf_k, g))
        logits = LOGIT_SCALE * (
            both[0:8] * 0.25
            + pb_s[0:8, pl.ds(at, 1024)]
            + gain * (both[8:16] - 0.5 * q_square)
        )
        att_s[:, pl.ds(at, 1024)] = logits
        return jnp.maximum(top, jnp.max(logits, axis=1, keepdims=True))

    top = lax.fori_loop(0, 8, logit_step, jnp.full((8, 1), -3.0e38, F32))

    def exp_step(g, total):
        at = pl.multiple_of(g * 1024, 1024)
        e = jnp.exp(att_s[:, pl.ds(at, 1024)] - top)
        att_s[:, pl.ds(at, 1024)] = e
        return total + jnp.sum(e, axis=1, keepdims=True)

    total = lax.fori_loop(0, 8, exp_step, jnp.zeros((8, 1), F32))

    rotate = row // 16
    rc, _ = iotas((8, 1024))

    def start_sends(message, landing, send, recv, g):
        for n in range(16):
            target = g * 16 + (row + n) % 16

            def start(target=target):
                at = pl.multiple_of((target // 2) * 128, 128)
                pltpu.make_async_remote_copy(
                    src_ref=message.at[:, pl.ds(at, 128)],
                    dst_ref=landing.at[row],
                    send_sem=send,
                    recv_sem=recv,
                    device_id=(target, core),
                    device_id_type=MESH,
                ).start()

            if n:
                start()
            else:
                pl.when(target != row)(start)

    def own_copy(message, landing):
        at = pl.multiple_of((row // 2) * 128, 128)
        return pltpu.make_async_copy(message.at[:, pl.ds(at, 128)], landing.at[row], own_sem)

    def all_of(landing, sem):
        everyone = landing.at[pl.ds(0, ROWS - 1)]
        return pltpu.make_async_copy(everyone, everyone, sem)

    def attend_step(i, carry):
        acc_v, acc_p = carry
        g = (i + rotate) % 8

        @pl.when(i > 0)
        def _():
            start_sends(msg_a, recv_a, a_send, a_recv, (i - 1 + rotate) % 8)

        at = pl.multiple_of(g * 1024, 1024)
        a = att_s[:, pl.ds(at, 1024)] / total
        att_s[:, pl.ds(at, 1024)] = a
        msg_a[:, pl.ds(at, 1024)] = jnp.where(rc < 3, a, side_k)[0:4].astype(BF)
        a = a.astype(BF)
        return (
            acc_v + nn(a, chunk(buf_v, g)),
            acc_p + nn(a, pair_s[pl.ds(at, 1024), :]),
        )

    side_k = jnp.concatenate([q8] * 8, axis=1)
    zero8 = jnp.zeros((8, 128), F32)
    acc_v, acc_p = lax.fori_loop(0, 8, attend_step, (zero8, zero8))
    start_sends(msg_a, recv_a, a_send, a_recv, (7 + rotate) % 8)
    own_a = own_copy(msg_a, recv_a)
    own_a.start()
    row_v = jnp.sum(jnp.where(values8, acc_v, 0.0), axis=0, keepdims=True)
    is_point = within(l1, 48, 72)
    local = jnp.where(is_point, unrotated(jnp.where(is_point, row_v - part(pat_q, 5), 0.0), pat_q), 0.0)
    squares = local * local
    norm = squares
    for d in SHIFTS[1:]:
        norm = norm + jnp.where((x1 + d >= 0) & (x1 + d < 3), shifted(squares, d), 0.0)
    lengths = jnp.sqrt(1.0 + norm)
    f_v = jnp.where(l1 < 48, row_v, local).astype(BF)
    f_len = jnp.where(is_point & (x1 == 0), lengths, 0.0).astype(BF)
    out_row = nn(f_v, wp_s[0:128, :]) + nn(f_len, wp_s[128:256, :])
    for h in range(3):
        out_row = out_row + nn(
            acc_p[h : h + 1, :].astype(BF), w_o[176 * h + 48 : 176 * h + 176, :]
        )
    part_s[64:65, :] = out_row

    d_local = d_feat[:, 0:128] + d_feat[:, 128:256] / lengths * local
    d_local = jnp.where(is_point, d_local, 0.0)
    side_v = jnp.where(
        l1 < 48, d_feat[:, 0:128], jnp.where(is_point, rotated(d_local, pat_q), 0.0)
    )
    side_v8 = jnp.broadcast_to(side_v, (8, 128))
    lhs_v = jnp.where(values8, side_v8, 0.0).astype(BF)

    def grad_step(g, carry):
        at = pl.multiple_of(g * 1024, 1024)
        d_att = nt(lhs_v, chunk(buf_v, g)) + pb_s[8:16, pl.ds(at, 1024)]
        da_s[:, pl.ds(at, 1024)] = d_att
        return carry + jnp.sum(att_s[:, pl.ds(at, 1024)] * d_att, axis=1, keepdims=True)

    row_total = lax.fori_loop(0, 8, grad_step, jnp.zeros((8, 1), F32))
    side_v = jnp.concatenate([side_v8] * 8, axis=1)

    def score_step(i, carry):
        acc, sums = carry
        g = (i + rotate) % 8

        @pl.when(i > 0)
        def _():
            start_sends(msg_s, recv_s, s_send, s_recv, (i - 1 + rotate) % 8)

        at = pl.multiple_of(g * 1024, 1024)
        a = att_s[:, pl.ds(at, 1024)]
        score = LOGIT_SCALE * a * (da_s[:, pl.ds(at, 1024)] - row_total)
        msg_s[:, pl.ds(at, 1024)] = jnp.where(rc < 3, score, side_v)[0:4].astype(BF)
        score = score.astype(BF)
        acc = acc + nn(score, chunk(buf_k, g))
        return acc, sums + jnp.sum(score.astype(F32), axis=1, keepdims=True)

    acc_k, score_rows = lax.fori_loop(0, 8, score_step, (zero8, jnp.zeros((8, 1), F32)))
    start_sends(msg_s, recv_s, s_send, s_recv, (7 + rotate) % 8)
    own_a.wait()
    own_s = own_copy(msg_s, recv_s)
    own_s.start()

    q_terms = jnp.where(keys8, acc_k * 0.25, 0.0) + jnp.where(
        points8, gain * (acc_k - score_rows * q8), 0.0
    )
    d_q = jnp.sum(q_terms, axis=0, keepdims=True)
    d_q = jnp.where(l1 < 48, d_q, jnp.where(l1 < 84, unrotated(d_q, pat_q), 0.0)).astype(BF)
    part_s[72:73, :] = nn(d_q, wq_s[...])

    _, l128 = iotas((ROWS, 128))

    def unpack(landing, unpacked):
        def step(i, _):
            at = pl.multiple_of(i * 32, 32)
            unpacked[pl.ds(at, 32), :] = landing[pl.ds(i * 8, 8)].astype(F32).reshape(32, 128)
            return 0

        lax.fori_loop(0, ROWS // 8, step, 0)
        return [unpacked[pl.ds(n, ROWS, stride=4), :] for n in range(4)]

    all_of(recv_a, a_recv).wait()
    *att_h, side_k = unpack(recv_a, unpack_a)
    all_of(recv_s, s_recv).wait()
    own_s.wait()
    *score_h, side_v = unpack(recv_s, unpack_s)
    out_k = out_v = sums = jnp.zeros((128, 128), F32)
    for h in range(3):
        keys_h = within(l128, 16 * h, 16)
        points_h = within(l128, 48 + 12 * h, 12)
        vpoints_h = within(l128, 48 + 24 * h, 24)
        score = score_h[h].astype(BF)
        out_v = out_v + tn(
            att_h[h].astype(BF), jnp.where(keys_h | vpoints_h, side_v, 0.0).astype(BF)
        )
        out_k = out_k + tn(score, jnp.where(keys_h | points_h, side_k, 0.0).astype(BF))
        sums = sums + tn(score, jnp.where(points_h, 1.0, 0.0).astype(BF))
    odd = row % 2 == 1

    def mine_of(x):
        return jnp.where(odd, x[64:128], x[0:64])

    out_k, out_v, sums = mine_of(out_k), mine_of(out_v), mine_of(sums)
    pat = pat_s[...]
    kf = buf_k[mine].reshape(LK, 128).astype(F32)
    gain_l = softplus(by_head(jnp.where(l1 < 60, 0, jnp.where(l1 < 72, 1, 2)), raw)) * POINT_SCALE
    d_points = jnp.where(within(l64, 48, 36), gain_l * (out_k - sums * kf), 0.0)
    d_k = jnp.where(l64 < 48, out_k * 0.25, jnp.where(l64 < 84, unrotated(d_points, pat), 0.0))
    d_v = jnp.where(l64 < 48, out_v, jnp.where(l64 < 120, unrotated(out_v, pat), 0.0))
    part_s[0:64, :] = nn(d_k.astype(BF), wk_s[...]) + nn(d_v.astype(BF), wv_s[...])

    exchange = pltpu.make_async_remote_copy(
        src_ref=part_s,
        dst_ref=got_s,
        send_sem=ex_send,
        recv_sem=ex_recv,
        device_id=(row, 1 - core),
        device_id_type=MESH,
    )
    exchange.start()
    for s in range(4):
        for item in PLAN:
            gather_copy(s, item).wait_send()
    all_of(recv_a, a_send).wait()
    all_of(recv_s, s_send).wait()
    exchange.wait()
    o_sum[...] = part_s[...] + got_s[...]


def finish(total, o_out, o_gq, o_gk):
    o_gk[...] = total[0:64, :]
    o_out[...] = total[64:65, :].astype(BF)
    o_gq[...] = total[72:73, :]


def shards(
    query_single, key_single, pair, query_frames, key_frames, w_query, w_key, w_value,
    w_query_points, w_key_points, w_value_points, head_weight, bias_weight, w_out, d_out,
):
    vmem = pl.BlockSpec(memory_space=pltpu.VMEM)
    specs = [pl.BlockSpec(memory_space=pltpu.HBM)] * 15
    dma = pltpu.SemaphoreType.DMA
    total = pl.pallas_call(
        kernel,
        out_shape=jax.ShapeDtypeStruct((80, 384), F32),
        in_specs=specs,
        out_specs=vmem,
        scratch_shapes=[
            pltpu.VMEM((1, 384), BF),
            pltpu.VMEM((LK, 384), BF),
            pltpu.VMEM((1, 12), F32),
            pltpu.VMEM((12, LK), F32),
            pltpu.VMEM((48, 384), BF),
            pltpu.VMEM((48, 384), BF),
            pltpu.VMEM((48, 384), BF),
            pltpu.VMEM((36, 384), BF),
            pltpu.VMEM((36, 384), BF),
            pltpu.VMEM((72, 384), BF),
            pltpu.SMEM((3,), F32),
            pltpu.VMEM((3, 128), BF),
            pltpu.VMEM((528, 384), BF),
            pltpu.VMEM((1, 384), BF),
            pltpu.SemaphoreType.DMA((14,)),
            pltpu.VMEM((NY, NZ, NX, LK, 128), BF),
            pltpu.VMEM((NY, NZ, NX, LK, 128), BF),
            pltpu.VMEM((K, 128), BF),
            pltpu.VMEM((128, 384), BF),
            pltpu.VMEM((128, 384), BF),
            pltpu.VMEM((128, 384), BF),
            pltpu.VMEM((256, 384), BF),
            pltpu.VMEM((16, 128), F32),
            pltpu.VMEM((16, K), F32),
            pltpu.VMEM((8, K), F32),
            pltpu.VMEM((8, K), F32),
            pltpu.VMEM((4, K), BF),
            pltpu.VMEM((4, K), BF),
            pltpu.VMEM((ROWS, 4, 128), BF),
            pltpu.VMEM((ROWS, 4, 128), BF),
            pltpu.VMEM((ROWS * 4, 128), F32),
            pltpu.VMEM((ROWS * 4, 128), F32),
            pltpu.VMEM((LK, 1280), F32),
            pltpu.VMEM((80, 384), F32),
            pltpu.VMEM((80, 384), F32),
            dma, dma((4, len(PLAN))), dma((4, len(PLAN))), dma, dma, dma, dma, dma, dma, dma,
        ],
        compiler_params=pltpu.CompilerParams(
            collective_id=0, has_side_effects=True, vmem_limit_bytes=67043328
        ),
    )(
        query_single, key_single, pair, query_frames.T, key_frames, w_query.T, w_key.T, w_value.T,
        w_query_points.T, w_key_points.T, w_value_points.T, head_weight, bias_weight, w_out, d_out,
    )
    return pl.pallas_call(
        finish,
        out_shape=(
            jax.ShapeDtypeStruct((1, 384), BF),
            jax.ShapeDtypeStruct((1, 384), F32),
            jax.ShapeDtypeStruct((LK, 384), F32),
        ),
        in_specs=[vmem],
        out_specs=(vmem, vmem, vmem),
    )(total)


def solution(mesh):
    return jax.shard_map(
        shards,
        mesh=mesh,
        in_specs=(
            P("row", None),
            P("row", None),
            P("row", None, None),
            P(None, "row"),
            P(None, "row"),
            P(None, "head"),
            P(None, "head"),
            P(None, "head"),
            P(None, "head"),
            P(None, "head"),
            P(None, "head"),
            P("head"),
            P("head", None),
            P("head", None),
            P("row", None),
        ),
        out_specs=(P("row", None), P("row", None), P("row", None)),
        check_vma=False,
    )
```

```python
import functools
import math

import jax
import jax.numpy as jnp
from jax import lax
from jax.experimental import pallas as pl
from jax.experimental.pallas import tpu as pltpu
from jax.sharding import PartitionSpec as P

NY, NZ, NX = 4, 8, 4
ROWS = NY * NZ * NX
LK = 64
K = ROWS * LK
SIZES = (NY, NZ, NX)
LOGIT_SCALE = math.sqrt(1.0 / 3.0)
POINT_SCALE = math.sqrt(2.0 / 36.0)
MESH = pl.DeviceIdType.MESH
BF, F32 = jnp.bfloat16, jnp.float32

STREAMS = (
    (0, 0, 32, (0, 1, 2)),
    (0, 32, 32, (2, 1, 0)),
    (1, 0, 32, (0, 1, 2)),
    (1, 32, 32, (2, 1, 0)),
)
SLOTS = 7


def gather_plan():
    plan = []

    def add(rnd, name, needs, axis, step, offsets, half=None):
        plan.append((rnd, name, needs, axis, step, offsets, half))

    for sign, mark in ((1, "+"), (-1, "-")):
        add(0, "a" + mark, (), 0, sign, (0, 0, 0))
    add(0, "b", (), 0, 2, (0, 0, 0))
    first = ("a+", "a-", "b")
    for k in range(NZ // 2):
        for sign, mark in ((1, "+"), (-1, "-")):
            needs = first if k == 0 else ("c%d%s" % (k - 1, mark),)
            half = "blocks" if k == NZ // 2 - 1 else None
            add(1 + k, "c%d%s" % (k, mark), needs, 1, sign, (None, -sign * k, 0), half)
    for k in range(NZ // 2 + 1):
        for side in (1, -1) if 0 < k < NZ // 2 else (1,):
            offset = -side * k
            if k == 0:
                needs = first
            elif k == NZ // 2:
                needs = ("c%d+" % (k - 1), "c%d-" % (k - 1))
            else:
                needs = ("c%d%s" % (k - 1, "+" if side == 1 else "-"),)
            for sign, mark in ((1, "+"), (-1, "-")):
                name = "%d%s" % (offset, mark)
                add(1 + k, "d" + name, needs, 2, sign, (None, offset, 0))
                if k < NZ // 2:
                    add(2 + k, "e" + name, ("d" + name,), 2, sign, (None, offset, -sign), "blocks")
            if k == NZ // 2:
                add(1 + k, "e%d" % offset, needs, 2, 2, (None, offset, 0))
    return sorted(plan, key=lambda item: (item[0], item[1]))


PLAN = gather_plan()
NUMBER = {item[1]: n for n, item in enumerate(PLAN)}


def nt(a, b):
    return lax.dot_general(a, b, (((1,), (1,)), ((), ())), preferred_element_type=F32)


def nn(a, b):
    return lax.dot_general(a, b, (((1,), (0,)), ((), ())), preferred_element_type=F32)


def tn(a, b, precision=None):
    return lax.dot_general(
        a, b, (((0,), (0,)), ((), ())), preferred_element_type=F32, precision=precision
    )


def iotas(shape):
    return (
        lax.broadcasted_iota(jnp.int32, shape, 0),
        lax.broadcasted_iota(jnp.int32, shape, 1),
    )


def third(value):
    return lax.shift_right_logical(value * 43, 7)


def within(lane, start, count):
    return (lane >= start) & (lane < start + count)


SHIFTS = (0, 1, 2, -1, -2)


def selection():
    j, l = iotas((12, 128))
    x = l - 3 * third(l)
    parts = []
    for d in SHIFTS:
        ok = (x + d >= 0) & (x + d < 3)
        parts.append(ok & (j == 4 * x + d))
    parts.append(j == 9 + x)
    for d in SHIFTS[1:]:
        ok = (x + d >= 0) & (x + d < 3)
        parts.append(ok & (j == 4 * x + 3 * d))
    return jnp.concatenate([jnp.where(p, 1.0, 0.0) for p in parts], axis=1)


def part(pat, i):
    return pat[:, 128 * i : 128 * i + 128]


def shifted(v, d):
    return v if d == 0 else pltpu.roll(v, (-d) % 128, 1)


def rotated(v, pat):
    return sum(part(pat, i) * shifted(v, d) for i, d in enumerate(SHIFTS))


def unrotated(v, pat):
    out = part(pat, 0) * v
    for i, d in enumerate(SHIFTS[1:]):
        out = out + part(pat, 6 + i) * shifted(v, d)
    return out


def fold(x, combine):
    parts = [x[:, 128 * n : 128 * n + 128] for n in range(x.shape[1] // 128)]
    while len(parts) > 1:
        parts = [combine(*parts[n : n + 2]) for n in range(0, len(parts), 2)]
    return parts[0]


def softplus(x):
    return jnp.maximum(x, 0.0) + jnp.log1p(jnp.exp(-jnp.abs(x)))


def by_head(index, values):
    return jnp.where(index == 0, values[0], jnp.where(index == 1, values[1], values[2]))


def mask_k(r, l):
    return within(l, 16 * r, 16) & (r < 3), within(l, 48 + 12 * r, 12) & (r < 3)


def mask_v(r, l):
    return (within(l, 16 * r, 16) | within(l, 48 + 24 * r, 24)) & (r < 3)


def kernel(
    qs_h, ks_h, pair, qfr_h, kfr_h, w_q_h, w_k_h, w_v_h, w_qp_h, w_kp_h, w_vp_h, hw_h, bw_h,
    w_o_h, d_o_h,
    o_sum,
    qs, ks, qfr, kfr, w_q, w_k, w_v, w_qp, w_kp, w_vp, hw, bw, w_o, d_o, in_sem,
    buf_k, buf_v, pair_s, wq_s, wk_s, wv_s, wp_s, lhs_s, pb_s, att_s, da_s, msg_a, msg_s, recv_a, recv_s, unpack_a, unpack_s,
    pat_s, part_s, got_s,
    pair_sem, send_sem, recv_sem, a_send, a_recv, s_send, s_recv, own_sem, ex_send, ex_recv,
):
    row = lax.axis_index("row")
    core = lax.axis_index("head")
    loads = [
        pltpu.make_async_copy(src, dst, in_sem.at[n])
        for n, (src, dst) in enumerate(
            (
                (ks_h, ks), (kfr_h, kfr), (w_k_h, w_k), (w_kp_h, w_kp), (w_v_h, w_v), (w_vp_h, w_vp),
                (qs_h, qs), (qfr_h, qfr), (w_q_h, w_q), (w_qp_h, w_qp), (hw_h, hw), (bw_h, bw),
                (w_o_h, w_o), (d_o_h, d_o),
            )
        )
    ]
    for load in loads:
        load.start()
    coords = (row // (NZ * NX), (row // NX) % NZ, row % NX)

    def neighbour(axis, step):
        moved = list(coords)
        moved[axis] = (coords[axis] + step + SIZES[axis]) % SIZES[axis]
        return (moved[0] * NZ + moved[1]) * NX + moved[2]

    barrier = pltpu.get_barrier_semaphore()
    for axis, steps in ((0, (1, -1, 2)), (1, (1, -1)), (2, (1, -1, 2))):
        for step in steps:
            pl.semaphore_signal(
                barrier, inc=1, device_id=(neighbour(axis, step), core), device_id_type=MESH
            )
    pl.semaphore_signal(barrier, inc=1, device_id=(row, 1 - core), device_id_type=MESH)
    pair_copy = pltpu.make_async_copy(pair.at[0], pair_s, pair_sem)
    pair_copy.start()

    select = selection()
    for load in loads[:6]:
        load.wait()
    wk_s[...] = jnp.zeros_like(wk_s)
    wk_s[0:48, :] = w_k[...]
    wk_s[48:84, :] = w_kp[...]
    wv_s[...] = jnp.zeros_like(wv_s)
    wv_s[0:48, :] = w_v[...]
    wv_s[48:120, :] = w_vp[...]
    pat = tn(kfr[...], select, lax.Precision.HIGHEST)
    pat_s[...] = pat
    r64, l64 = iotas((LK, 128))
    feat = nt(ks[...], wk_s[...])
    k_rows = jnp.where(
        l64 < 48, feat, jnp.where(l64 < 84, rotated(feat, pat) + part(pat, 5), 0.0)
    ).astype(BF)
    k_full = k_rows.astype(F32)
    square = k_full * k_full
    for h in range(3):
        total = jnp.sum(
            jnp.where(within(l64, 48 + 12 * h, 12), square, 0.0), axis=1, keepdims=True
        )
        high = total.astype(BF).astype(F32)
        middle = (total - high).astype(BF).astype(F32)
        low = total - high - middle
        at = 84 + 3 * h
        k_full = jnp.where(
            l64 == at, high, jnp.where(l64 == at + 1, middle, jnp.where(l64 == at + 2, low, k_full))
        )
    feat = nt(ks[...], wv_s[...])
    v_rows = jnp.where(
        l64 < 48, feat, jnp.where(l64 < 120, rotated(feat, pat) + part(pat, 5), 0.0)
    ).astype(BF)
    mine = (pl.ds(coords[0], 1), pl.ds(coords[1], 1), pl.ds(coords[2], 1))
    buf_k[mine] = k_full.astype(BF).reshape(1, 1, 1, LK, 128)
    buf_v[mine] = v_rows.reshape(1, 1, 1, LK, 128)

    bufs = (buf_k, buf_v)

    seen = [set() for _ in STREAMS]

    def gather_copy(s, item):
        which, start, count, order = STREAMS[s]
        _, name, _, axis, step, offsets, half = item
        at = [None] * 3
        for a, offset in zip(order, offsets):
            if offset is None:
                at[a] = pl.ds(0, SIZES[a])
            elif offset == 0:
                at[a] = pl.ds(coords[a], 1)
            else:
                at[a] = pl.ds((coords[a] + offset + SIZES[a]) % SIZES[a], 1)
        second = 0 if step == 1 else 1
        if half == "blocks":
            a = order[0]
            at[a] = pl.ds(second * (SIZES[a] // 2), SIZES[a] // 2)
        where = bufs[which].at[at[0], at[1], at[2], pl.ds(start, count)]
        n = NUMBER[name]
        return pltpu.make_async_remote_copy(
            src_ref=where,
            dst_ref=where,
            send_sem=send_sem.at[s, n],
            recv_sem=recv_sem.at[s, n],
            device_id=(neighbour(order[axis], step), core),
            device_id_type=MESH,
        )

    def arrive(s, name):
        if name not in seen[s]:
            seen[s].add(name)
            gather_copy(s, PLAN[NUMBER[name]]).wait_recv()

    def gather_round(s, rnd, last):
        for item in PLAN:
            if item[0] == rnd and (item[1][0] == "e") == last:
                for name in item[2]:
                    arrive(s, name)
                gather_copy(s, item).start()
        if rnd == SLOTS - 1 and last:
            for item in PLAN:
                arrive(s, item[1])

    def gather_slot(slot):
        for last in (False, True):
            for s in range(4):
                gather_round(s, slot, last)

    pl.semaphore_wait(barrier, 9)
    gather_slot(0)

    for load in loads[6:]:
        load.wait()
    wq_s[...] = jnp.zeros_like(wq_s)
    wq_s[0:48, :] = w_q[...]
    wq_s[48:84, :] = w_qp[...]
    pat_q = lax.dot_general(
        qfr[...], select, (((1,), (0,)), ((), ())),
        preferred_element_type=F32, precision=lax.Precision.HIGHEST,
    )
    _, l1 = iotas((1, 128))
    x1 = l1 - 3 * third(l1)
    feat = nt(qs[...], wq_s[...])
    q_row = jnp.where(
        l1 < 48, feat, jnp.where(l1 < 84, rotated(feat, pat_q) + part(pat_q, 5), 0.0)
    )
    q_row = q_row.astype(BF).astype(F32)
    r8, l8 = iotas((8, 128))
    raw = [hw[0], hw[1], hw[2]]
    gain = (softplus(by_head(r8, raw)) * POINT_SCALE)[:, 0:1]
    keys8, points8 = mask_k(r8, l8)
    values8 = mask_v(r8, l8)
    q8 = jnp.broadcast_to(q_row, (8, 128))
    q_square = jnp.sum(jnp.where(points8, q8 * q8, 0.0), axis=1, keepdims=True)
    lhs_q = jnp.concatenate(
        [
            jnp.where(keys8, q8, 0.0),
            jnp.where(points8, q8, jnp.where(within(l8, 84 + 3 * r8, 3) & (r8 < 3), -0.5, 0.0)),
        ],
        axis=0,
    ).astype(BF)

    i256, _ = iotas((256, 1))
    i = i256 & 127
    j = i - 48
    head = lax.shift_right_logical(j * 43, 10)
    point = third(j)
    p_head = lax.shift_right_logical(point, 3)
    source = jnp.where(
        i256 < 128,
        jnp.where(i < 48, 176 * lax.shift_right_logical(i, 4) + (i & 15), 152 * head + 16 + j),
        176 * p_head + 40 + (point & 7),
    )
    valid = (i < 120) & ((i256 < 128) | (i >= 48))
    source = jnp.where(valid, source, -1)
    _, lane_o = iotas((256, 528))
    pick = jnp.where(lane_o == source, 1.0, 0.0).astype(BF)
    wp_s[...] = nn(pick, w_o[...]).astype(BF)
    d_feat = nt(d_o[...], wp_s[...])
    lhs_s[...] = jnp.zeros_like(lhs_s)
    lhs_s[0:3, :] = bw[...].astype(F32)
    for h in range(3):
        lhs_s[8 + h : 9 + h, :] = nt(d_o[...], w_o[176 * h + 48 : 176 * h + 176, :])
    lhs_p = lhs_s[...].astype(BF)
    pair_copy.wait()

    def pair_step(g, _):
        at = pl.multiple_of(g * 1024, 1024)
        pb_s[:, pl.ds(at, 1024)] = nt(lhs_p, pair_s[pl.ds(at, 1024), :])
        return 0

    for slot in range(1, SLOTS - 1):
        lax.fori_loop((slot - 1) * 8 // (SLOTS - 2), slot * 8 // (SLOTS - 2), pair_step, 0)
        gather_slot(slot)
    gather_slot(SLOTS - 1)

    def chunk(ref, g):
        return ref[pl.ds(g // 2, 1), pl.ds((g % 2) * 4, 4)].reshape(1024, 128)

    def logit_step(g, top):
        at = pl.multiple_of(g * 1024, 1024)
        both = nt(lhs_q, chunk(buf_k, g))
        logits = LOGIT_SCALE * (
            both[0:8] * 0.25
            + pb_s[0:8, pl.ds(at, 1024)]
            + gain * (both[8:16] - 0.5 * q_square)
        )
        att_s[:, pl.ds(at, 1024)] = logits
        return jnp.maximum(top, fold(logits, jnp.maximum))

    top = lax.fori_loop(0, 8, logit_step, jnp.full((8, 128), -3.0e38, F32), unroll=8)
    top = jnp.max(top, axis=1, keepdims=True)

    def exp_step(g, total):
        at = pl.multiple_of(g * 1024, 1024)
        e = jnp.exp(att_s[:, pl.ds(at, 1024)] - top)
        att_s[:, pl.ds(at, 1024)] = e
        return total + fold(e, jnp.add)

    zero8 = jnp.zeros((8, 128), F32)
    total = lax.fori_loop(0, 8, exp_step, zero8, unroll=8)
    inverse = 1.0 / jnp.sum(total, axis=1, keepdims=True)

    rotate = row // 16
    rc, _ = iotas((8, 1024))

    def start_sends(message, landing, send, recv, g):
        for n in range(16):
            target = g * 16 + (row + n) % 16

            def start(target=target):
                at = pl.multiple_of((target // 2) * 128, 128)
                pltpu.make_async_remote_copy(
                    src_ref=message.at[:, pl.ds(at, 128)],
                    dst_ref=landing.at[row],
                    send_sem=send,
                    recv_sem=recv,
                    device_id=(target, core),
                    device_id_type=MESH,
                ).start()

            if n:
                start()
            else:
                pl.when(target != row)(start)

    def own_copy(message, landing):
        at = pl.multiple_of((row // 2) * 128, 128)
        return pltpu.make_async_copy(message.at[:, pl.ds(at, 128)], landing.at[row], own_sem)

    def all_of(landing, sem):
        everyone = landing.at[pl.ds(0, ROWS - 1)]
        return pltpu.make_async_copy(everyone, everyone, sem)

    def attend_step(i, carry):
        acc_v, acc_p = carry
        g = (i + rotate) % 8

        @pl.when(i > 0)
        def _():
            start_sends(msg_a, recv_a, a_send, a_recv, (i - 1 + rotate) % 8)

        at = pl.multiple_of(g * 1024, 1024)
        a = att_s[:, pl.ds(at, 1024)] * inverse
        att_s[:, pl.ds(at, 1024)] = a
        msg_a[:, pl.ds(at, 1024)] = jnp.where(rc < 3, a, side_k)[0:4].astype(BF)
        a = a.astype(BF)
        return (
            acc_v + nn(a, chunk(buf_v, g)),
            acc_p + nn(a, pair_s[pl.ds(at, 1024), :]),
        )

    side_k = jnp.concatenate([q8] * 8, axis=1)
    acc_v, acc_p = lax.fori_loop(0, 8, attend_step, (zero8, zero8), unroll=4)
    start_sends(msg_a, recv_a, a_send, a_recv, (7 + rotate) % 8)
    own_a = own_copy(msg_a, recv_a)
    own_a.start()
    row_v = jnp.sum(jnp.where(values8, acc_v, 0.0), axis=0, keepdims=True)
    is_point = within(l1, 48, 72)
    local = jnp.where(is_point, unrotated(jnp.where(is_point, row_v - part(pat_q, 5), 0.0), pat_q), 0.0)
    squares = local * local
    norm = squares
    for d in SHIFTS[1:]:
        norm = norm + jnp.where((x1 + d >= 0) & (x1 + d < 3), shifted(squares, d), 0.0)
    lengths = jnp.sqrt(1.0 + norm)
    f_v = jnp.where(l1 < 48, row_v, local).astype(BF)
    f_len = jnp.where(is_point & (x1 == 0), lengths, 0.0).astype(BF)
    out_row = nn(f_v, wp_s[0:128, :]) + nn(f_len, wp_s[128:256, :])
    for h in range(3):
        out_row = out_row + nn(
            acc_p[h : h + 1, :].astype(BF), w_o[176 * h + 48 : 176 * h + 176, :]
        )
    part_s[64:65, :] = out_row

    d_local = d_feat[:, 0:128] + d_feat[:, 128:256] / lengths * local
    d_local = jnp.where(is_point, d_local, 0.0)
    side_v = jnp.where(
        l1 < 48, d_feat[:, 0:128], jnp.where(is_point, rotated(d_local, pat_q), 0.0)
    )
    side_v8 = jnp.broadcast_to(side_v, (8, 128))
    lhs_v = jnp.where(values8, side_v8, 0.0).astype(BF)

    def grad_step(g, carry):
        at = pl.multiple_of(g * 1024, 1024)
        d_att = nt(lhs_v, chunk(buf_v, g)) + pb_s[8:16, pl.ds(at, 1024)]
        da_s[:, pl.ds(at, 1024)] = d_att
        return carry + fold(att_s[:, pl.ds(at, 1024)] * d_att, jnp.add)

    row_total = lax.fori_loop(0, 8, grad_step, zero8, unroll=8)
    row_total = jnp.sum(row_total, axis=1, keepdims=True)
    side_v = jnp.concatenate([side_v8] * 8, axis=1)

    def score_step(i, carry):
        acc, sums = carry
        g = (i + rotate) % 8

        @pl.when(i > 0)
        def _():
            start_sends(msg_s, recv_s, s_send, s_recv, (i - 1 + rotate) % 8)

        at = pl.multiple_of(g * 1024, 1024)
        a = att_s[:, pl.ds(at, 1024)]
        score = LOGIT_SCALE * a * (da_s[:, pl.ds(at, 1024)] - row_total)
        msg_s[:, pl.ds(at, 1024)] = jnp.where(rc < 3, score, side_v)[0:4].astype(BF)
        score = score.astype(BF)
        acc = acc + nn(score, chunk(buf_k, g))
        return acc, sums + fold(score.astype(F32), jnp.add)

    acc_k, score_rows = lax.fori_loop(0, 8, score_step, (zero8, zero8), unroll=4)
    score_rows = jnp.sum(score_rows, axis=1, keepdims=True)
    start_sends(msg_s, recv_s, s_send, s_recv, (7 + rotate) % 8)
    own_a.wait()
    own_s = own_copy(msg_s, recv_s)
    own_s.start()

    q_terms = jnp.where(keys8, acc_k * 0.25, 0.0) + jnp.where(
        points8, gain * (acc_k - score_rows * q8), 0.0
    )
    d_q = jnp.sum(q_terms, axis=0, keepdims=True)
    d_q = jnp.where(l1 < 48, d_q, jnp.where(l1 < 84, unrotated(d_q, pat_q), 0.0)).astype(BF)
    part_s[72:73, :] = nn(d_q, wq_s[...])

    _, l128 = iotas((ROWS, 128))

    def unpack(landing, unpacked):
        def step(i, _):
            at = pl.multiple_of(i * 32, 32)
            unpacked[pl.ds(at, 32), :] = landing[pl.ds(i * 8, 8)].astype(F32).reshape(32, 128)
            return 0

        lax.fori_loop(0, ROWS // 8, step, 0)
        return [unpacked[pl.ds(n, ROWS, stride=4), :] for n in range(4)]

    odd = row % 2 == 1

    def mine_of(x):
        return jnp.where(odd, x[64:128], x[0:64])

    for s in range(4):
        for item in PLAN:
            gather_copy(s, item).wait_send()
    all_of(recv_a, a_recv).wait()
    *att_h, side_k = unpack(recv_a, unpack_a)
    keys_h = [within(l128, 16 * h, 16) for h in range(3)]
    points_h = [within(l128, 48 + 12 * h, 12) for h in range(3)]
    rights_k = [jnp.where(keys_h[h] | points_h[h], side_k, 0.0).astype(BF) for h in range(3)]
    rights_n = [jnp.where(points_h[h], 1.0, 0.0).astype(BF) for h in range(3)]
    pat = pat_s[...]
    kf = buf_k[mine].reshape(LK, 128).astype(F32)
    gain_l = softplus(by_head(jnp.where(l1 < 60, 0, jnp.where(l1 < 72, 1, 2)), raw)) * POINT_SCALE

    all_of(recv_s, s_recv).wait()
    own_s.wait()
    *score_h, side_v = unpack(recv_s, unpack_s)
    out_k = out_v = sums = jnp.zeros((128, 128), F32)
    for h in range(3):
        score = score_h[h].astype(BF)
        vpoints_h = within(l128, 48 + 24 * h, 24)
        out_v = out_v + tn(
            att_h[h].astype(BF), jnp.where(keys_h[h] | vpoints_h, side_v, 0.0).astype(BF)
        )
        out_k = out_k + tn(score, rights_k[h])
        sums = sums + tn(score, rights_n[h])
    out_k, out_v, sums = mine_of(out_k), mine_of(out_v), mine_of(sums)
    d_points = jnp.where(within(l64, 48, 36), gain_l * (out_k - sums * kf), 0.0)
    d_k = jnp.where(l64 < 48, out_k * 0.25, jnp.where(l64 < 84, unrotated(d_points, pat), 0.0))
    d_v = jnp.where(l64 < 48, out_v, jnp.where(l64 < 120, unrotated(out_v, pat), 0.0))
    part_s[0:64, :] = nn(d_k.astype(BF), wk_s[...]) + nn(d_v.astype(BF), wv_s[...])

    exchange = pltpu.make_async_remote_copy(
        src_ref=part_s,
        dst_ref=got_s,
        send_sem=ex_send,
        recv_sem=ex_recv,
        device_id=(row, 1 - core),
        device_id_type=MESH,
    )
    exchange.start()
    all_of(recv_a, a_send).wait()
    all_of(recv_s, s_send).wait()
    exchange.wait()
    o_sum[...] = part_s[...] + got_s[...]


def finish(total, o_out, o_gq, o_gk):
    o_gk[...] = total[0:64, :]
    o_out[...] = total[64:65, :].astype(BF)
    o_gq[...] = total[72:73, :]


def shards(
    query_single, key_single, pair, query_frames, key_frames, w_query, w_key, w_value,
    w_query_points, w_key_points, w_value_points, head_weight, bias_weight, w_out, d_out,
):
    vmem = pl.BlockSpec(memory_space=pltpu.VMEM)
    specs = [pl.BlockSpec(memory_space=pltpu.HBM)] * 15
    dma = pltpu.SemaphoreType.DMA
    total = pl.pallas_call(
        kernel,
        out_shape=pltpu.VMEM((80, 384), F32),
        in_specs=specs,
        out_specs=vmem,
        scratch_shapes=[
            pltpu.VMEM((1, 384), BF),
            pltpu.VMEM((LK, 384), BF),
            pltpu.VMEM((1, 12), F32),
            pltpu.VMEM((12, LK), F32),
            pltpu.VMEM((48, 384), BF),
            pltpu.VMEM((48, 384), BF),
            pltpu.VMEM((48, 384), BF),
            pltpu.VMEM((36, 384), BF),
            pltpu.VMEM((36, 384), BF),
            pltpu.VMEM((72, 384), BF),
            pltpu.SMEM((3,), F32),
            pltpu.VMEM((3, 128), BF),
            pltpu.VMEM((528, 384), BF),
            pltpu.VMEM((1, 384), BF),
            pltpu.SemaphoreType.DMA((14,)),
            pltpu.VMEM((NY, NZ, NX, LK, 128), BF),
            pltpu.VMEM((NY, NZ, NX, LK, 128), BF),
            pltpu.VMEM((K, 128), BF),
            pltpu.VMEM((128, 384), BF),
            pltpu.VMEM((128, 384), BF),
            pltpu.VMEM((128, 384), BF),
            pltpu.VMEM((256, 384), BF),
            pltpu.VMEM((16, 128), F32),
            pltpu.VMEM((16, K), F32),
            pltpu.VMEM((8, K), F32),
            pltpu.VMEM((8, K), F32),
            pltpu.VMEM((4, K), BF),
            pltpu.VMEM((4, K), BF),
            pltpu.VMEM((ROWS, 4, 128), BF),
            pltpu.VMEM((ROWS, 4, 128), BF),
            pltpu.VMEM((ROWS * 4, 128), F32),
            pltpu.VMEM((ROWS * 4, 128), F32),
            pltpu.VMEM((LK, 1280), F32),
            pltpu.VMEM((80, 384), F32),
            pltpu.VMEM((80, 384), F32),
            dma, dma((4, len(PLAN))), dma((4, len(PLAN))), dma, dma, dma, dma, dma, dma, dma,
        ],
        compiler_params=pltpu.CompilerParams(
            collective_id=0, has_side_effects=True, vmem_limit_bytes=66900000
        ),
    )(
        query_single, key_single, pair, query_frames.T, key_frames, w_query.T, w_key.T, w_value.T,
        w_query_points.T, w_key_points.T, w_value_points.T, head_weight, bias_weight, w_out, d_out,
    )
    return pl.pallas_call(
        finish,
        out_shape=(
            jax.ShapeDtypeStruct((1, 384), BF),
            jax.ShapeDtypeStruct((1, 384), F32),
            jax.ShapeDtypeStruct((LK, 384), F32),
        ),
        in_specs=[vmem],
        out_specs=(vmem, vmem, vmem),
        compiler_params=pltpu.CompilerParams(vmem_limit_bytes=16 * 1024 * 1024),
    )(total)


def solution(mesh):
    return jax.shard_map(
        shards,
        mesh=mesh,
        in_specs=(
            P("row", None),
            P("row", None),
            P("row", None, None),
            P(None, "row"),
            P(None, "row"),
            P(None, "head"),
            P(None, "head"),
            P(None, "head"),
            P(None, "head"),
            P(None, "head"),
            P(None, "head"),
            P("head"),
            P("head", None),
            P("head", None),
            P("row", None),
        ),
        out_specs=(P("row", None), P("row", None), P("row", None)),
        check_vma=False,
    )
```

```python
import functools
import math

import jax
import jax.numpy as jnp
from jax import lax
from jax.experimental import pallas as pl
from jax.experimental.pallas import tpu as pltpu
from jax.sharding import PartitionSpec as P

NY, NZ, NX = 4, 8, 4
ROWS = NY * NZ * NX
LK = 64
K = ROWS * LK
SIZES = (NY, NZ, NX)
LOGIT_SCALE = math.sqrt(1.0 / 3.0)
POINT_SCALE = math.sqrt(2.0 / 36.0)
MESH = pl.DeviceIdType.MESH
BF, F32 = jnp.bfloat16, jnp.float32

STREAMS = (
    (0, 0, 32, (0, 1, 2)),
    (0, 32, 32, (2, 1, 0)),
    (1, 0, 32, (0, 1, 2)),
    (1, 32, 32, (2, 1, 0)),
)
SLOTS = 7


def gather_plan():
    plan = []

    def add(rnd, name, needs, axis, step, offsets, half=None):
        plan.append((rnd, name, needs, axis, step, offsets, half))

    for sign, mark in ((1, "+"), (-1, "-")):
        add(0, "a" + mark, (), 0, sign, (0, 0, 0))
    add(0, "b", (), 0, 2, (0, 0, 0))
    first = ("a+", "a-", "b")
    for k in range(NZ // 2):
        for sign, mark in ((1, "+"), (-1, "-")):
            needs = first if k == 0 else ("c%d%s" % (k - 1, mark),)
            half = "blocks" if k == NZ // 2 - 1 else None
            add(1 + k, "c%d%s" % (k, mark), needs, 1, sign, (None, -sign * k, 0), half)
    for k in range(NZ // 2 + 1):
        for side in (1, -1) if 0 < k < NZ // 2 else (1,):
            offset = -side * k
            if k == 0:
                needs = first
            elif k == NZ // 2:
                needs = ("c%d+" % (k - 1), "c%d-" % (k - 1))
            else:
                needs = ("c%d%s" % (k - 1, "+" if side == 1 else "-"),)
            for sign, mark in ((1, "+"), (-1, "-")):
                name = "%d%s" % (offset, mark)
                add(1 + k, "d" + name, needs, 2, sign, (None, offset, 0))
                if k < NZ // 2:
                    add(2 + k, "e" + name, ("d" + name,), 2, sign, (None, offset, -sign), "blocks")
            if k == NZ // 2:
                add(1 + k, "e%d" % offset, needs, 2, 2, (None, offset, 0))
    return sorted(plan, key=lambda item: (item[0], item[1]))


PLAN = gather_plan()
NUMBER = {item[1]: n for n, item in enumerate(PLAN)}


def nt(a, b):
    return lax.dot_general(a, b, (((1,), (1,)), ((), ())), preferred_element_type=F32)


def nn(a, b):
    return lax.dot_general(a, b, (((1,), (0,)), ((), ())), preferred_element_type=F32)


def tn(a, b, precision=None):
    return lax.dot_general(
        a, b, (((0,), (0,)), ((), ())), preferred_element_type=F32, precision=precision
    )


def iotas(shape):
    return (
        lax.broadcasted_iota(jnp.int32, shape, 0),
        lax.broadcasted_iota(jnp.int32, shape, 1),
    )


def third(value):
    return lax.shift_right_logical(value * 43, 7)


def within(lane, start, count):
    return (lane >= start) & (lane < start + count)


SHIFTS = (0, 1, 2, -1, -2)


def selection():
    j, l = iotas((12, 128))
    x = l - 3 * third(l)
    parts = []
    for d in SHIFTS:
        ok = (x + d >= 0) & (x + d < 3)
        parts.append(ok & (j == 4 * x + d))
    parts.append(j == 9 + x)
    for d in SHIFTS[1:]:
        ok = (x + d >= 0) & (x + d < 3)
        parts.append(ok & (j == 4 * x + 3 * d))
    return jnp.concatenate([jnp.where(p, 1.0, 0.0) for p in parts], axis=1)


def part(pat, i):
    return pat[:, 128 * i : 128 * i + 128]


def shifted(v, d):
    return v if d == 0 else pltpu.roll(v, (-d) % 128, 1)


def rotated(v, pat):
    return sum(part(pat, i) * shifted(v, d) for i, d in enumerate(SHIFTS))


def unrotated(v, pat):
    out = part(pat, 0) * v
    for i, d in enumerate(SHIFTS[1:]):
        out = out + part(pat, 6 + i) * shifted(v, d)
    return out


def fold(x, combine):
    parts = [x[:, 128 * n : 128 * n + 128] for n in range(x.shape[1] // 128)]
    while len(parts) > 1:
        parts = [combine(*parts[n : n + 2]) for n in range(0, len(parts), 2)]
    return parts[0]


def softplus(x):
    return jnp.maximum(x, 0.0) + jnp.log1p(jnp.exp(-jnp.abs(x)))


def by_head(index, values):
    return jnp.where(index == 0, values[0], jnp.where(index == 1, values[1], values[2]))


def mask_k(r, l):
    return within(l, 16 * r, 16) & (r < 3), within(l, 48 + 12 * r, 12) & (r < 3)


def mask_v(r, l):
    return (within(l, 16 * r, 16) | within(l, 48 + 24 * r, 24)) & (r < 3)


def kernel(
    qs_h, ks_h, pair, qfr_h, kfr_h, w_q_h, w_k_h, w_v_h, w_qp_h, w_kp_h, w_vp_h, hw_h, bw_h,
    w_o_h, d_o_h,
    o_sum,
    qs, ks, qfr, kfr, w_q, w_k, w_v, w_qp, w_kp, w_vp, hw, bw, w_o, d_o, in_sem,
    buf_k, buf_v, pair_s, wq_s, wk_s, wv_s, wp_s, lhs_s, pb_s, att_s, da_s, msg_a, msg_s, recv_a, recv_s, unpack_a, unpack_s,
    pat_s, part_s, got_s,
    pair_sem, send_sem, recv_sem, a_send, a_recv, s_send, s_recv, own_sem, ex_send, ex_recv,
):
    row = lax.axis_index("row")
    core = lax.axis_index("head")
    loads = [
        pltpu.make_async_copy(src, dst, in_sem.at[n])
        for n, (src, dst) in enumerate(
            (
                (ks_h, ks), (kfr_h, kfr), (w_k_h, w_k), (w_kp_h, w_kp), (w_v_h, w_v), (w_vp_h, w_vp),
                (qs_h, qs), (qfr_h, qfr), (w_q_h, w_q), (w_qp_h, w_qp), (hw_h, hw), (bw_h, bw),
                (w_o_h, w_o), (d_o_h, d_o),
            )
        )
    ]
    for load in loads:
        load.start()
    coords = (row // (NZ * NX), (row // NX) % NZ, row % NX)

    def neighbour(axis, step):
        moved = list(coords)
        moved[axis] = (coords[axis] + step + SIZES[axis]) % SIZES[axis]
        return (moved[0] * NZ + moved[1]) * NX + moved[2]

    barrier = pltpu.get_barrier_semaphore()
    for axis, steps in ((0, (1, -1, 2)), (1, (1, -1)), (2, (1, -1, 2))):
        for step in steps:
            pl.semaphore_signal(
                barrier, inc=1, device_id=(neighbour(axis, step), core), device_id_type=MESH
            )
    pl.semaphore_signal(barrier, inc=1, device_id=(row, 1 - core), device_id_type=MESH)
    pair_copy = pltpu.make_async_copy(pair.at[0], pair_s, pair_sem)
    pair_copy.start()

    select = selection()
    for load in loads[:4]:
        load.wait()
    wk_s[...] = jnp.zeros_like(wk_s)
    wk_s[0:48, :] = w_k[...]
    wk_s[48:84, :] = w_kp[...]
    pat = tn(kfr[...], select, lax.Precision.HIGHEST)
    pat_s[...] = pat
    r64, l64 = iotas((LK, 128))
    feat = nt(ks[...], wk_s[...])
    k_rows = jnp.where(
        l64 < 48, feat, jnp.where(l64 < 84, rotated(feat, pat) + part(pat, 5), 0.0)
    ).astype(BF)
    k_full = k_rows.astype(F32)
    square = k_full * k_full
    for h in range(3):
        total = jnp.sum(
            jnp.where(within(l64, 48 + 12 * h, 12), square, 0.0), axis=1, keepdims=True
        )
        high = total.astype(BF).astype(F32)
        middle = (total - high).astype(BF).astype(F32)
        low = total - high - middle
        at = 84 + 3 * h
        k_full = jnp.where(
            l64 == at, high, jnp.where(l64 == at + 1, middle, jnp.where(l64 == at + 2, low, k_full))
        )
    mine = (pl.ds(coords[0], 1), pl.ds(coords[1], 1), pl.ds(coords[2], 1))
    buf_k[mine] = k_full.astype(BF).reshape(1, 1, 1, LK, 128)

    bufs = (buf_k, buf_v)

    seen = [set() for _ in STREAMS]

    def gather_copy(s, item):
        which, start, count, order = STREAMS[s]
        _, name, _, axis, step, offsets, half = item
        at = [None] * 3
        for a, offset in zip(order, offsets):
            if offset is None:
                at[a] = pl.ds(0, SIZES[a])
            elif offset == 0:
                at[a] = pl.ds(coords[a], 1)
            else:
                at[a] = pl.ds((coords[a] + offset + SIZES[a]) % SIZES[a], 1)
        second = 0 if step == 1 else 1
        if half == "blocks":
            a = order[0]
            at[a] = pl.ds(second * (SIZES[a] // 2), SIZES[a] // 2)
        where = bufs[which].at[at[0], at[1], at[2], pl.ds(start, count)]
        n = NUMBER[name]
        return pltpu.make_async_remote_copy(
            src_ref=where,
            dst_ref=where,
            send_sem=send_sem.at[s, n],
            recv_sem=recv_sem.at[s, n],
            device_id=(neighbour(order[axis], step), core),
            device_id_type=MESH,
        )

    def arrive(s, name):
        if name not in seen[s]:
            seen[s].add(name)
            gather_copy(s, PLAN[NUMBER[name]]).wait_recv()

    def gather_round(s, rnd, last):
        for item in PLAN:
            if item[0] == rnd and (item[1][0] == "e") == last:
                for name in item[2]:
                    arrive(s, name)
                gather_copy(s, item).start()
        if rnd == SLOTS - 1 and last:
            for item in PLAN:
                arrive(s, item[1])

    def gather_slot(slot, streams=range(4)):
        for last in (False, True):
            for s in streams:
                gather_round(s, slot, last)

    pl.semaphore_wait(barrier, 9)
    gather_slot(0, (0, 1))
    for load in loads[4:6]:
        load.wait()
    wv_s[...] = jnp.zeros_like(wv_s)
    wv_s[0:48, :] = w_v[...]
    wv_s[48:120, :] = w_vp[...]
    feat = nt(ks[...], wv_s[...])
    v_rows = jnp.where(
        l64 < 48, feat, jnp.where(l64 < 120, rotated(feat, pat) + part(pat, 5), 0.0)
    ).astype(BF)
    buf_v[mine] = v_rows.reshape(1, 1, 1, LK, 128)
    gather_slot(0, (2, 3))

    for load in loads[6:]:
        load.wait()
    wq_s[...] = jnp.zeros_like(wq_s)
    wq_s[0:48, :] = w_q[...]
    wq_s[48:84, :] = w_qp[...]
    pat_q = lax.dot_general(
        qfr[...], select, (((1,), (0,)), ((), ())),
        preferred_element_type=F32, precision=lax.Precision.HIGHEST,
    )
    _, l1 = iotas((1, 128))
    x1 = l1 - 3 * third(l1)
    feat = nt(qs[...], wq_s[...])
    q_row = jnp.where(
        l1 < 48, feat, jnp.where(l1 < 84, rotated(feat, pat_q) + part(pat_q, 5), 0.0)
    )
    q_row = q_row.astype(BF).astype(F32)
    r8, l8 = iotas((8, 128))
    raw = [hw[0], hw[1], hw[2]]
    gain = (softplus(by_head(r8, raw)) * POINT_SCALE)[:, 0:1]
    keys8, points8 = mask_k(r8, l8)
    values8 = mask_v(r8, l8)
    q8 = jnp.broadcast_to(q_row, (8, 128))
    q_square = jnp.sum(jnp.where(points8, q8 * q8, 0.0), axis=1, keepdims=True)
    lhs_q = jnp.concatenate(
        [
            jnp.where(keys8, q8, 0.0),
            jnp.where(points8, q8, jnp.where(within(l8, 84 + 3 * r8, 3) & (r8 < 3), -0.5, 0.0)),
        ],
        axis=0,
    ).astype(BF)

    gather_slot(1)
    i256, _ = iotas((256, 1))
    i = i256 & 127
    j = i - 48
    head = lax.shift_right_logical(j * 43, 10)
    point = third(j)
    p_head = lax.shift_right_logical(point, 3)
    source = jnp.where(
        i256 < 128,
        jnp.where(i < 48, 176 * lax.shift_right_logical(i, 4) + (i & 15), 152 * head + 16 + j),
        176 * p_head + 40 + (point & 7),
    )
    valid = (i < 120) & ((i256 < 128) | (i >= 48))
    source = jnp.where(valid, source, -1)
    _, lane_o = iotas((256, 528))
    pick = jnp.where(lane_o == source, 1.0, 0.0).astype(BF)
    wp_s[...] = nn(pick, w_o[...]).astype(BF)
    d_feat = nt(d_o[...], wp_s[...])
    lhs_s[...] = jnp.zeros_like(lhs_s)
    lhs_s[0:3, :] = bw[...].astype(F32)
    for h in range(3):
        lhs_s[8 + h : 9 + h, :] = nt(d_o[...], w_o[176 * h + 48 : 176 * h + 176, :])
    lhs_p = lhs_s[...].astype(BF)
    pair_copy.wait()

    def pair_step(g, _):
        at = pl.multiple_of(g * 1024, 1024)
        pb_s[:, pl.ds(at, 1024)] = nt(lhs_p, pair_s[pl.ds(at, 1024), :])
        return 0

    for slot in range(2, SLOTS - 1):
        lax.fori_loop((slot - 2) * 2, (slot - 1) * 2, pair_step, 0)
        gather_slot(slot)
    gather_slot(SLOTS - 1, (0, 1))

    def chunk(ref, g):
        return ref[pl.ds(g // 2, 1), pl.ds((g % 2) * 4, 4)].reshape(1024, 128)

    def logit_step(g, top):
        at = pl.multiple_of(g * 1024, 1024)
        both = nt(lhs_q, chunk(buf_k, g))
        logits = LOGIT_SCALE * (
            both[0:8] * 0.25
            + pb_s[0:8, pl.ds(at, 1024)]
            + gain * (both[8:16] - 0.5 * q_square)
        )
        att_s[:, pl.ds(at, 1024)] = logits
        return jnp.maximum(top, fold(logits, jnp.maximum))

    top = lax.fori_loop(0, 8, logit_step, jnp.full((8, 128), -3.0e38, F32), unroll=8)
    top = jnp.max(top, axis=1, keepdims=True)

    def exp_step(g, total):
        at = pl.multiple_of(g * 1024, 1024)
        e = jnp.exp(att_s[:, pl.ds(at, 1024)] - top)
        att_s[:, pl.ds(at, 1024)] = e
        return total + fold(e, jnp.add)

    zero8 = jnp.zeros((8, 128), F32)
    total = lax.fori_loop(0, 8, exp_step, zero8, unroll=8)
    gather_slot(SLOTS - 1, (2, 3))
    inverse = 1.0 / jnp.sum(total, axis=1, keepdims=True)

    rotate = row // 16
    rc, _ = iotas((8, 1024))

    def start_sends(message, landing, send, recv, g):
        for n in range(16):
            target = g * 16 + (row + n) % 16

            def start(target=target):
                at = pl.multiple_of((target // 2) * 128, 128)
                pltpu.make_async_remote_copy(
                    src_ref=message.at[:, pl.ds(at, 128)],
                    dst_ref=landing.at[row],
                    send_sem=send,
                    recv_sem=recv,
                    device_id=(target, core),
                    device_id_type=MESH,
                ).start()

            if n:
                start()
            else:
                pl.when(target != row)(start)

    def own_copy(message, landing):
        at = pl.multiple_of((row // 2) * 128, 128)
        return pltpu.make_async_copy(message.at[:, pl.ds(at, 128)], landing.at[row], own_sem)

    def all_of(landing, sem):
        everyone = landing.at[pl.ds(0, ROWS - 1)]
        return pltpu.make_async_copy(everyone, everyone, sem)

    def attend_step(i, acc_v):
        g = (i + rotate) % 8

        @pl.when(i > 0)
        def _():
            start_sends(msg_a, recv_a, a_send, a_recv, (i - 1 + rotate) % 8)

        at = pl.multiple_of(g * 1024, 1024)
        a = att_s[:, pl.ds(at, 1024)] * inverse
        att_s[:, pl.ds(at, 1024)] = a
        msg_a[:, pl.ds(at, 1024)] = jnp.where(rc < 3, a, side_k)[0:4].astype(BF)
        return acc_v + nn(a.astype(BF), chunk(buf_v, g))

    side_k = jnp.concatenate([q8] * 8, axis=1)
    acc_v = lax.fori_loop(0, 8, attend_step, zero8, unroll=4)
    start_sends(msg_a, recv_a, a_send, a_recv, (7 + rotate) % 8)
    own_a = own_copy(msg_a, recv_a)
    own_a.start()
    row_v = jnp.sum(jnp.where(values8, acc_v, 0.0), axis=0, keepdims=True)
    is_point = within(l1, 48, 72)
    local = jnp.where(is_point, unrotated(jnp.where(is_point, row_v - part(pat_q, 5), 0.0), pat_q), 0.0)
    squares = local * local
    norm = squares
    for d in SHIFTS[1:]:
        norm = norm + jnp.where((x1 + d >= 0) & (x1 + d < 3), shifted(squares, d), 0.0)
    lengths = jnp.sqrt(1.0 + norm)
    d_local = d_feat[:, 0:128] + d_feat[:, 128:256] / lengths * local
    d_local = jnp.where(is_point, d_local, 0.0)
    side_v = jnp.where(
        l1 < 48, d_feat[:, 0:128], jnp.where(is_point, rotated(d_local, pat_q), 0.0)
    )
    side_v8 = jnp.broadcast_to(side_v, (8, 128))
    lhs_v = jnp.where(values8, side_v8, 0.0).astype(BF)

    def grad_step(g, carry):
        at = pl.multiple_of(g * 1024, 1024)
        d_att = nt(lhs_v, chunk(buf_v, g)) + pb_s[8:16, pl.ds(at, 1024)]
        da_s[:, pl.ds(at, 1024)] = d_att
        return carry + fold(att_s[:, pl.ds(at, 1024)] * d_att, jnp.add)

    row_total = lax.fori_loop(0, 8, grad_step, zero8, unroll=8)
    row_total = jnp.sum(row_total, axis=1, keepdims=True)
    side_v = jnp.concatenate([side_v8] * 8, axis=1)

    def score_step(i, sums):
        g = (i + rotate) % 8

        @pl.when(i > 0)
        def _():
            start_sends(msg_s, recv_s, s_send, s_recv, (i - 1 + rotate) % 8)

        at = pl.multiple_of(g * 1024, 1024)
        a = att_s[:, pl.ds(at, 1024)]
        score = LOGIT_SCALE * a * (da_s[:, pl.ds(at, 1024)] - row_total)
        msg_s[:, pl.ds(at, 1024)] = jnp.where(rc < 3, score, side_v)[0:4].astype(BF)
        score = score.astype(BF).astype(F32)
        da_s[:, pl.ds(at, 1024)] = score
        return sums + fold(score, jnp.add)

    score_rows = lax.fori_loop(0, 8, score_step, zero8, unroll=4)
    score_rows = jnp.sum(score_rows, axis=1, keepdims=True)
    start_sends(msg_s, recv_s, s_send, s_recv, (7 + rotate) % 8)
    own_a.wait()
    own_s = own_copy(msg_s, recv_s)
    own_s.start()

    def rest_step(g, carry):
        acc_k, acc_p = carry
        at = pl.multiple_of(g * 1024, 1024)
        return (
            acc_k + nn(da_s[:, pl.ds(at, 1024)].astype(BF), chunk(buf_k, g)),
            acc_p + nn(att_s[:, pl.ds(at, 1024)].astype(BF), pair_s[pl.ds(at, 1024), :]),
        )

    acc_k, acc_p = lax.fori_loop(0, 8, rest_step, (zero8, zero8), unroll=4)
    f_v = jnp.where(l1 < 48, row_v, local).astype(BF)
    f_len = jnp.where(is_point & (x1 == 0), lengths, 0.0).astype(BF)
    out_row = nn(f_v, wp_s[0:128, :]) + nn(f_len, wp_s[128:256, :])
    for h in range(3):
        out_row = out_row + nn(
            acc_p[h : h + 1, :].astype(BF), w_o[176 * h + 48 : 176 * h + 176, :]
        )
    part_s[64:65, :] = out_row

    q_terms = jnp.where(keys8, acc_k * 0.25, 0.0) + jnp.where(
        points8, gain * (acc_k - score_rows * q8), 0.0
    )
    d_q = jnp.sum(q_terms, axis=0, keepdims=True)
    d_q = jnp.where(l1 < 48, d_q, jnp.where(l1 < 84, unrotated(d_q, pat_q), 0.0)).astype(BF)
    part_s[72:73, :] = nn(d_q, wq_s[...])

    _, l128 = iotas((ROWS, 128))

    def unpack(landing, unpacked):
        def step(i, _):
            at = pl.multiple_of(i * 32, 32)
            unpacked[pl.ds(at, 32), :] = landing[pl.ds(i * 8, 8)].astype(F32).reshape(32, 128)
            return 0

        lax.fori_loop(0, ROWS // 8, step, 0, unroll=4)
        return [unpacked[pl.ds(n, ROWS, stride=4), :] for n in range(4)]

    odd = row % 2 == 1

    def mine_of(x):
        return jnp.where(odd, x[64:128], x[0:64])

    for s in range(4):
        for item in PLAN:
            gather_copy(s, item).wait_send()
    all_of(recv_a, a_recv).wait()
    *att_h, side_k = unpack(recv_a, unpack_a)
    keys_h = [within(l128, 16 * h, 16) for h in range(3)]
    points_h = [within(l128, 48 + 12 * h, 12) for h in range(3)]
    rights_k = [jnp.where(keys_h[h] | points_h[h], side_k, 0.0).astype(BF) for h in range(3)]
    rights_n = [jnp.where(points_h[h], 1.0, 0.0).astype(BF) for h in range(3)]
    pat = pat_s[...]
    kf = buf_k[mine].reshape(LK, 128).astype(F32)
    gain_l = softplus(by_head(jnp.where(l1 < 60, 0, jnp.where(l1 < 72, 1, 2)), raw)) * POINT_SCALE

    all_of(recv_s, s_recv).wait()
    own_s.wait()
    *score_h, side_v = unpack(recv_s, unpack_s)
    out_k = out_v = sums = jnp.zeros((128, 128), F32)
    for h in range(3):
        score = score_h[h].astype(BF)
        vpoints_h = within(l128, 48 + 24 * h, 24)
        out_v = out_v + tn(
            att_h[h].astype(BF), jnp.where(keys_h[h] | vpoints_h, side_v, 0.0).astype(BF)
        )
        out_k = out_k + tn(score, rights_k[h])
        sums = sums + tn(score, rights_n[h])
    out_k, out_v, sums = mine_of(out_k), mine_of(out_v), mine_of(sums)
    d_points = jnp.where(within(l64, 48, 36), gain_l * (out_k - sums * kf), 0.0)
    d_k = jnp.where(l64 < 48, out_k * 0.25, jnp.where(l64 < 84, unrotated(d_points, pat), 0.0))
    d_v = jnp.where(l64 < 48, out_v, jnp.where(l64 < 120, unrotated(out_v, pat), 0.0))
    part_s[0:64, :] = nn(d_k.astype(BF), wk_s[...]) + nn(d_v.astype(BF), wv_s[...])

    exchange = pltpu.make_async_remote_copy(
        src_ref=part_s,
        dst_ref=got_s,
        send_sem=ex_send,
        recv_sem=ex_recv,
        device_id=(row, 1 - core),
        device_id_type=MESH,
    )
    exchange.start()
    all_of(recv_a, a_send).wait()
    all_of(recv_s, s_send).wait()
    exchange.wait()
    o_sum[...] = part_s[...] + got_s[...]


def finish(total, o_out, o_gq, o_gk):
    o_gk[...] = total[0:64, :]
    o_out[...] = total[64:65, :].astype(BF)
    o_gq[...] = total[72:73, :]


def shards(
    query_single, key_single, pair, query_frames, key_frames, w_query, w_key, w_value,
    w_query_points, w_key_points, w_value_points, head_weight, bias_weight, w_out, d_out,
):
    vmem = pl.BlockSpec(memory_space=pltpu.VMEM)
    specs = [pl.BlockSpec(memory_space=pltpu.HBM)] * 15
    dma = pltpu.SemaphoreType.DMA
    total = pl.pallas_call(
        kernel,
        out_shape=pltpu.VMEM((80, 384), F32),
        in_specs=specs,
        out_specs=vmem,
        scratch_shapes=[
            pltpu.VMEM((1, 384), BF),
            pltpu.VMEM((LK, 384), BF),
            pltpu.VMEM((1, 12), F32),
            pltpu.VMEM((12, LK), F32),
            pltpu.VMEM((48, 384), BF),
            pltpu.VMEM((48, 384), BF),
            pltpu.VMEM((48, 384), BF),
            pltpu.VMEM((36, 384), BF),
            pltpu.VMEM((36, 384), BF),
            pltpu.VMEM((72, 384), BF),
            pltpu.SMEM((3,), F32),
            pltpu.VMEM((3, 128), BF),
            pltpu.VMEM((528, 384), BF),
            pltpu.VMEM((1, 384), BF),
            pltpu.SemaphoreType.DMA((14,)),
            pltpu.VMEM((NY, NZ, NX, LK, 128), BF),
            pltpu.VMEM((NY, NZ, NX, LK, 128), BF),
            pltpu.VMEM((K, 128), BF),
            pltpu.VMEM((128, 384), BF),
            pltpu.VMEM((128, 384), BF),
            pltpu.VMEM((128, 384), BF),
            pltpu.VMEM((256, 384), BF),
            pltpu.VMEM((16, 128), F32),
            pltpu.VMEM((16, K), F32),
            pltpu.VMEM((8, K), F32),
            pltpu.VMEM((8, K), F32),
            pltpu.VMEM((4, K), BF),
            pltpu.VMEM((4, K), BF),
            pltpu.VMEM((ROWS, 4, 128), BF),
            pltpu.VMEM((ROWS, 4, 128), BF),
            pltpu.VMEM((ROWS * 4, 128), F32),
            pltpu.VMEM((ROWS * 4, 128), F32),
            pltpu.VMEM((LK, 1280), F32),
            pltpu.VMEM((80, 384), F32),
            pltpu.VMEM((80, 384), F32),
            dma, dma((4, len(PLAN))), dma((4, len(PLAN))), dma, dma, dma, dma, dma, dma, dma,
        ],
        compiler_params=pltpu.CompilerParams(
            collective_id=0, has_side_effects=True, vmem_limit_bytes=66900000
        ),
    )(
        query_single, key_single, pair, query_frames.T, key_frames, w_query.T, w_key.T, w_value.T,
        w_query_points.T, w_key_points.T, w_value_points.T, head_weight, bias_weight, w_out, d_out,
    )
    return pl.pallas_call(
        finish,
        out_shape=(
            jax.ShapeDtypeStruct((1, 384), BF),
            jax.ShapeDtypeStruct((1, 384), F32),
            jax.ShapeDtypeStruct((LK, 384), F32),
        ),
        in_specs=[vmem],
        out_specs=(vmem, vmem, vmem),
        compiler_params=pltpu.CompilerParams(vmem_limit_bytes=16 * 1024 * 1024),
    )(total)


def solution(mesh):
    return jax.shard_map(
        shards,
        mesh=mesh,
        in_specs=(
            P("row", None),
            P("row", None),
            P("row", None, None),
            P(None, "row"),
            P(None, "row"),
            P(None, "head"),
            P(None, "head"),
            P(None, "head"),
            P(None, "head"),
            P(None, "head"),
            P(None, "head"),
            P("head"),
            P("head", None),
            P("head", None),
            P("row", None),
        ),
        out_specs=(P("row", None), P("row", None), P("row", None)),
        check_vma=False,
    )
```

```python
import functools
import math

import jax
import jax.numpy as jnp
from jax import lax
from jax.experimental import pallas as pl
from jax.experimental.pallas import tpu as pltpu
from jax.sharding import PartitionSpec as P

NY, NZ, NX = 4, 8, 4
ROWS = NY * NZ * NX
LK = 64
K = ROWS * LK
SIZES = (NY, NZ, NX)
LOGIT_SCALE = math.sqrt(1.0 / 3.0)
POINT_SCALE = math.sqrt(2.0 / 36.0)
MESH = pl.DeviceIdType.MESH
BF, F32 = jnp.bfloat16, jnp.float32

STREAMS = (
    (0, 0, 32, (0, 1, 2)),
    (0, 32, 32, (2, 1, 0)),
    (1, 0, 32, (0, 1, 2)),
    (1, 32, 32, (2, 1, 0)),
)
SLOTS = 7


def gather_plan():
    plan = []

    def add(rnd, name, needs, axis, step, offsets, half=None):
        plan.append((rnd, name, needs, axis, step, offsets, half))

    for sign, mark in ((1, "+"), (-1, "-")):
        add(0, "a" + mark, (), 0, sign, (0, 0, 0))
    add(0, "b", (), 0, 2, (0, 0, 0))
    first = ("a+", "a-", "b")
    for k in range(NZ // 2):
        for sign, mark in ((1, "+"), (-1, "-")):
            needs = first if k == 0 else ("c%d%s" % (k - 1, mark),)
            half = "blocks" if k == NZ // 2 - 1 else None
            add(1 + k, "c%d%s" % (k, mark), needs, 1, sign, (None, -sign * k, 0), half)
    for k in range(NZ // 2 + 1):
        for side in (1, -1) if 0 < k < NZ // 2 else (1,):
            offset = -side * k
            if k == 0:
                needs = first
            elif k == NZ // 2:
                needs = ("c%d+" % (k - 1), "c%d-" % (k - 1))
            else:
                needs = ("c%d%s" % (k - 1, "+" if side == 1 else "-"),)
            for sign, mark in ((1, "+"), (-1, "-")):
                name = "%d%s" % (offset, mark)
                add(1 + k, "d" + name, needs, 2, sign, (None, offset, 0))
                if k < NZ // 2:
                    add(2 + k, "e" + name, ("d" + name,), 2, sign, (None, offset, -sign), "blocks")
            if k == NZ // 2:
                add(1 + k, "e%d" % offset, needs, 2, 2, (None, offset, 0))
    return sorted(plan, key=lambda item: (item[0], item[1]))


PLAN = gather_plan()
NUMBER = {item[1]: n for n, item in enumerate(PLAN)}


def nt(a, b):
    return lax.dot_general(a, b, (((1,), (1,)), ((), ())), preferred_element_type=F32)


def nn(a, b):
    return lax.dot_general(a, b, (((1,), (0,)), ((), ())), preferred_element_type=F32)


def tn(a, b, precision=None):
    return lax.dot_general(
        a, b, (((0,), (0,)), ((), ())), preferred_element_type=F32, precision=precision
    )


def iotas(shape):
    return (
        lax.broadcasted_iota(jnp.int32, shape, 0),
        lax.broadcasted_iota(jnp.int32, shape, 1),
    )


def third(value):
    return lax.shift_right_logical(value * 43, 7)


def within(lane, start, count):
    return (lane >= start) & (lane < start + count)


SHIFTS = (0, 1, 2, -1, -2)


def selection():
    j, l = iotas((12, 128))
    x = l - 3 * third(l)
    parts = []
    for d in SHIFTS:
        ok = (x + d >= 0) & (x + d < 3)
        parts.append(ok & (j == 4 * x + d))
    parts.append(j == 9 + x)
    for d in SHIFTS[1:]:
        ok = (x + d >= 0) & (x + d < 3)
        parts.append(ok & (j == 4 * x + 3 * d))
    return jnp.concatenate([jnp.where(p, 1.0, 0.0) for p in parts], axis=1)


def part(pat, i):
    return pat[:, 128 * i : 128 * i + 128]


def shifted(v, d):
    return v if d == 0 else pltpu.roll(v, (-d) % 128, 1)


def rotated(v, pat):
    return sum(part(pat, i) * shifted(v, d) for i, d in enumerate(SHIFTS))


def unrotated(v, pat):
    out = part(pat, 0) * v
    for i, d in enumerate(SHIFTS[1:]):
        out = out + part(pat, 6 + i) * shifted(v, d)
    return out


def fold(x, combine):
    parts = [x[:, 128 * n : 128 * n + 128] for n in range(x.shape[1] // 128)]
    while len(parts) > 1:
        parts = [combine(*parts[n : n + 2]) for n in range(0, len(parts), 2)]
    return parts[0]


def softplus(x):
    return jnp.maximum(x, 0.0) + jnp.log1p(jnp.exp(-jnp.abs(x)))


def by_head(index, values):
    return jnp.where(index == 0, values[0], jnp.where(index == 1, values[1], values[2]))


def mask_k(r, l):
    return within(l, 16 * r, 16) & (r < 3), within(l, 48 + 12 * r, 12) & (r < 3)


def mask_v(r, l):
    return (within(l, 16 * r, 16) | within(l, 48 + 24 * r, 24)) & (r < 3)


def kernel(
    qs_h, ks_h, pair, qfr_h, kfr_h, w_q_h, w_k_h, w_v_h, w_qp_h, w_kp_h, w_vp_h, hw_h, bw_h,
    w_o_h, d_o_h,
    o_sum,
    qs, ks, qfr, kfr, w_q, w_k, w_v, w_qp, w_kp, w_vp, hw, bw, w_o, d_o, in_sem,
    buf_k, buf_v, pair_s, wq_s, wk_s, wv_s, wp_s, lhs_s, pb_s, att_s, da_s, msg_a, msg_s, recv_a, recv_s, unpack_a, unpack_s,
    pat_s, part_s, got_s,
    pair_sem, send_sem, recv_sem, a_send, a_recv, s_send, s_recv, own_sem, ex_send, ex_recv,
):
    row = lax.axis_index("row")
    core = lax.axis_index("head")
    loads = [
        pltpu.make_async_copy(src, dst, in_sem.at[n])
        for n, (src, dst) in enumerate(
            (
                (ks_h, ks), (kfr_h, kfr), (w_k_h, w_k), (w_kp_h, w_kp), (w_v_h, w_v), (w_vp_h, w_vp),
                (qs_h, qs), (qfr_h, qfr), (w_q_h, w_q), (w_qp_h, w_qp), (hw_h, hw), (bw_h, bw),
                (w_o_h, w_o), (d_o_h, d_o),
            )
        )
    ]
    for load in loads:
        load.start()
    coords = (lax.div(row, NZ * NX), lax.rem(lax.div(row, NX), NZ), lax.rem(row, NX))
    places = {}

    def place(axis, offset):
        if offset == 0:
            return coords[axis]
        if (axis, offset) not in places:
            places[axis, offset] = lax.rem(coords[axis] + offset + SIZES[axis], SIZES[axis])
        return places[axis, offset]

    def neighbour(axis, step):
        moved = list(coords)
        moved[axis] = place(axis, step)
        return (moved[0] * NZ + moved[1]) * NX + moved[2]

    barrier = pltpu.get_barrier_semaphore()
    for axis, steps in ((0, (1, -1, 2)), (1, (1, -1)), (2, (1, -1, 2))):
        for step in steps:
            pl.semaphore_signal(
                barrier, inc=1, device_id=(neighbour(axis, step), core), device_id_type=MESH
            )
    pl.semaphore_signal(barrier, inc=1, device_id=(row, 1 - core), device_id_type=MESH)
    pair_copy = pltpu.make_async_copy(pair.at[0], pair_s, pair_sem)
    pair_copy.start()

    select = selection()
    for load in loads[:4]:
        load.wait()
    wk_s[...] = jnp.zeros_like(wk_s)
    wk_s[0:48, :] = w_k[...]
    wk_s[48:84, :] = w_kp[...]
    pat = tn(kfr[...], select, lax.Precision.HIGHEST)
    pat_s[...] = pat
    r64, l64 = iotas((LK, 128))
    feat = nt(ks[...], wk_s[...])
    k_rows = jnp.where(
        l64 < 48, feat, jnp.where(l64 < 84, rotated(feat, pat) + part(pat, 5), 0.0)
    ).astype(BF)
    k_full = k_rows.astype(F32)
    square = k_full * k_full
    for h in range(3):
        total = jnp.sum(
            jnp.where(within(l64, 48 + 12 * h, 12), square, 0.0), axis=1, keepdims=True
        )
        high = total.astype(BF).astype(F32)
        middle = (total - high).astype(BF).astype(F32)
        low = total - high - middle
        at = 84 + 3 * h
        k_full = jnp.where(
            l64 == at, high, jnp.where(l64 == at + 1, middle, jnp.where(l64 == at + 2, low, k_full))
        )
    mine = (pl.ds(coords[0], 1), pl.ds(coords[1], 1), pl.ds(coords[2], 1))
    buf_k[mine] = k_full.astype(BF).reshape(1, 1, 1, LK, 128)

    bufs = (buf_k, buf_v)

    seen = [set() for _ in STREAMS]

    def gather_copy(s, item):
        which, start, count, order = STREAMS[s]
        _, name, _, axis, step, offsets, half = item
        at = [None] * 3
        for a, offset in zip(order, offsets):
            if offset is None:
                at[a] = pl.ds(0, SIZES[a])
            else:
                at[a] = pl.ds(place(a, offset), 1)
        second = 0 if step == 1 else 1
        if half == "blocks":
            a = order[0]
            at[a] = pl.ds(second * (SIZES[a] // 2), SIZES[a] // 2)
        where = bufs[which].at[at[0], at[1], at[2], pl.ds(start, count)]
        n = NUMBER[name]
        return pltpu.make_async_remote_copy(
            src_ref=where,
            dst_ref=where,
            send_sem=send_sem.at[s, n],
            recv_sem=recv_sem.at[s, n],
            device_id=(neighbour(order[axis], step), core),
            device_id_type=MESH,
        )

    def arrive(s, name):
        if name not in seen[s]:
            seen[s].add(name)
            gather_copy(s, PLAN[NUMBER[name]]).wait_recv()

    def gather_round(s, rnd, last):
        for item in PLAN:
            if item[0] == rnd and (item[1][0] == "e") == last:
                for name in item[2]:
                    arrive(s, name)
                gather_copy(s, item).start()
        if rnd == SLOTS - 1 and last:
            for item in PLAN:
                arrive(s, item[1])

    def gather_slot(slot, streams=range(4)):
        for last in (False, True):
            for s in streams:
                gather_round(s, slot, last)

    pl.semaphore_wait(barrier, 9)
    gather_slot(0, (0, 1))
    for load in loads[4:6]:
        load.wait()
    wv_s[...] = jnp.zeros_like(wv_s)
    wv_s[0:48, :] = w_v[...]
    wv_s[48:120, :] = w_vp[...]
    feat = nt(ks[...], wv_s[...])
    v_rows = jnp.where(
        l64 < 48, feat, jnp.where(l64 < 120, rotated(feat, pat) + part(pat, 5), 0.0)
    ).astype(BF)
    buf_v[mine] = v_rows.reshape(1, 1, 1, LK, 128)
    gather_slot(0, (2, 3))

    for load in loads[6:]:
        load.wait()
    wq_s[...] = jnp.zeros_like(wq_s)
    wq_s[0:48, :] = w_q[...]
    wq_s[48:84, :] = w_qp[...]
    pat_q = lax.dot_general(
        qfr[...], select, (((1,), (0,)), ((), ())),
        preferred_element_type=F32, precision=lax.Precision.HIGHEST,
    )
    _, l1 = iotas((1, 128))
    x1 = l1 - 3 * third(l1)
    feat = nt(qs[...], wq_s[...])
    q_row = jnp.where(
        l1 < 48, feat, jnp.where(l1 < 84, rotated(feat, pat_q) + part(pat_q, 5), 0.0)
    )
    q_row = q_row.astype(BF).astype(F32)
    r8, l8 = iotas((8, 128))
    raw = [hw[0], hw[1], hw[2]]
    gain = (softplus(by_head(r8, raw)) * POINT_SCALE)[:, 0:1]
    keys8, points8 = mask_k(r8, l8)
    values8 = mask_v(r8, l8)
    q8 = jnp.broadcast_to(q_row, (8, 128))
    q_square = jnp.sum(jnp.where(points8, q8 * q8, 0.0), axis=1, keepdims=True)
    lhs_q = jnp.concatenate(
        [
            jnp.where(keys8, q8, 0.0),
            jnp.where(points8, q8, jnp.where(within(l8, 84 + 3 * r8, 3) & (r8 < 3), -0.5, 0.0)),
        ],
        axis=0,
    ).astype(BF)

    gather_slot(1)
    i256, _ = iotas((256, 1))
    i = i256 & 127
    j = i - 48
    head = lax.shift_right_logical(j * 43, 10)
    point = third(j)
    p_head = lax.shift_right_logical(point, 3)
    source = jnp.where(
        i256 < 128,
        jnp.where(i < 48, 176 * lax.shift_right_logical(i, 4) + (i & 15), 152 * head + 16 + j),
        176 * p_head + 40 + (point & 7),
    )
    valid = (i < 120) & ((i256 < 128) | (i >= 48))
    source = jnp.where(valid, source, -1)
    _, lane_o = iotas((256, 528))
    pick = jnp.where(lane_o == source, 1.0, 0.0).astype(BF)
    wp_s[...] = nn(pick, w_o[...]).astype(BF)
    d_feat = nt(d_o[...], wp_s[...])
    lhs_s[...] = jnp.zeros_like(lhs_s)
    lhs_s[0:3, :] = bw[...].astype(F32)
    for h in range(3):
        lhs_s[8 + h : 9 + h, :] = nt(d_o[...], w_o[176 * h + 48 : 176 * h + 176, :])
    lhs_p = lhs_s[...].astype(BF)
    pair_copy.wait()

    def pair_step(g, _):
        at = pl.multiple_of(g * 1024, 1024)
        pb_s[:, pl.ds(at, 1024)] = nt(lhs_p, pair_s[pl.ds(at, 1024), :])
        return 0

    for slot in range(2, SLOTS - 1):
        lax.fori_loop((slot - 2) * 2, (slot - 1) * 2, pair_step, 0)
        gather_slot(slot)
    gather_slot(SLOTS - 1, (0, 1))

    def chunk(ref, g):
        return ref[pl.ds(lax.div(g, 2), 1), pl.ds(lax.rem(g, 2) * 4, 4)].reshape(1024, 128)

    def logit_step(g, top):
        at = pl.multiple_of(g * 1024, 1024)
        both = nt(lhs_q, chunk(buf_k, g))
        logits = LOGIT_SCALE * (
            both[0:8] * 0.25
            + pb_s[0:8, pl.ds(at, 1024)]
            + gain * (both[8:16] - 0.5 * q_square)
        )
        att_s[:, pl.ds(at, 1024)] = logits
        return jnp.maximum(top, fold(logits, jnp.maximum))

    top = lax.fori_loop(0, 8, logit_step, jnp.full((8, 128), -3.0e38, F32), unroll=8)
    top = jnp.max(top, axis=1, keepdims=True)

    def exp_step(g, total):
        at = pl.multiple_of(g * 1024, 1024)
        e = jnp.exp(att_s[:, pl.ds(at, 1024)] - top)
        att_s[:, pl.ds(at, 1024)] = e
        return total + fold(e, jnp.add)

    zero8 = jnp.zeros((8, 128), F32)
    total = lax.fori_loop(0, 8, exp_step, zero8, unroll=8)
    gather_slot(SLOTS - 1, (2, 3))
    inverse = 1.0 / jnp.sum(total, axis=1, keepdims=True)

    rotate = lax.div(row, 16)
    inner = [lax.rem(row + n, 16) for n in range(16)]
    pairs = [lax.div(n, 2) * 128 for n in inner]
    rc, _ = iotas((8, 1024))

    def group(i):
        return lax.rem(i + rotate, 8)

    def start_sends(message, landing, send, recv, i):
        g = group(i)
        for n in range(1 if i == 0 else 0, 16):
            at = pl.multiple_of(g * 1024 + pairs[n], 128)
            pltpu.make_async_remote_copy(
                src_ref=message.at[:, pl.ds(at, 128)],
                dst_ref=landing.at[row],
                send_sem=send,
                recv_sem=recv,
                device_id=(g * 16 + inner[n], core),
                device_id_type=MESH,
            ).start()

    def own_copy(message, landing):
        at = pl.multiple_of(lax.div(row, 2) * 128, 128)
        return pltpu.make_async_copy(message.at[:, pl.ds(at, 128)], landing.at[row], own_sem)

    def all_of(landing, sem):
        everyone = landing.at[pl.ds(0, ROWS - 1)]
        return pltpu.make_async_copy(everyone, everyone, sem)

    def attend_step(i, acc_v):
        g = group(i)
        if i:
            start_sends(msg_a, recv_a, a_send, a_recv, i - 1)

        at = pl.multiple_of(g * 1024, 1024)
        a = att_s[:, pl.ds(at, 1024)] * inverse
        att_s[:, pl.ds(at, 1024)] = a
        msg_a[:, pl.ds(at, 1024)] = jnp.where(rc < 3, a, side_k)[0:4].astype(BF)
        return acc_v + nn(a.astype(BF), chunk(buf_v, g))

    side_k = jnp.concatenate([q8] * 8, axis=1)
    acc_v = zero8
    for i in range(8):
        acc_v = attend_step(i, acc_v)
    start_sends(msg_a, recv_a, a_send, a_recv, 7)
    own_a = own_copy(msg_a, recv_a)
    own_a.start()
    row_v = jnp.sum(jnp.where(values8, acc_v, 0.0), axis=0, keepdims=True)
    is_point = within(l1, 48, 72)
    local = jnp.where(is_point, unrotated(jnp.where(is_point, row_v - part(pat_q, 5), 0.0), pat_q), 0.0)
    squares = local * local
    norm = squares
    for d in SHIFTS[1:]:
        norm = norm + jnp.where((x1 + d >= 0) & (x1 + d < 3), shifted(squares, d), 0.0)
    lengths = jnp.sqrt(1.0 + norm)
    d_local = d_feat[:, 0:128] + d_feat[:, 128:256] / lengths * local
    d_local = jnp.where(is_point, d_local, 0.0)
    side_v = jnp.where(
        l1 < 48, d_feat[:, 0:128], jnp.where(is_point, rotated(d_local, pat_q), 0.0)
    )
    side_v8 = jnp.broadcast_to(side_v, (8, 128))
    lhs_v = jnp.where(values8, side_v8, 0.0).astype(BF)

    def grad_step(g, carry):
        at = pl.multiple_of(g * 1024, 1024)
        d_att = nt(lhs_v, chunk(buf_v, g)) + pb_s[8:16, pl.ds(at, 1024)]
        da_s[:, pl.ds(at, 1024)] = d_att
        return carry + fold(att_s[:, pl.ds(at, 1024)] * d_att, jnp.add)

    row_total = lax.fori_loop(0, 8, grad_step, zero8, unroll=8)
    row_total = jnp.sum(row_total, axis=1, keepdims=True)
    side_v = jnp.concatenate([side_v8] * 8, axis=1)

    def score_step(i, sums):
        g = group(i)
        if i:
            start_sends(msg_s, recv_s, s_send, s_recv, i - 1)

        at = pl.multiple_of(g * 1024, 1024)
        a = att_s[:, pl.ds(at, 1024)]
        score = LOGIT_SCALE * a * (da_s[:, pl.ds(at, 1024)] - row_total)
        msg_s[:, pl.ds(at, 1024)] = jnp.where(rc < 3, score, side_v)[0:4].astype(BF)
        score = score.astype(BF).astype(F32)
        da_s[:, pl.ds(at, 1024)] = score
        return sums + fold(score, jnp.add)

    score_rows = zero8
    for i in range(8):
        score_rows = score_step(i, score_rows)
    score_rows = jnp.sum(score_rows, axis=1, keepdims=True)
    start_sends(msg_s, recv_s, s_send, s_recv, 7)
    own_a.wait()
    own_s = own_copy(msg_s, recv_s)
    own_s.start()

    def rest_step(g, carry):
        acc_k, acc_p = carry
        at = pl.multiple_of(g * 1024, 1024)
        return (
            acc_k + nn(da_s[:, pl.ds(at, 1024)].astype(BF), chunk(buf_k, g)),
            acc_p + nn(att_s[:, pl.ds(at, 1024)].astype(BF), pair_s[pl.ds(at, 1024), :]),
        )

    acc_k, acc_p = lax.fori_loop(0, 8, rest_step, (zero8, zero8), unroll=4)
    f_v = jnp.where(l1 < 48, row_v, local).astype(BF)
    f_len = jnp.where(is_point & (x1 == 0), lengths, 0.0).astype(BF)
    out_row = nn(f_v, wp_s[0:128, :]) + nn(f_len, wp_s[128:256, :])
    for h in range(3):
        out_row = out_row + nn(
            acc_p[h : h + 1, :].astype(BF), w_o[176 * h + 48 : 176 * h + 176, :]
        )
    part_s[64:65, :] = out_row

    q_terms = jnp.where(keys8, acc_k * 0.25, 0.0) + jnp.where(
        points8, gain * (acc_k - score_rows * q8), 0.0
    )
    d_q = jnp.sum(q_terms, axis=0, keepdims=True)
    d_q = jnp.where(l1 < 48, d_q, jnp.where(l1 < 84, unrotated(d_q, pat_q), 0.0)).astype(BF)
    part_s[72:73, :] = nn(d_q, wq_s[...])

    _, l128 = iotas((ROWS, 128))

    def unpack(landing, unpacked):
        def step(i, _):
            at = pl.multiple_of(i * 32, 32)
            unpacked[pl.ds(at, 32), :] = landing[pl.ds(i * 8, 8)].astype(F32).reshape(32, 128)
            return 0

        lax.fori_loop(0, ROWS // 8, step, 0, unroll=4)
        return [unpacked[pl.ds(n, ROWS, stride=4), :] for n in range(4)]

    odd = lax.rem(row, 2) == 1

    def mine_of(x):
        return jnp.where(odd, x[64:128], x[0:64])

    for s in range(4):
        for item in PLAN:
            gather_copy(s, item).wait_send()
    all_of(recv_a, a_recv).wait()
    *att_h, side_k = unpack(recv_a, unpack_a)
    keys_h = [within(l128, 16 * h, 16) for h in range(3)]
    points_h = [within(l128, 48 + 12 * h, 12) for h in range(3)]
    rights = [
        jnp.concatenate(
            [
                jnp.where(keys_h[h] | points_h[h], side_k, 0.0).astype(BF),
                jnp.where(points_h[h], 1.0, 0.0).astype(BF),
            ],
            axis=1,
        )
        for h in range(3)
    ]
    pat = pat_s[...]
    kf = buf_k[mine].reshape(LK, 128).astype(F32)
    gain_l = softplus(by_head(jnp.where(l1 < 60, 0, jnp.where(l1 < 72, 1, 2)), raw)) * POINT_SCALE

    all_of(recv_s, s_recv).wait()
    own_s.wait()
    *score_h, side_v = unpack(recv_s, unpack_s)
    out_v = jnp.zeros((128, 128), F32)
    both = jnp.zeros((128, 256), F32)
    for h in range(3):
        score = score_h[h].astype(BF)
        vpoints_h = within(l128, 48 + 24 * h, 24)
        out_v = out_v + tn(
            att_h[h].astype(BF), jnp.where(keys_h[h] | vpoints_h, side_v, 0.0).astype(BF)
        )
        both = both + tn(score, rights[h])
    out_v, both = mine_of(out_v), mine_of(both)
    out_k, sums = both[:, 0:128], both[:, 128:256]
    d_points = jnp.where(within(l64, 48, 36), gain_l * (out_k - sums * kf), 0.0)
    d_k = jnp.where(l64 < 48, out_k * 0.25, jnp.where(l64 < 84, unrotated(d_points, pat), 0.0))
    d_v = jnp.where(l64 < 48, out_v, jnp.where(l64 < 120, unrotated(out_v, pat), 0.0))
    part_s[0:64, :] = nn(d_k.astype(BF), wk_s[...]) + nn(d_v.astype(BF), wv_s[...])

    exchange = pltpu.make_async_remote_copy(
        src_ref=part_s,
        dst_ref=got_s,
        send_sem=ex_send,
        recv_sem=ex_recv,
        device_id=(row, 1 - core),
        device_id_type=MESH,
    )
    exchange.start()
    all_of(recv_a, a_send).wait()
    all_of(recv_s, s_send).wait()
    exchange.wait()
    o_sum[...] = part_s[...] + got_s[...]


def finish(total, o_out, o_gq, o_gk):
    o_gk[...] = total[0:64, :]
    o_out[...] = total[64:65, :].astype(BF)
    o_gq[...] = total[72:73, :]


def shards(
    query_single, key_single, pair, query_frames, key_frames, w_query, w_key, w_value,
    w_query_points, w_key_points, w_value_points, head_weight, bias_weight, w_out, d_out,
):
    vmem = pl.BlockSpec(memory_space=pltpu.VMEM)
    specs = [pl.BlockSpec(memory_space=pltpu.HBM)] * 15
    dma = pltpu.SemaphoreType.DMA
    total = pl.pallas_call(
        kernel,
        out_shape=pltpu.VMEM((80, 384), F32),
        in_specs=specs,
        out_specs=vmem,
        scratch_shapes=[
            pltpu.VMEM((1, 384), BF),
            pltpu.VMEM((LK, 384), BF),
            pltpu.VMEM((1, 12), F32),
            pltpu.VMEM((12, LK), F32),
            pltpu.VMEM((48, 384), BF),
            pltpu.VMEM((48, 384), BF),
            pltpu.VMEM((48, 384), BF),
            pltpu.VMEM((36, 384), BF),
            pltpu.VMEM((36, 384), BF),
            pltpu.VMEM((72, 384), BF),
            pltpu.SMEM((3,), F32),
            pltpu.VMEM((3, 128), BF),
            pltpu.VMEM((528, 384), BF),
            pltpu.VMEM((1, 384), BF),
            pltpu.SemaphoreType.DMA((14,)),
            pltpu.VMEM((NY, NZ, NX, LK, 128), BF),
            pltpu.VMEM((NY, NZ, NX, LK, 128), BF),
            pltpu.VMEM((K, 128), BF),
            pltpu.VMEM((128, 384), BF),
            pltpu.VMEM((128, 384), BF),
            pltpu.VMEM((128, 384), BF),
            pltpu.VMEM((256, 384), BF),
            pltpu.VMEM((16, 128), F32),
            pltpu.VMEM((16, K), F32),
            pltpu.VMEM((8, K), F32),
            pltpu.VMEM((8, K), F32),
            pltpu.VMEM((4, K), BF),
            pltpu.VMEM((4, K), BF),
            pltpu.VMEM((ROWS, 4, 128), BF),
            pltpu.VMEM((ROWS, 4, 128), BF),
            pltpu.VMEM((ROWS * 4, 128), F32),
            pltpu.VMEM((ROWS * 4, 128), F32),
            pltpu.VMEM((LK, 1280), F32),
            pltpu.VMEM((80, 384), F32),
            pltpu.VMEM((80, 384), F32),
            dma, dma((4, len(PLAN))), dma((4, len(PLAN))), dma, dma, dma, dma, dma, dma, dma,
        ],
        compiler_params=pltpu.CompilerParams(
            collective_id=0, has_side_effects=True, vmem_limit_bytes=66900000
        ),
    )(
        query_single, key_single, pair, query_frames.T, key_frames, w_query.T, w_key.T, w_value.T,
        w_query_points.T, w_key_points.T, w_value_points.T, head_weight, bias_weight, w_out, d_out,
    )
    return pl.pallas_call(
        finish,
        out_shape=(
            jax.ShapeDtypeStruct((1, 384), BF),
            jax.ShapeDtypeStruct((1, 384), F32),
            jax.ShapeDtypeStruct((LK, 384), F32),
        ),
        in_specs=[vmem],
        out_specs=(vmem, vmem, vmem),
        compiler_params=pltpu.CompilerParams(vmem_limit_bytes=16 * 1024 * 1024),
    )(total)


def solution(mesh):
    return jax.shard_map(
        shards,
        mesh=mesh,
        in_specs=(
            P("row", None),
            P("row", None),
            P("row", None, None),
            P(None, "row"),
            P(None, "row"),
            P(None, "head"),
            P(None, "head"),
            P(None, "head"),
            P(None, "head"),
            P(None, "head"),
            P(None, "head"),
            P("head"),
            P("head", None),
            P("head", None),
            P("row", None),
        ),
        out_specs=(P("row", None), P("row", None), P("row", None)),
        check_vma=False,
    )
```

```python
import functools
import math

import jax
import jax.numpy as jnp
from jax import lax
from jax.experimental import pallas as pl
from jax.experimental.pallas import tpu as pltpu
from jax.sharding import PartitionSpec as P

NY, NZ, NX = 4, 8, 4
ROWS = NY * NZ * NX
LK = 64
K = ROWS * LK
SIZES = (NY, NZ, NX)
LOGIT_SCALE = math.sqrt(1.0 / 3.0)
POINT_SCALE = math.sqrt(2.0 / 36.0)
MESH = pl.DeviceIdType.MESH
BF, F32 = jnp.bfloat16, jnp.float32

STREAMS = (
    (0, 0, 32, (0, 1, 2)),
    (0, 32, 32, (2, 1, 0)),
    (1, 0, 32, (0, 1, 2)),
    (1, 32, 32, (2, 1, 0)),
)
SLOTS = 7


def gather_plan():
    plan = []

    def add(rnd, name, needs, axis, step, offsets, half=None):
        plan.append((rnd, name, needs, axis, step, offsets, half))

    for sign, mark in ((1, "+"), (-1, "-")):
        add(0, "a" + mark, (), 0, sign, (0, 0, 0))
    add(0, "b", (), 0, 2, (0, 0, 0))
    first = ("a+", "a-", "b")
    for k in range(NZ // 2):
        for sign, mark in ((1, "+"), (-1, "-")):
            needs = first if k == 0 else ("c%d%s" % (k - 1, mark),)
            half = "blocks" if k == NZ // 2 - 1 else None
            add(1 + k, "c%d%s" % (k, mark), needs, 1, sign, (None, -sign * k, 0), half)
    for k in range(NZ // 2 + 1):
        for side in (1, -1) if 0 < k < NZ // 2 else (1,):
            offset = -side * k
            if k == 0:
                needs = first
            elif k == NZ // 2:
                needs = ("c%d+" % (k - 1), "c%d-" % (k - 1))
            else:
                needs = ("c%d%s" % (k - 1, "+" if side == 1 else "-"),)
            for sign, mark in ((1, "+"), (-1, "-")):
                name = "%d%s" % (offset, mark)
                add(1 + k, "d" + name, needs, 2, sign, (None, offset, 0))
                if k < NZ // 2:
                    add(2 + k, "e" + name, ("d" + name,), 2, sign, (None, offset, -sign), "blocks")
            if k == NZ // 2:
                add(1 + k, "e%d" % offset, needs, 2, 2, (None, offset, 0))
    return sorted(plan, key=lambda item: (item[0], item[1]))


PLAN = gather_plan()
NUMBER = {item[1]: n for n, item in enumerate(PLAN)}


def nt(a, b):
    return lax.dot_general(a, b, (((1,), (1,)), ((), ())), preferred_element_type=F32)


def nn(a, b):
    return lax.dot_general(a, b, (((1,), (0,)), ((), ())), preferred_element_type=F32)


def tn(a, b, precision=None):
    return lax.dot_general(
        a, b, (((0,), (0,)), ((), ())), preferred_element_type=F32, precision=precision
    )


def iotas(shape):
    return (
        lax.broadcasted_iota(jnp.int32, shape, 0),
        lax.broadcasted_iota(jnp.int32, shape, 1),
    )


def third(value):
    return lax.shift_right_logical(value * 43, 7)


def within(lane, start, count):
    return (lane >= start) & (lane < start + count)


SHIFTS = (0, 1, 2, -1, -2)


def selection():
    j, l = iotas((12, 128))
    x = l - 3 * third(l)
    parts = []
    for d in SHIFTS:
        ok = (x + d >= 0) & (x + d < 3)
        parts.append(ok & (j == 4 * x + d))
    parts.append(j == 9 + x)
    back = []
    for d in SHIFTS[1:]:
        ok = (x + d >= 0) & (x + d < 3)
        back.append(ok & (j == 4 * x + 3 * d))
    return tuple(
        jnp.concatenate([jnp.where(p, 1.0, 0.0) for p in group], axis=1) for group in (parts, back)
    )


def part(pat, i):
    return pat[:, 128 * i : 128 * i + 128]


def shifted(v, d):
    return v if d == 0 else pltpu.roll(v, (-d) % 128, 1)


def rotated(v, pat):
    return sum(part(pat, i) * shifted(v, d) for i, d in enumerate(SHIFTS))


def unrotated(v, pat):
    out = part(pat, 0) * v
    for i, d in enumerate(SHIFTS[1:]):
        out = out + part(pat, 6 + i) * shifted(v, d)
    return out


def fold(x, combine):
    parts = [x[:, 128 * n : 128 * n + 128] for n in range(x.shape[1] // 128)]
    while len(parts) > 1:
        parts = [combine(*parts[n : n + 2]) for n in range(0, len(parts), 2)]
    return parts[0]


def softplus(x):
    return jnp.maximum(x, 0.0) + jnp.log1p(jnp.exp(-jnp.abs(x)))


def by_head(index, values):
    return jnp.where(index == 0, values[0], jnp.where(index == 1, values[1], values[2]))


def mask_k(r, l):
    return within(l, 16 * r, 16) & (r < 3), within(l, 48 + 12 * r, 12) & (r < 3)


def mask_v(r, l):
    return (within(l, 16 * r, 16) | within(l, 48 + 24 * r, 24)) & (r < 3)


def kernel(
    qs_h, ks_h, pair, qfr_h, kfr_h, w_q_h, w_k_h, w_v_h, w_qp_h, w_kp_h, w_vp_h, hw_h, bw_h,
    w_o_h, d_o_h,
    o_sum,
    qs, ks, qfr, kfr, w_q, w_k, w_v, w_qp, w_kp, w_vp, hw, bw, w_o, d_o, in_sem,
    buf_k, buf_v, pair_s, wq_s, wk_s, wv_s, wp_s, lhs_s, pb_s, att_s, da_s, msg_a, msg_s, recv_a, recv_s, unpack_a, unpack_s,
    pat_s, part_s, got_s,
    pair_sem, send_sem, recv_sem, a_send, a_recv, s_send, s_recv, own_sem, ex_send, ex_recv,
):
    row = lax.axis_index("row")
    core = lax.axis_index("head")
    loads = [
        pltpu.make_async_copy(src, dst, in_sem.at[n])
        for n, (src, dst) in enumerate(
            (
                (ks_h, ks), (kfr_h, kfr), (w_k_h, w_k), (w_kp_h, w_kp), (w_v_h, w_v), (w_vp_h, w_vp),
                (qs_h, qs), (qfr_h, qfr), (w_q_h, w_q), (w_qp_h, w_qp), (hw_h, hw), (bw_h, bw),
                (w_o_h, w_o), (d_o_h, d_o),
            )
        )
    ]
    for load in loads:
        load.start()
    coords = (lax.div(row, NZ * NX), lax.rem(lax.div(row, NX), NZ), lax.rem(row, NX))
    places = {}

    def place(axis, offset):
        if offset == 0:
            return coords[axis]
        if (axis, offset) not in places:
            places[axis, offset] = lax.rem(coords[axis] + offset + SIZES[axis], SIZES[axis])
        return places[axis, offset]

    def neighbour(axis, step):
        moved = list(coords)
        moved[axis] = place(axis, step)
        return (moved[0] * NZ + moved[1]) * NX + moved[2]

    barrier = pltpu.get_barrier_semaphore()
    for axis, steps in ((0, (1, -1, 2)), (1, (1, -1)), (2, (1, -1, 2))):
        for step in steps:
            pl.semaphore_signal(
                barrier, inc=1, device_id=(neighbour(axis, step), core), device_id_type=MESH
            )
    pl.semaphore_signal(barrier, inc=1, device_id=(row, 1 - core), device_id_type=MESH)
    pair_copy = pltpu.make_async_copy(pair.at[0], pair_s, pair_sem)
    pair_copy.start()

    select, select_back = selection()
    for load in loads[:4]:
        load.wait()
    wk_s[...] = jnp.zeros_like(wk_s)
    wk_s[0:48, :] = w_k[...]
    wk_s[48:84, :] = w_kp[...]
    pat = tn(kfr[...], select, lax.Precision.HIGHEST)
    pat_s[:, 0:768] = pat
    r64, l64 = iotas((LK, 128))
    feat = nt(ks[...], wk_s[...])
    k_rows = jnp.where(
        l64 < 48, feat, jnp.where(l64 < 84, rotated(feat, pat) + part(pat, 5), 0.0)
    ).astype(BF)
    k_full = k_rows.astype(F32)
    square = k_full * k_full
    for h in range(3):
        total = jnp.sum(
            jnp.where(within(l64, 48 + 12 * h, 12), square, 0.0), axis=1, keepdims=True
        )
        high = total.astype(BF).astype(F32)
        middle = (total - high).astype(BF).astype(F32)
        low = total - high - middle
        at = 84 + 3 * h
        k_full = jnp.where(
            l64 == at, high, jnp.where(l64 == at + 1, middle, jnp.where(l64 == at + 2, low, k_full))
        )
    mine = (pl.ds(coords[0], 1), pl.ds(coords[1], 1), pl.ds(coords[2], 1))
    buf_k[mine] = k_full.astype(BF).reshape(1, 1, 1, LK, 128)

    bufs = (buf_k, buf_v)

    seen = [set() for _ in STREAMS]

    def gather_copy(s, item):
        which, start, count, order = STREAMS[s]
        _, name, _, axis, step, offsets, half = item
        at = [None] * 3
        for a, offset in zip(order, offsets):
            if offset is None:
                at[a] = pl.ds(0, SIZES[a])
            else:
                at[a] = pl.ds(place(a, offset), 1)
        second = 0 if step == 1 else 1
        if half == "blocks":
            a = order[0]
            at[a] = pl.ds(second * (SIZES[a] // 2), SIZES[a] // 2)
        where = bufs[which].at[at[0], at[1], at[2], pl.ds(start, count)]
        n = NUMBER[name]
        return pltpu.make_async_remote_copy(
            src_ref=where,
            dst_ref=where,
            send_sem=send_sem.at[s, n],
            recv_sem=recv_sem.at[s, n],
            device_id=(neighbour(order[axis], step), core),
            device_id_type=MESH,
        )

    def arrive(s, name):
        if name not in seen[s]:
            seen[s].add(name)
            gather_copy(s, PLAN[NUMBER[name]]).wait_recv()

    def gather_round(s, rnd, last):
        for item in PLAN:
            if item[0] == rnd and (item[1][0] == "e") == last:
                for name in item[2]:
                    arrive(s, name)
                gather_copy(s, item).start()
        if rnd == SLOTS - 1 and last:
            for item in PLAN:
                arrive(s, item[1])

    def gather_slot(slot, streams=range(4)):
        for last in (False, True):
            for s in streams:
                gather_round(s, slot, last)

    pl.semaphore_wait(barrier, 9)
    gather_slot(0, (0, 1))
    for load in loads[4:6]:
        load.wait()
    wv_s[...] = jnp.zeros_like(wv_s)
    wv_s[0:48, :] = w_v[...]
    wv_s[48:120, :] = w_vp[...]
    feat = nt(ks[...], wv_s[...])
    v_rows = jnp.where(
        l64 < 48, feat, jnp.where(l64 < 120, rotated(feat, pat) + part(pat, 5), 0.0)
    ).astype(BF)
    buf_v[mine] = v_rows.reshape(1, 1, 1, LK, 128)
    gather_slot(0, (2, 3))
    pat_s[:, 768:1280] = tn(kfr[...], select_back, lax.Precision.HIGHEST)

    for load in loads[6:]:
        load.wait()
    wq_s[...] = jnp.zeros_like(wq_s)
    wq_s[0:48, :] = w_q[...]
    wq_s[48:84, :] = w_qp[...]
    pat_q = lax.dot_general(
        qfr[...], jnp.concatenate([select, select_back], axis=1), (((1,), (0,)), ((), ())),
        preferred_element_type=F32, precision=lax.Precision.HIGHEST,
    )
    _, l1 = iotas((1, 128))
    x1 = l1 - 3 * third(l1)
    feat = nt(qs[...], wq_s[...])
    q_row = jnp.where(
        l1 < 48, feat, jnp.where(l1 < 84, rotated(feat, pat_q) + part(pat_q, 5), 0.0)
    )
    q_row = q_row.astype(BF).astype(F32)
    r8, l8 = iotas((8, 128))
    raw = [hw[0], hw[1], hw[2]]
    gain = (softplus(by_head(r8, raw)) * POINT_SCALE)[:, 0:1]
    keys8, points8 = mask_k(r8, l8)
    values8 = mask_v(r8, l8)
    q8 = jnp.broadcast_to(q_row, (8, 128))
    q_square = jnp.sum(jnp.where(points8, q8 * q8, 0.0), axis=1, keepdims=True)
    lhs_q = jnp.concatenate(
        [
            jnp.where(keys8, q8, 0.0),
            jnp.where(points8, q8, jnp.where(within(l8, 84 + 3 * r8, 3) & (r8 < 3), -0.5, 0.0)),
        ],
        axis=0,
    ).astype(BF)

    gather_slot(1)
    i256, _ = iotas((256, 1))
    i = i256 & 127
    j = i - 48
    head = lax.shift_right_logical(j * 43, 10)
    point = third(j)
    p_head = lax.shift_right_logical(point, 3)
    source = jnp.where(
        i256 < 128,
        jnp.where(i < 48, 176 * lax.shift_right_logical(i, 4) + (i & 15), 152 * head + 16 + j),
        176 * p_head + 40 + (point & 7),
    )
    valid = (i < 120) & ((i256 < 128) | (i >= 48))
    source = jnp.where(valid, source, -1)
    _, lane_o = iotas((256, 528))
    pick = jnp.where(lane_o == source, 1.0, 0.0).astype(BF)
    wp_s[...] = nn(pick, w_o[...]).astype(BF)
    d_feat = nt(d_o[...], wp_s[...])
    lhs_s[...] = jnp.zeros_like(lhs_s)
    lhs_s[0:3, :] = bw[...].astype(F32)
    for h in range(3):
        lhs_s[8 + h : 9 + h, :] = nt(d_o[...], w_o[176 * h + 48 : 176 * h + 176, :])
    lhs_p = lhs_s[...].astype(BF)
    pair_copy.wait()

    def pair_step(g, _):
        at = pl.multiple_of(g * 1024, 1024)
        pb_s[:, pl.ds(at, 1024)] = nt(lhs_p, pair_s[pl.ds(at, 1024), :])
        return 0

    for slot in range(2, SLOTS - 1):
        lax.fori_loop((slot - 2) * 2, (slot - 1) * 2, pair_step, 0)
        gather_slot(slot)
    gather_slot(SLOTS - 1, (0, 1))

    def chunk(ref, g):
        return ref[pl.ds(lax.div(g, 2), 1), pl.ds(lax.rem(g, 2) * 4, 4)].reshape(1024, 128)

    def logit_step(g, top):
        at = pl.multiple_of(g * 1024, 1024)
        both = nt(lhs_q, chunk(buf_k, g))
        logits = LOGIT_SCALE * (
            both[0:8] * 0.25
            + pb_s[0:8, pl.ds(at, 1024)]
            + gain * (both[8:16] - 0.5 * q_square)
        )
        att_s[:, pl.ds(at, 1024)] = logits
        return jnp.maximum(top, fold(logits, jnp.maximum))

    top = lax.fori_loop(0, 8, logit_step, jnp.full((8, 128), -3.0e38, F32), unroll=8)
    top = jnp.max(top, axis=1, keepdims=True)

    def exp_step(g, total):
        at = pl.multiple_of(g * 1024, 1024)
        e = jnp.exp(att_s[:, pl.ds(at, 1024)] - top)
        att_s[:, pl.ds(at, 1024)] = e
        return total + fold(e, jnp.add)

    zero8 = jnp.zeros((8, 128), F32)
    total = lax.fori_loop(0, 8, exp_step, zero8, unroll=8)
    gather_slot(SLOTS - 1, (2, 3))
    inverse = 1.0 / jnp.sum(total, axis=1, keepdims=True)

    rotate = lax.div(row, 16)
    inner = [lax.rem(row + n, 16) for n in range(16)]
    pairs = [lax.div(n, 2) * 128 for n in inner]
    rc, _ = iotas((8, 1024))

    def group(i):
        return lax.rem(i + rotate, 8)

    def start_sends(message, landing, send, recv, i):
        g = group(i)
        for n in range(1 if i == 0 else 0, 16):
            at = pl.multiple_of(g * 1024 + pairs[n], 128)
            pltpu.make_async_remote_copy(
                src_ref=message.at[:, pl.ds(at, 128)],
                dst_ref=landing.at[row],
                send_sem=send,
                recv_sem=recv,
                device_id=(g * 16 + inner[n], core),
                device_id_type=MESH,
            ).start()

    def own_copy(message, landing):
        at = pl.multiple_of(lax.div(row, 2) * 128, 128)
        return pltpu.make_async_copy(message.at[:, pl.ds(at, 128)], landing.at[row], own_sem)

    def all_of(landing, sem):
        everyone = landing.at[pl.ds(0, ROWS - 1)]
        return pltpu.make_async_copy(everyone, everyone, sem)

    def attend_step(i, acc_v):
        g = group(i)
        if i:
            start_sends(msg_a, recv_a, a_send, a_recv, i - 1)

        at = pl.multiple_of(g * 1024, 1024)
        a = att_s[:, pl.ds(at, 1024)] * inverse
        att_s[:, pl.ds(at, 1024)] = a
        msg_a[:, pl.ds(at, 1024)] = jnp.where(rc < 3, a, side_k)[0:4].astype(BF)
        return acc_v + nn(a.astype(BF), chunk(buf_v, g))

    side_k = jnp.concatenate([q8] * 8, axis=1)
    acc_v = zero8
    for i in range(8):
        acc_v = attend_step(i, acc_v)
    start_sends(msg_a, recv_a, a_send, a_recv, 7)
    own_a = own_copy(msg_a, recv_a)
    own_a.start()
    row_v = jnp.sum(jnp.where(values8, acc_v, 0.0), axis=0, keepdims=True)
    is_point = within(l1, 48, 72)
    local = jnp.where(is_point, unrotated(jnp.where(is_point, row_v - part(pat_q, 5), 0.0), pat_q), 0.0)
    squares = local * local
    norm = squares
    for d in SHIFTS[1:]:
        norm = norm + jnp.where((x1 + d >= 0) & (x1 + d < 3), shifted(squares, d), 0.0)
    lengths = jnp.sqrt(1.0 + norm)
    d_local = d_feat[:, 0:128] + d_feat[:, 128:256] / lengths * local
    d_local = jnp.where(is_point, d_local, 0.0)
    side_v = jnp.where(
        l1 < 48, d_feat[:, 0:128], jnp.where(is_point, rotated(d_local, pat_q), 0.0)
    )
    side_v8 = jnp.broadcast_to(side_v, (8, 128))
    lhs_v = jnp.where(values8, side_v8, 0.0).astype(BF)

    def grad_step(g, carry):
        at = pl.multiple_of(g * 1024, 1024)
        d_att = nt(lhs_v, chunk(buf_v, g)) + pb_s[8:16, pl.ds(at, 1024)]
        da_s[:, pl.ds(at, 1024)] = d_att
        return carry + fold(att_s[:, pl.ds(at, 1024)] * d_att, jnp.add)

    row_total = lax.fori_loop(0, 8, grad_step, zero8, unroll=8)
    row_total = jnp.sum(row_total, axis=1, keepdims=True)
    side_v = jnp.concatenate([side_v8] * 8, axis=1)

    def score_step(i, sums):
        g = group(i)
        if i:
            start_sends(msg_s, recv_s, s_send, s_recv, i - 1)

        at = pl.multiple_of(g * 1024, 1024)
        a = att_s[:, pl.ds(at, 1024)]
        score = LOGIT_SCALE * a * (da_s[:, pl.ds(at, 1024)] - row_total)
        msg_s[:, pl.ds(at, 1024)] = jnp.where(rc < 3, score, side_v)[0:4].astype(BF)
        score = score.astype(BF).astype(F32)
        da_s[:, pl.ds(at, 1024)] = score
        return sums + fold(score, jnp.add)

    score_rows = zero8
    for i in range(8):
        score_rows = score_step(i, score_rows)
    score_rows = jnp.sum(score_rows, axis=1, keepdims=True)
    start_sends(msg_s, recv_s, s_send, s_recv, 7)
    own_a.wait()
    own_s = own_copy(msg_s, recv_s)
    own_s.start()

    def rest_step(g, carry):
        acc_k, acc_p = carry
        at = pl.multiple_of(g * 1024, 1024)
        return (
            acc_k + nn(da_s[:, pl.ds(at, 1024)].astype(BF), chunk(buf_k, g)),
            acc_p + nn(att_s[:, pl.ds(at, 1024)].astype(BF), pair_s[pl.ds(at, 1024), :]),
        )

    acc_k, acc_p = lax.fori_loop(0, 8, rest_step, (zero8, zero8), unroll=4)
    f_v = jnp.where(l1 < 48, row_v, local).astype(BF)
    f_len = jnp.where(is_point & (x1 == 0), lengths, 0.0).astype(BF)
    out_row = nn(f_v, wp_s[0:128, :]) + nn(f_len, wp_s[128:256, :])
    for h in range(3):
        out_row = out_row + nn(
            acc_p[h : h + 1, :].astype(BF), w_o[176 * h + 48 : 176 * h + 176, :]
        )
    part_s[64:65, :] = out_row

    q_terms = jnp.where(keys8, acc_k * 0.25, 0.0) + jnp.where(
        points8, gain * (acc_k - score_rows * q8), 0.0
    )
    d_q = jnp.sum(q_terms, axis=0, keepdims=True)
    d_q = jnp.where(l1 < 48, d_q, jnp.where(l1 < 84, unrotated(d_q, pat_q), 0.0)).astype(BF)
    part_s[72:73, :] = nn(d_q, wq_s[...])

    _, l128 = iotas((ROWS, 128))

    def unpack(landing, unpacked):
        def step(i, _):
            at = pl.multiple_of(i * 32, 32)
            unpacked[pl.ds(at, 32), :] = landing[pl.ds(i * 8, 8)].astype(F32).reshape(32, 128)
            return 0

        lax.fori_loop(0, ROWS // 8, step, 0, unroll=16)
        return [unpacked[pl.ds(n, ROWS, stride=4), :] for n in range(4)]

    odd = lax.rem(row, 2) == 1

    def mine_of(x):
        return jnp.where(odd, x[64:128], x[0:64])

    for s in range(4):
        for item in PLAN:
            gather_copy(s, item).wait_send()
    all_of(recv_a, a_recv).wait()
    *att_h, side_k = unpack(recv_a, unpack_a)
    keys_h = [within(l128, 16 * h, 16) for h in range(3)]
    points_h = [within(l128, 48 + 12 * h, 12) for h in range(3)]
    rights = [
        jnp.concatenate(
            [
                jnp.where(keys_h[h] | points_h[h], side_k, 0.0).astype(BF),
                jnp.where(points_h[h], 1.0, 0.0).astype(BF),
            ],
            axis=1,
        )
        for h in range(3)
    ]
    pat = pat_s[...]
    kf = buf_k[mine].reshape(LK, 128).astype(F32)
    gain_l = softplus(by_head(jnp.where(l1 < 60, 0, jnp.where(l1 < 72, 1, 2)), raw)) * POINT_SCALE

    all_of(recv_s, s_recv).wait()
    own_s.wait()
    *score_h, side_v = unpack(recv_s, unpack_s)
    out_v = jnp.zeros((128, 128), F32)
    both = jnp.zeros((128, 256), F32)
    for h in range(3):
        score = score_h[h].astype(BF)
        vpoints_h = within(l128, 48 + 24 * h, 24)
        out_v = out_v + tn(
            att_h[h].astype(BF), jnp.where(keys_h[h] | vpoints_h, side_v, 0.0).astype(BF)
        )
        both = both + tn(score, rights[h])
    out_v, both = mine_of(out_v), mine_of(both)
    out_k, sums = both[:, 0:128], both[:, 128:256]
    d_points = jnp.where(within(l64, 48, 36), gain_l * (out_k - sums * kf), 0.0)
    d_k = jnp.where(l64 < 48, out_k * 0.25, jnp.where(l64 < 84, unrotated(d_points, pat), 0.0))
    d_v = jnp.where(l64 < 48, out_v, jnp.where(l64 < 120, unrotated(out_v, pat), 0.0))
    part_s[0:64, :] = nn(d_k.astype(BF), wk_s[...]) + nn(d_v.astype(BF), wv_s[...])

    exchange = pltpu.make_async_remote_copy(
        src_ref=part_s,
        dst_ref=got_s,
        send_sem=ex_send,
        recv_sem=ex_recv,
        device_id=(row, 1 - core),
        device_id_type=MESH,
    )
    exchange.start()
    all_of(recv_a, a_send).wait()
    all_of(recv_s, s_send).wait()
    exchange.wait()
    o_sum[...] = part_s[...] + got_s[...]


def finish(total, o_out, o_gq, o_gk):
    o_gk[...] = total[0:64, :]
    o_out[...] = total[64:65, :].astype(BF)
    o_gq[...] = total[72:73, :]


def shards(
    query_single, key_single, pair, query_frames, key_frames, w_query, w_key, w_value,
    w_query_points, w_key_points, w_value_points, head_weight, bias_weight, w_out, d_out,
):
    vmem = pl.BlockSpec(memory_space=pltpu.VMEM)
    specs = [pl.BlockSpec(memory_space=pltpu.HBM)] * 15
    dma = pltpu.SemaphoreType.DMA
    total = pl.pallas_call(
        kernel,
        out_shape=pltpu.VMEM((80, 384), F32),
        in_specs=specs,
        out_specs=vmem,
        scratch_shapes=[
            pltpu.VMEM((1, 384), BF),
            pltpu.VMEM((LK, 384), BF),
            pltpu.VMEM((1, 12), F32),
            pltpu.VMEM((12, LK), F32),
            pltpu.VMEM((48, 384), BF),
            pltpu.VMEM((48, 384), BF),
            pltpu.VMEM((48, 384), BF),
            pltpu.VMEM((36, 384), BF),
            pltpu.VMEM((36, 384), BF),
            pltpu.VMEM((72, 384), BF),
            pltpu.SMEM((3,), F32),
            pltpu.VMEM((3, 128), BF),
            pltpu.VMEM((528, 384), BF),
            pltpu.VMEM((1, 384), BF),
            pltpu.SemaphoreType.DMA((14,)),
            pltpu.VMEM((NY, NZ, NX, LK, 128), BF),
            pltpu.VMEM((NY, NZ, NX, LK, 128), BF),
            pltpu.VMEM((K, 128), BF),
            pltpu.VMEM((128, 384), BF),
            pltpu.VMEM((128, 384), BF),
            pltpu.VMEM((128, 384), BF),
            pltpu.VMEM((256, 384), BF),
            pltpu.VMEM((16, 128), F32),
            pltpu.VMEM((16, K), F32),
            pltpu.VMEM((8, K), F32),
            pltpu.VMEM((8, K), F32),
            pltpu.VMEM((4, K), BF),
            pltpu.VMEM((4, K), BF),
            pltpu.VMEM((ROWS, 4, 128), BF),
            pltpu.VMEM((ROWS, 4, 128), BF),
            pltpu.VMEM((ROWS * 4, 128), F32),
            pltpu.VMEM((ROWS * 4, 128), F32),
            pltpu.VMEM((LK, 1280), F32),
            pltpu.VMEM((80, 384), F32),
            pltpu.VMEM((80, 384), F32),
            dma, dma((4, len(PLAN))), dma((4, len(PLAN))), dma, dma, dma, dma, dma, dma, dma,
        ],
        compiler_params=pltpu.CompilerParams(
            collective_id=0, has_side_effects=True, vmem_limit_bytes=66900000
        ),
    )(
        query_single, key_single, pair, query_frames.T, key_frames, w_query.T, w_key.T, w_value.T,
        w_query_points.T, w_key_points.T, w_value_points.T, head_weight, bias_weight, w_out, d_out,
    )
    return pl.pallas_call(
        finish,
        out_shape=(
            jax.ShapeDtypeStruct((1, 384), BF),
            jax.ShapeDtypeStruct((1, 384), F32),
            jax.ShapeDtypeStruct((LK, 384), F32),
        ),
        in_specs=[vmem],
        out_specs=(vmem, vmem, vmem),
        compiler_params=pltpu.CompilerParams(vmem_limit_bytes=16 * 1024 * 1024),
    )(total)


def solution(mesh):
    return jax.shard_map(
        shards,
        mesh=mesh,
        in_specs=(
            P("row", None),
            P("row", None),
            P("row", None, None),
            P(None, "row"),
            P(None, "row"),
            P(None, "head"),
            P(None, "head"),
            P(None, "head"),
            P(None, "head"),
            P(None, "head"),
            P(None, "head"),
            P("head"),
            P("head", None),
            P("head", None),
            P("row", None),
        ),
        out_specs=(P("row", None), P("row", None), P("row", None)),
        check_vma=False,
    )
```
